128 devices in a mesh: grp: 4 (over y), loc: 32 (over x, z, core).
Axes of the slice: x: 4, y: 4, z: 4, core: 2. Of those that a mesh axis runs over, the one named last changes fastest.
Arguments:
- tokens: bfloat16 [16384, 7168], P(('grp', 'loc')), may hold values from -1.5 to 1.5
- grad_out: bfloat16 [16384, 7168], P(('grp', 'loc')), may hold values from -0.8984375 to 0.8984375
- expert_ids: int32 [16384, 8], P(('grp', 'loc')), may hold values from 0 to 255, as said below
- route_weight: bfloat16 [16384, 8], P(('grp', 'loc')), may hold values from 0.25 to 2
- gate_weight: bfloat16 [32, 7168, 512], P('loc', None, 'grp'), may hold values from -0.25 to 0.25
- up_weight: bfloat16 [32, 7168, 512], P('loc', None, 'grp'), may hold values from -0.25 to 0.25
- down_weight: bfloat16 [32, 512, 7168], P('loc', 'grp'), may hold values from -0.1875 to 0.1875
Outputs:
- tokens_grad: bfloat16 [16384, 7168], P(('grp', 'loc'))
- gate_grad: bfloat16 [32, 7168, 512], P('loc', None, 'grp')
- up_grad: bfloat16 [32, 7168, 512], P('loc', None, 'grp')
- down_grad: bfloat16 [32, 512, 7168], P('loc', 'grp')
The draws below stay inside these ranges and needn't reach their ends.
Inputs may be any that keep to these rules, and one draw needn't show every extreme that they name: `expert_ids`: each row names 8 different experts.
All inputs are finite; a program needn't handle non-finite values.
Results may differ from the reference program's by a relative error of at most 0.015.
Values may be sent and summed in bfloat16 or wider, within the bound.
No kernel may reach another device: no remote copies, remote signals or barrier semaphores. Data moves between devices by JAX's collectives and lax.ppermute only.
A program may use at most 128 MiB of HBM per device.

```python
import math
import jax
import jax.numpy as jnp
from jax import lax

D = 7168
EXPERTS = 256
TOPK = 8
FF_WIN = 1024
TOK_DEV = 128
TOKENS = 16384
EXP_FL = 16
CAP = 4
FF_HALF = 512
FF_DEV = 128
N_GRP = 4
N_LOC = 32


def draw_expert_ids(key, part):
    key_base, key_order, key_noise = jax.random.split(key, 3)
    base = jax.random.randint(key_base, (EXPERTS,), 0, 4096)
    order = jax.random.permutation(key_order, EXP_FL)
    favored = jnp.zeros((EXPERTS,), jnp.int32).at[order[:2]].set(1 << 20)
    noise = jax.random.randint(key_noise, (TOKENS, EXPERTS), 0, 8192)
    score = (noise + base[None, :] + favored[None, :]) * EXPERTS + jnp.arange(EXPERTS, dtype=jnp.int32)[None, :]
    _, chosen = lax.top_k(score, TOPK)
    return chosen.astype(jnp.int32)


def steps_of(own_key, extent, pieces, least, top_value):
    def one(axis_at, parts):
        draws = jax.random.uniform(jax.random.fold_in(jax.random.fold_in(own_key, 6), axis_at), (parts,), jnp.float32, least / len(pieces), top_value / len(pieces))
        return jnp.repeat(jnp.exp(draws), extent[axis_at] // parts).reshape((-1,) + (1,) * (len(extent) - axis_at - 1))

    gain = one(*pieces[0])
    for cut in pieces[1:]:
        gain = gain * one(*cut)
    return gain


def centred(own_key, dims, spread, bound, cuts=(), held_as=jnp.bfloat16):
    values = jax.random.normal(own_key, dims, jnp.float32) * spread
    if len(cuts) > 0:
        values = steps_of(own_key, dims, cuts, -0.22, 0.18) * values
    return jnp.clip(values, min=-bound, max=bound).astype(held_as)


def setup_inputs(seed: int = 0) -> dict:
    arg_keys = jax.random.split(jax.random.key(seed), 8)
    return {
        "tokens": centred(arg_keys[0], (TOKENS, D), 0.25, 1.5, ((0, 128),)),
        "grad_out": centred(arg_keys[1], (TOKENS, D), 0.15, 0.8984375, ((0, 128),)),
        "expert_ids": draw_expert_ids(jax.random.fold_in(arg_keys[7], 71), 0),
        "route_weight": jnp.clip(jnp.exp(math.log(2.0) - 2.0794415 * jax.random.uniform(arg_keys[3], (TOKENS, TOPK), jnp.float32) ** steps_of(arg_keys[3], (TOKENS, TOPK), ((0, 128),), -0.2, 0.2)), 0.25, 2.0).astype(jnp.bfloat16),
        "gate_weight": centred(arg_keys[4], (2 * EXP_FL, D, FF_HALF), (D // 16) ** -0.5, 0.25, ((0, 32), (2, 4))),
        "up_weight": centred(arg_keys[5], (2 * EXP_FL, D, FF_HALF), (D // 16) ** -0.5, 0.25, ((0, 32), (2, 4))),
        "down_weight": centred(arg_keys[6], (2 * EXP_FL, FF_HALF, D), FF_WIN ** -0.5, 0.1875, ((0, 32), (1, 4))),
    }


def place_pairs(id_block, expert_fl):
    expert_iota = jnp.arange(expert_fl, dtype=jnp.int32)
    onehot = (id_block[:, None] == expert_iota[None, :]).astype(jnp.int32)
    before = jnp.cumsum(onehot, axis=0) - onehot
    slot_index = jnp.sum(before * onehot, axis=1)
    keep_mask = (id_block < expert_fl) & (slot_index < CAP)
    return jnp.where(keep_mask, id_block * CAP + slot_index, expert_fl * CAP).astype(jnp.int32)


def contract_rows(left, right):
    return lax.dot_general(left, right, (((0,), (0,)), ((), ())), preferred_element_type=jnp.float32)


def contract_cols(left, right):
    return lax.dot_general(left, right, (((1,), (1,)), ((), ())), preferred_element_type=jnp.float32)


def reference(tokens, grad_out, expert_ids, route_weight, gate_weight, up_weight, down_weight):
    devices_all = N_GRP * N_LOC
    expert_fl = N_LOC // 2
    buffer = expert_fl * CAP
    pair_count = TOK_DEV * TOPK
    id_blocks = expert_ids.reshape(devices_all, pair_count)
    positions = jax.vmap(lambda blk: place_pairs(blk, expert_fl))(id_blocks)
    pair_token = jnp.arange(pair_count, dtype=jnp.int32) // TOPK
    weight_blocks = route_weight.reshape(devices_all, pair_count)

    def fill_tokens(pos):
        return jnp.full((buffer + 1,), -1, jnp.int32).at[pos].set(pair_token)[:buffer]

    def fill_weights(pos, wts):
        return jnp.zeros((buffer + 1,), route_weight.dtype).at[pos].set(wts)[:buffer]

    token_at = jax.vmap(fill_tokens)(positions)
    weight_at = jax.vmap(fill_weights)(positions, weight_blocks)
    valid = token_at >= 0
    offsets = (jnp.arange(devices_all, dtype=jnp.int32) * TOK_DEV)[:, None]
    global_token = jnp.where(valid, token_at + offsets, 0).astype(jnp.int32)
    block_count = 2 * N_GRP

    def one_expert(expert):
        start = (expert * CAP).astype(jnp.int32)
        index = lax.dynamic_slice_in_dim(global_token, start, CAP, 1).reshape(-1)
        present = lax.dynamic_slice_in_dim(valid, start, CAP, 1).reshape(-1)
        weights = lax.dynamic_slice_in_dim(weight_at, start, CAP, 1).reshape(-1)
        x_rows = jnp.where(present[:, None], tokens[index], jnp.zeros((), tokens.dtype))
        g_rows = jnp.where(present[:, None], grad_out[index], jnp.zeros((), grad_out.dtype))
        w_rows = weights.astype(jnp.float32)[:, None]
        w_gate = jnp.concatenate([gate_weight[expert], gate_weight[expert_fl + expert]], axis=1)
        w_up = jnp.concatenate([up_weight[expert], up_weight[expert_fl + expert]], axis=1)
        w_down = jnp.concatenate([down_weight[expert], down_weight[expert_fl + expert]], axis=0)
        pre_gate = jnp.dot(x_rows, w_gate, preferred_element_type=jnp.float32)
        pre_up = jnp.dot(x_rows, w_up, preferred_element_type=jnp.float32)
        sigmoid_gate = jax.nn.sigmoid(pre_gate)
        swish = pre_gate * sigmoid_gate
        hidden_grad = w_rows * contract_cols(g_rows, w_down)
        gate_delta = (hidden_grad * pre_up * sigmoid_gate * (1.0 + pre_gate * (1.0 - sigmoid_gate))).astype(jnp.bfloat16)
        up_delta = (hidden_grad * swish).astype(jnp.bfloat16)
        weighted = (w_rows * swish * pre_up).astype(jnp.bfloat16)
        gate_full = contract_rows(x_rows, gate_delta).astype(jnp.bfloat16)
        up_full = contract_rows(x_rows, up_delta).astype(jnp.bfloat16)
        down_full = contract_rows(weighted, g_rows).astype(jnp.bfloat16)

        def add_block(total, block):
            first = (block * FF_DEV).astype(jnp.int32)
            part = contract_cols(lax.dynamic_slice_in_dim(gate_delta, first, FF_DEV, 1), lax.dynamic_slice_in_dim(w_gate, first, FF_DEV, 1))
            part = part + contract_cols(lax.dynamic_slice_in_dim(up_delta, first, FF_DEV, 1), lax.dynamic_slice_in_dim(w_up, first, FF_DEV, 1))
            rounded = lax.optimization_barrier(part.astype(jnp.bfloat16)).astype(jnp.float32)
            return total + rounded, None

        start_total = jnp.zeros((devices_all * CAP, D), jnp.float32)
        row_grad, _ = lax.scan(add_block, start_total, jnp.arange(block_count, dtype=jnp.int32))
        return row_grad, gate_full, up_full, down_full

    row_grads, gate_stack, up_stack, down_stack = lax.map(one_expert, jnp.arange(expert_fl, dtype=jnp.int32))
    returned = row_grads.reshape(expert_fl, devices_all, CAP, D).transpose(1, 0, 2, 3).reshape(devices_all, buffer, D)
    columns = jnp.arange(buffer, dtype=jnp.int32)
    tables = (positions.reshape(devices_all, TOK_DEV, TOPK)[..., None] == columns).any(axis=2).astype(jnp.float32)
    tokens_grad = jnp.einsum("dtb,dbr->dtr", tables, returned, precision=lax.Precision.HIGHEST)
    tokens_grad = tokens_grad.reshape(TOKENS, D).astype(jnp.bfloat16)
    gate_grad = gate_stack.reshape(expert_fl, D, 2, FF_HALF).transpose(2, 0, 1, 3).reshape(2 * expert_fl, D, FF_HALF)
    up_grad = up_stack.reshape(expert_fl, D, 2, FF_HALF).transpose(2, 0, 1, 3).reshape(2 * expert_fl, D, FF_HALF)
    down_grad = down_stack.reshape(expert_fl, 2, FF_HALF, D).transpose(1, 0, 2, 3).reshape(2 * expert_fl, FF_HALF, D)
    return (tokens_grad, gate_grad, up_grad, down_grad)
```

```python
import functools

import jax
import jax.numpy as jnp
from jax import lax
from jax.experimental import pallas as pl
from jax.experimental.pallas import tpu as pltpu
from jax.sharding import PartitionSpec as P

CAP = 4
BF = jnp.bfloat16
F32 = jnp.float32
MIB = 1 << 20


def contract_rows(left, right):
    return lax.dot_general(left, right, (((0,), (0,)), ((), ())), preferred_element_type=F32)


def contract_cols(left, right):
    return lax.dot_general(left, right, (((1,), (1,)), ((), ())), preferred_element_type=F32)


def cost(flops, nbytes):
    return pl.CostEstimate(flops=flops, bytes_accessed=nbytes, transcendentals=0)


def params(mib):
    return pltpu.CompilerParams(vmem_limit_bytes=mib * MIB)


def dispatch_kernel(ids_ref, w_ref, t_ref, g_ref, table_ref, x_ref, gw_ref, tab, wtab):
    tok, topk = ids_ref.shape
    buf = tab.shape[1]

    @pl.when(pl.program_id(0) == 0)
    def _():
        column = lax.broadcasted_iota(jnp.int32, (tok, buf), 1)
        expert = lax.div(column, CAP)
        chosen = jnp.zeros((tok, buf), F32)
        weight = jnp.zeros((tok, buf), F32)
        for k in range(topk):
            hit = ids_ref[:, k : k + 1] == expert
            chosen = jnp.where(hit, 1.0, chosen)
            weight = jnp.where(hit, w_ref[:, k : k + 1].astype(F32), weight)
        row = lax.broadcasted_iota(jnp.int32, (tok, tok), 0)
        col = lax.broadcasted_iota(jnp.int32, (tok, tok), 1)
        earlier = jnp.where(col < row, 1.0, 0.0).astype(BF)
        slot = jnp.dot(earlier, chosen.astype(BF), preferred_element_type=F32)
        want = lax.rem(column, CAP).astype(F32)
        mine = (chosen > 0.5) & (slot == want)
        table = jnp.where(mine, 1.0, 0.0).astype(BF)
        tab[...] = table
        wtab[...] = jnp.where(mine, weight, 0.0).astype(BF)
        table_ref[...] = table

    rows = contract_rows(tab[...], t_ref[...])
    rows = rows.reshape(buf // CAP, CAP, rows.shape[1]).astype(BF)
    x_ref[0] = rows
    x_ref[1] = rows
    gw_ref[...] = contract_rows(wtab[...], g_ref[...]).astype(BF)


def dispatch(ids, weights, tokens, grad_out, expert_fl):
    tok, width = tokens.shape
    buf = expert_fl * CAP
    tile = 1024
    return pl.pallas_call(
        dispatch_kernel,
        grid=(width // tile,),
        in_specs=[
            pl.BlockSpec(ids.shape, lambda j: (0, 0)),
            pl.BlockSpec(weights.shape, lambda j: (0, 0)),
            pl.BlockSpec((tok, tile), lambda j: (0, j)),
            pl.BlockSpec((tok, tile), lambda j: (0, j)),
        ],
        out_specs=[
            pl.BlockSpec((tok, buf), lambda j: (0, 0)),
            pl.BlockSpec((2, expert_fl, CAP, tile), lambda j: (0, 0, 0, j)),
            pl.BlockSpec((buf, tile), lambda j: (0, j)),
        ],
        out_shape=[
            jax.ShapeDtypeStruct((tok, buf), BF),
            jax.ShapeDtypeStruct((2, expert_fl, CAP, width), BF),
            jax.ShapeDtypeStruct((buf, width), BF),
        ],
        scratch_shapes=[pltpu.VMEM((tok, buf), BF), pltpu.VMEM((tok, buf), BF)],
        compiler_params=params(16),
        cost_estimate=cost(4 * tok * buf * width, 2 * width * (2 * tok + 3 * buf)),
        name="dispatch",
    )(ids, weights, tokens, grad_out)


def regroup_kernel(in_ref, out_ref):
    groups, buf, tile = in_ref.shape
    experts = buf // CAP
    blocks = [in_ref[y].astype(F32).reshape(experts, CAP, tile) for y in range(groups)]
    rows = jnp.concatenate(blocks, axis=1).astype(BF)
    out_ref[0] = rows
    out_ref[1] = rows


def regroup(rows):
    groups, buf, width = rows.shape
    experts = buf // CAP
    tile = 512
    return pl.pallas_call(
        regroup_kernel,
        grid=(width // tile,),
        in_specs=[pl.BlockSpec((groups, buf, tile), lambda j: (0, 0, j))],
        out_specs=pl.BlockSpec((2, experts, groups * CAP, tile), lambda j: (0, 0, 0, j)),
        out_shape=jax.ShapeDtypeStruct((2, experts, groups * CAP, width), BF),
        compiler_params=params(24),
        cost_estimate=cost(0, 6 * groups * buf * width),
        name="regroup",
    )(rows)


def row_part_kernel(gd_ref, ud_ref, wg_ref, wu_ref, out_ref):
    total = contract_cols(gd_ref[...], wg_ref[...]) + contract_cols(ud_ref[...], wu_ref[...])
    out_ref[...] = total.astype(BF)


def row_part(gate_delta, up_delta, w_gate, w_up, first, count):
    rows, ff = gate_delta.shape
    tile = 512
    skip = first // tile
    return pl.pallas_call(
        row_part_kernel,
        grid=(count // tile,),
        in_specs=[
            pl.BlockSpec((rows, ff), lambda j: (0, 0)),
            pl.BlockSpec((rows, ff), lambda j: (0, 0)),
            pl.BlockSpec((tile, ff), lambda j: (j + skip, 0)),
            pl.BlockSpec((tile, ff), lambda j: (j + skip, 0)),
        ],
        out_specs=pl.BlockSpec((rows, tile), lambda j: (0, j)),
        out_shape=jax.ShapeDtypeStruct((rows, count), BF),
        compiler_params=params(16),
        cost_estimate=cost(4 * rows * ff * count, 2 * count * (rows + 2 * ff)),
        name="row_part",
    )(gate_delta, up_delta, w_gate, w_up)


def fold_kernel(in_ref, out_ref):
    _, experts, depth, tile = in_ref.shape
    groups = depth // CAP
    total = in_ref[0].astype(F32) + in_ref[1].astype(F32)
    for y in range(groups):
        part = total[:, y * CAP : (y + 1) * CAP, :]
        out_ref[y] = part.reshape(experts * CAP, tile).astype(BF)


def fold(home):
    _, experts, depth, width = home.shape
    groups = depth // CAP
    tile = 512
    return pl.pallas_call(
        fold_kernel,
        grid=(width // tile,),
        in_specs=[pl.BlockSpec((2, experts, depth, tile), lambda j: (0, 0, 0, j))],
        out_specs=pl.BlockSpec((groups, experts * CAP, tile), lambda j: (0, 0, j)),
        out_shape=jax.ShapeDtypeStruct((groups, experts * CAP, width), BF),
        compiler_params=params(24),
        cost_estimate=cost(experts * depth * width, 6 * experts * depth * width),
        name="fold",
    )(home)


def combine_kernel(split, table_ref, ring_ref, whole_ref, out_ref):
    table = table_ref[...]

    @pl.when(pl.program_id(0) < split)
    def _():
        out_ref[...] = jnp.dot(table, ring_ref[...], preferred_element_type=F32).astype(BF)

    @pl.when(pl.program_id(0) >= split)
    def _():
        count, _, tile = whole_ref.shape
        rows = whole_ref[...].astype(F32).reshape(count * CAP, tile).astype(BF)
        both = jnp.concatenate([table, table], axis=1)
        out_ref[...] = jnp.dot(both, rows, preferred_element_type=F32).astype(BF)


def combine(table, ring, whole):
    tok, buf = table.shape
    tile = 512
    width = ring.shape[1] + whole.shape[2]
    split = ring.shape[1] // tile
    return pl.pallas_call(
        functools.partial(combine_kernel, split),
        grid=(width // tile,),
        in_specs=[
            pl.BlockSpec((tok, buf), lambda j: (0, 0)),
            pl.BlockSpec((buf, tile), lambda j: (0, jnp.minimum(j, split - 1))),
            pl.BlockSpec((whole.shape[0], CAP, tile), lambda j: (0, 0, jnp.maximum(j - split, 0))),
        ],
        out_specs=pl.BlockSpec((tok, tile), lambda j: (0, j)),
        out_shape=jax.ShapeDtypeStruct((tok, width), BF),
        compiler_params=params(16),
        cost_estimate=cost(2 * tok * buf * width, 2 * width * (tok + 2 * buf)),
        name="combine",
    )(table, ring, whole)


def body(tokens, grad_out, expert_ids, route_weight, gate_weight, up_weight, down_weight):
    groups = lax.axis_size("grp")
    locs = lax.axis_size("loc")
    expert_fl = locs // 2
    width = tokens.shape[1]
    buf = expert_fl * CAP
    rows = groups * locs * CAP
    ring_cols = 3072

    w_gate, w_up, w_down = gate_weight[0], up_weight[0], down_weight[0]
    ff = w_gate.shape[1]

    table, x_send, g_send = dispatch(expert_ids, route_weight, tokens, grad_out, expert_fl)

    g_ring = lax.all_gather(g_send, "grp", axis=0, tiled=False)
    g_out = regroup(g_ring).reshape(locs, groups * CAP, width)
    x_here = lax.all_to_all(
        x_send.reshape(locs, CAP, width), "loc", split_axis=0, concat_axis=0, tiled=True
    )
    x_rows = lax.all_gather(x_here, "grp", axis=0, tiled=True).reshape(rows, width)
    g_rows = lax.all_to_all(g_out, "loc", split_axis=0, concat_axis=0, tiled=True).reshape(
        rows, width
    )

    def to_loc_first(a):
        return a.reshape(groups, locs, CAP, ff).transpose(1, 0, 2, 3).reshape(rows, ff)

    def to_grp_first(a):
        return a.reshape(locs, groups, CAP, ff).transpose(1, 0, 2, 3).reshape(rows, ff)

    pre_gate = to_loc_first(jnp.dot(x_rows, w_gate, preferred_element_type=F32))
    pre_up = to_loc_first(jnp.dot(x_rows, w_up, preferred_element_type=F32))
    sig = jax.nn.sigmoid(pre_gate)
    swish = pre_gate * sig
    slope = pre_up * sig * (1.0 + pre_gate * (1.0 - sig))
    unweighted = (swish * pre_up).astype(BF)

    hidden_grad = contract_cols(g_rows, w_down)
    gate_delta = (hidden_grad * slope).astype(BF)
    up_delta = (hidden_grad * swish).astype(BF)
    gate_delta_x = to_grp_first(gate_delta)
    up_delta_x = to_grp_first(up_delta)

    part_ring = row_part(gate_delta, up_delta, w_gate, w_up, 0, ring_cols)
    home_ring = lax.all_to_all(
        part_ring.reshape(locs, groups * CAP, ring_cols),
        "loc",
        split_axis=0,
        concat_axis=0,
        tiled=True,
    )
    part_whole = row_part(gate_delta_x, up_delta_x, w_gate, w_up, ring_cols, width - ring_cols)
    reduced = lax.psum_scatter(
        part_whole.reshape(groups, locs * CAP, width - ring_cols),
        "grp",
        scatter_dimension=0,
        tiled=True,
    )
    home_whole = lax.all_to_all(
        reduced.reshape(locs, CAP, width - ring_cols),
        "loc",
        split_axis=0,
        concat_axis=0,
        tiled=True,
    )
    folded = fold(home_ring.reshape(2, expert_fl, groups * CAP, ring_cols))
    ring = lax.psum_scatter(folded, "grp", scatter_dimension=0, tiled=True)

    gate_grad = contract_rows(x_rows, gate_delta_x).astype(BF)[None]
    up_grad = contract_rows(x_rows, up_delta_x).astype(BF)[None]
    down_grad = contract_rows(unweighted, g_rows).astype(BF)[None]
    tokens_grad = combine(table, ring.reshape(buf, ring_cols), home_whole)
    return (tokens_grad, gate_grad, up_grad, down_grad)


def solution(mesh):
    in_specs = (
        P(("grp", "loc"), None),
        P(("grp", "loc"), None),
        P(("grp", "loc"), None),
        P(("grp", "loc"), None),
        P("loc", None, "grp"),
        P("loc", None, "grp"),
        P("loc", "grp", None),
    )
    out_specs = (
        P(("grp", "loc"), None),
        P("loc", None, "grp"),
        P("loc", None, "grp"),
        P("loc", "grp", None),
    )
    return jax.shard_map(body, mesh=mesh, in_specs=in_specs, out_specs=out_specs, check_vma=False)
```

```python
import functools

import jax
import jax.numpy as jnp
from jax import lax
from jax.experimental import pallas as pl
from jax.experimental.pallas import tpu as pltpu
from jax.sharding import PartitionSpec as P

CAP = 4
BF = jnp.bfloat16
F32 = jnp.float32
TILE = 1024


def contract_rows(left, right):
    return lax.dot_general(left, right, (((0,), (0,)), ((), ())), preferred_element_type=F32)


def contract_cols(left, right):
    return lax.dot_general(left, right, (((1,), (1,)), ((), ())), preferred_element_type=F32)


def whole(shape):
    return pl.BlockSpec(shape, lambda *_: (0,) * len(shape))


def call(kernel, name, flops, nbytes, mib=56, **kwargs):
    return pl.pallas_call(
        kernel,
        name=name,
        compiler_params=pltpu.CompilerParams(vmem_limit_bytes=mib << 20),
        cost_estimate=pl.CostEstimate(flops=flops, bytes_accessed=nbytes, transcendentals=0),
        **kwargs,
    )


def dispatch_kernel(ids_ref, w_ref, t_ref, g_ref, table_ref, xg_ref, gw_ref, pick, wtab):
    tok, topk = ids_ref.shape
    buf = wtab.shape[1]
    experts = buf // CAP
    unit = 2 * CAP

    @pl.when(pl.program_id(0) == 0)
    def _():
        def tables(columns, expert, want):
            chosen = jnp.zeros((tok, columns), F32)
            weight = jnp.zeros((tok, columns), F32)
            for k in range(topk):
                hit = ids_ref[:, k : k + 1] == expert
                chosen = jnp.where(hit, 1.0, chosen)
                weight = jnp.where(hit, w_ref[:, k : k + 1].astype(F32), weight)
            slot = jnp.dot(earlier, chosen.astype(BF), preferred_element_type=F32)
            mine = (chosen > 0.5) & (slot == want)
            return jnp.where(mine, 1.0, 0.0), jnp.where(mine, weight, 0.0)

        row = lax.broadcasted_iota(jnp.int32, (tok, tok), 0)
        col = lax.broadcasted_iota(jnp.int32, (tok, tok), 1)
        earlier = jnp.where(col < row, 1.0, 0.0).astype(BF)

        column = lax.broadcasted_iota(jnp.int32, (tok, buf), 1)
        table, weighted = tables(buf, lax.div(column, CAP), lax.rem(column, CAP).astype(F32))
        table_ref[...] = table.astype(BF)
        wtab[...] = weighted.astype(BF)

        column = lax.broadcasted_iota(jnp.int32, (tok, experts * unit), 1)
        table, weighted = tables(
            experts * unit, lax.div(column, unit), lax.rem(column, CAP).astype(F32)
        )
        is_token = lax.rem(column, unit) < CAP
        pick[0] = jnp.where(is_token, table, 0.0).astype(BF)
        pick[1] = jnp.where(is_token, 0.0, weighted).astype(BF)

    rows = contract_rows(pick[0], t_ref[...]) + contract_rows(pick[1], g_ref[...])
    rows = rows.astype(BF).reshape(experts, unit, rows.shape[1])
    xg_ref[0] = rows
    xg_ref[1] = rows
    gw_ref[...] = contract_rows(wtab[...], g_ref[...]).astype(BF)


def dispatch(ids, weights, tokens, grad_out, experts):
    tok, width = tokens.shape
    buf = experts * CAP
    return call(
        dispatch_kernel,
        "dispatch",
        12 * tok * buf * width,
        2 * width * (2 * tok + 5 * buf),
        grid=(width // TILE,),
        in_specs=[
            whole(ids.shape),
            whole(weights.shape),
            pl.BlockSpec((tok, TILE), lambda j: (0, j)),
            pl.BlockSpec((tok, TILE), lambda j: (0, j)),
        ],
        out_specs=[
            whole((tok, buf)),
            pl.BlockSpec((2, experts, 2 * CAP, TILE), lambda j: (0, 0, 0, j)),
            pl.BlockSpec((buf, TILE), lambda j: (0, j)),
        ],
        out_shape=[
            jax.ShapeDtypeStruct((tok, buf), BF),
            jax.ShapeDtypeStruct((2, experts, 2 * CAP, width), BF),
            jax.ShapeDtypeStruct((buf, width), BF),
        ],
        scratch_shapes=[pltpu.VMEM((2, tok, 2 * buf), BF), pltpu.VMEM((tok, buf), BF)],
    )(ids, weights, tokens, grad_out)


def regroup_kernel(here_ref, low_ref, high_ref, out_ref):
    groups, buf, tile = low_ref.shape
    experts = buf // CAP
    blocks = []
    for in_ref in (low_ref, high_ref):
        for step in range(1, groups):
            block = in_ref[lax.rem(here_ref[0] + step, groups)]
            blocks.append(block.astype(F32).reshape(experts, CAP, tile))
    rows = jnp.concatenate(blocks, axis=1).astype(BF)
    out_ref[0] = rows
    out_ref[1] = rows


def regroup(here, rows):
    groups, buf, width = rows.shape
    experts = buf // CAP
    depth = 2 * (groups - 1) * CAP
    tile = 896
    steps = width // 2 // tile
    return call(
        regroup_kernel,
        "regroup",
        0,
        2 * (groups + 2 * (groups - 1)) * buf * width,
        grid_spec=pltpu.PrefetchScalarGridSpec(
            num_scalar_prefetch=1,
            grid=(steps,),
            in_specs=[
                pl.BlockSpec((groups, buf, tile), lambda j, _: (0, 0, j)),
                pl.BlockSpec((groups, buf, tile), lambda j, _: (0, 0, j + steps)),
            ],
            out_specs=pl.BlockSpec((2, experts, depth, tile), lambda j, _: (0, 0, 0, j)),
        ),
        out_shape=jax.ShapeDtypeStruct((2, experts, depth, width // 2), BF),
    )(here, rows, rows)


def take_tokens_kernel(in_ref, out_ref):
    locs, _, tile = in_ref.shape
    rows = in_ref[...].astype(F32)[:, :CAP, :]
    out_ref[...] = rows.reshape(locs * CAP, tile).astype(BF)


def take_tokens(xg):
    locs, unit, width = xg.shape
    return call(
        take_tokens_kernel,
        "take_tokens",
        0,
        4 * locs * unit * width,
        grid=(width // TILE,),
        in_specs=[pl.BlockSpec((locs, unit, TILE), lambda j: (0, 0, j))],
        out_specs=pl.BlockSpec((locs * CAP, TILE), lambda j: (0, j)),
        out_shape=jax.ShapeDtypeStruct((locs * CAP, width), BF),
    )(xg)


def pre_kernel(x_ref, wg_ref, wu_ref, xg_ref, wd_ref, pg_ref, pu_ref, own_ref):
    @pl.when(pl.program_id(0) == 0)
    def _():
        pg_ref[...] = jnp.zeros_like(pg_ref)
        pu_ref[...] = jnp.zeros_like(pu_ref)
        own_ref[...] = jnp.zeros_like(own_ref)

    pg_ref[...] += jnp.dot(x_ref[...], wg_ref[...], preferred_element_type=F32)
    pu_ref[...] += jnp.dot(x_ref[...], wu_ref[...], preferred_element_type=F32)
    own_ref[...] += contract_cols(xg_ref[...], wd_ref[...])


def pre(x_rows, w_gate, w_up, xg_rows, w_down):
    rows, width = x_rows.shape
    own, ff = xg_rows.shape[0], w_gate.shape[1]
    return call(
        pre_kernel,
        "pre",
        2 * width * ff * (2 * rows + own),
        2 * width * (rows + own + 3 * ff),
        grid=(width // TILE,),
        in_specs=[
            pl.BlockSpec((rows, TILE), lambda j: (0, j)),
            pl.BlockSpec((TILE, ff), lambda j: (j, 0)),
            pl.BlockSpec((TILE, ff), lambda j: (j, 0)),
            pl.BlockSpec((own, TILE), lambda j: (0, j)),
            pl.BlockSpec((ff, TILE), lambda j: (0, j)),
        ],
        out_specs=[whole((rows, ff)), whole((rows, ff)), whole((own, ff))],
        out_shape=[
            jax.ShapeDtypeStruct((rows, ff), F32),
            jax.ShapeDtypeStruct((rows, ff), F32),
            jax.ShapeDtypeStruct((own, ff), F32),
        ],
    )(x_rows, w_gate, w_up, xg_rows, w_down)


def delta_kernel(
    here_ref, g_ref, low_ref, high_ref, pg_ref, pu_ref, own_ref, gx_ref, ux_ref, gl_ref, ul_ref, uo_ref, ur_ref, rest
):
    groups, span, ff = pg_ref.shape
    locs = span // CAP
    depth = (groups - 1) * CAP

    @pl.when(pl.program_id(0) == 0)
    def _():
        rest[...] = jnp.zeros_like(rest)

    both = jnp.concatenate([low_ref[...], high_ref[...]], axis=0)
    rest[...] += contract_cols(g_ref[...], both)

    @pl.when(pl.program_id(0) == pl.num_programs(0) - 1)
    def _():
        halves = rest[...].reshape(locs, 2 * depth, 2 * ff)
        gate_blocks, up_blocks, outer_blocks = [], [], []
        for step in range(groups):
            group = lax.rem(here_ref[0] + step, groups)
            if step == 0:
                hidden = own_ref[...][:, CAP:, :]
            else:
                first = (step - 1) * CAP
                hidden = (
                    halves[:, first : first + CAP, :ff]
                    + halves[:, depth + first : depth + first + CAP, ff:]
                )
            hidden = hidden.reshape(span, ff)
            gate, up = pg_ref[group], pu_ref[group]
            sig = 1.0 / (1.0 + jnp.exp(-gate))
            swish = gate * sig
            gate_delta = hidden * up * sig * (1.0 + gate * (1.0 - sig))
            up_delta = hidden * swish
            gx_ref[group] = gate_delta.astype(BF)
            ux_ref[group] = up_delta.astype(BF)
            gate_blocks.append(gate_delta.reshape(locs, CAP, ff))
            up_blocks.append(up_delta.reshape(locs, CAP, ff))
            outer_blocks.append((swish * up).reshape(locs, CAP, ff))
        gl_ref[...] = jnp.concatenate(gate_blocks, axis=1).astype(BF)
        ul_ref[...] = jnp.concatenate(up_blocks, axis=1).astype(BF)
        zero = jnp.zeros((locs, CAP, ff), F32)
        uo_ref[...] = jnp.concatenate([zero, outer_blocks[0]], axis=1).astype(BF)
        outer = jnp.concatenate(outer_blocks[1:], axis=1)
        zero = jnp.zeros((locs, depth, ff), F32)
        low = jnp.concatenate([outer, zero], axis=1)
        high = jnp.concatenate([zero, outer], axis=1)
        outer = jnp.concatenate([low, high], axis=2).astype(BF)
        ur_ref[...] = outer.reshape(locs * 2 * depth, 2 * ff)


def deltas(here, g_rest, w_down, pre_gate, pre_up, own):
    groups, span, ff = pre_gate.shape
    rest, cols = g_rest.shape
    locs = span // CAP
    tile = 896
    steps = cols // tile
    small = lambda *shape: jax.ShapeDtypeStruct(shape, BF)
    outs = [
        small(groups, span, ff),
        small(groups, span, ff),
        small(locs, groups * CAP, ff),
        small(locs, groups * CAP, ff),
        small(locs, 2 * CAP, ff),
        small(rest, 2 * ff),
    ]
    return call(
        delta_kernel,
        "deltas",
        4 * rest * cols * ff,
        2 * cols * (rest + 2 * ff) + 14 * groups * span * ff,
        grid_spec=pltpu.PrefetchScalarGridSpec(
            num_scalar_prefetch=1,
            grid=(steps,),
            in_specs=[
                pl.BlockSpec((rest, tile), lambda j, _: (0, j)),
                pl.BlockSpec((ff, tile), lambda j, _: (0, j)),
                pl.BlockSpec((ff, tile), lambda j, _: (0, j + steps)),
                whole(pre_gate.shape),
                whole(pre_up.shape),
                whole(own.shape),
            ],
            out_specs=[whole(o.shape) for o in outs],
            scratch_shapes=[pltpu.VMEM((rest, 2 * ff), F32)],
        ),
        out_shape=outs,
    )(here, g_rest, w_down, w_down, pre_gate, pre_up, own)


def row_part_kernel(gd_ref, ud_ref, wg_ref, wu_ref, out_ref):
    total = contract_cols(gd_ref[...], wg_ref[...]) + contract_cols(ud_ref[...], wu_ref[...])
    out_ref[...] = total.astype(BF)


def row_part(gate_delta, up_delta, w_gate, w_up, first, count):
    rows, ff = gate_delta.shape
    skip = first // TILE
    return call(
        row_part_kernel,
        "row_part",
        4 * rows * ff * count,
        2 * count * (rows + 2 * ff),
        grid=(count // TILE,),
        in_specs=[
            whole((rows, ff)),
            whole((rows, ff)),
            pl.BlockSpec((TILE, ff), lambda j: (j + skip, 0)),
            pl.BlockSpec((TILE, ff), lambda j: (j + skip, 0)),
        ],
        out_specs=pl.BlockSpec((rows, TILE), lambda j: (0, j)),
        out_shape=jax.ShapeDtypeStruct((rows, count), BF),
    )(gate_delta, up_delta, w_gate, w_up)


def row_grads_kernel(x_ref, gd_ref, ud_ref, gate_ref, up_ref):
    gate_ref[...] = contract_rows(x_ref[...], gd_ref[...]).astype(BF)
    up_ref[...] = contract_rows(x_ref[...], ud_ref[...]).astype(BF)


def row_grads(x_rows, gate_delta, up_delta):
    rows, width = x_rows.shape
    ff = gate_delta.shape[1]
    return call(
        row_grads_kernel,
        "row_grads",
        4 * rows * width * ff,
        2 * width * (rows + 2 * ff),
        grid=(width // TILE,),
        in_specs=[
            pl.BlockSpec((rows, TILE), lambda j: (0, j)),
            whole((rows, ff)),
            whole((rows, ff)),
        ],
        out_specs=[pl.BlockSpec((TILE, ff), lambda j: (j, 0))] * 2,
        out_shape=[jax.ShapeDtypeStruct((width, ff), BF)] * 2,
    )(x_rows, gate_delta, up_delta)


def down_kernel(uo_ref, low_ref, high_ref, ur_ref, g_ref, out_ref):
    ff = uo_ref.shape[1]
    rest = contract_rows(ur_ref[...], g_ref[...])
    outer = uo_ref[...]
    out_ref[0] = (contract_rows(outer, low_ref[...]) + rest[:ff]).astype(BF)
    out_ref[1] = (contract_rows(outer, high_ref[...]) + rest[ff:]).astype(BF)


def down(outer_own, xg_rows, outer_rest, g_rest):
    own, ff = outer_own.shape
    rest, cols = g_rest.shape
    tile = 896
    steps = cols // tile
    halves = call(
        down_kernel,
        "down",
        4 * (own + rest) * cols * ff,
        2 * cols * (2 * own + rest + 2 * ff),
        grid=(steps,),
        in_specs=[
            whole((own, ff)),
            pl.BlockSpec((own, tile), lambda j: (0, j)),
            pl.BlockSpec((own, tile), lambda j: (0, j + steps)),
            whole((rest, 2 * ff)),
            pl.BlockSpec((rest, tile), lambda j: (0, j)),
        ],
        out_specs=pl.BlockSpec((2, ff, tile), lambda j: (0, 0, j)),
        out_shape=jax.ShapeDtypeStruct((2, ff, cols), BF),
    )(outer_own, xg_rows, xg_rows, outer_rest, g_rest)
    return jnp.concatenate([halves[0], halves[1]], axis=1)


def fold_kernel(here_ref, in_ref, out_ref):
    _, experts, depth, tile = in_ref.shape
    groups = depth // CAP
    total = in_ref[0].astype(F32) + in_ref[1].astype(F32)
    for step in range(groups):
        part = total[:, step * CAP : (step + 1) * CAP, :]
        group = lax.rem(here_ref[0] + step, groups)
        out_ref[group] = part.reshape(experts * CAP, tile).astype(BF)


def fold(here, home):
    _, experts, depth, width = home.shape
    groups = depth // CAP
    return call(
        fold_kernel,
        "fold",
        experts * depth * width,
        6 * experts * depth * width,
        mib=20,
        grid_spec=pltpu.PrefetchScalarGridSpec(
            num_scalar_prefetch=1,
            grid=(width // TILE,),
            in_specs=[pl.BlockSpec((2, experts, depth, TILE), lambda j, _: (0, 0, 0, j))],
            out_specs=pl.BlockSpec((groups, experts * CAP, TILE), lambda j, _: (0, 0, j)),
        ),
        out_shape=jax.ShapeDtypeStruct((groups, experts * CAP, width), BF),
    )(here, home)


def combine_kernel(split, table_ref, ring_ref, wide_ref, out_ref):
    table = table_ref[...]

    @pl.when(pl.program_id(0) < split)
    def _():
        out_ref[...] = jnp.dot(table, ring_ref[...], preferred_element_type=F32).astype(BF)

    @pl.when(pl.program_id(0) >= split)
    def _():
        count, _, tile = wide_ref.shape
        rows = wide_ref[...].astype(F32).reshape(count * CAP, tile).astype(BF)
        both = jnp.concatenate([table, table], axis=1)
        out_ref[...] = jnp.dot(both, rows, preferred_element_type=F32).astype(BF)


def combine(table, ring, wide):
    tok, buf = table.shape
    width = ring.shape[1] + wide.shape[2]
    split = ring.shape[1] // TILE
    return call(
        functools.partial(combine_kernel, split),
        "combine",
        2 * tok * buf * width,
        2 * width * (tok + 2 * buf),
        mib=20,
        grid=(width // TILE,),
        in_specs=[
            whole((tok, buf)),
            pl.BlockSpec((buf, TILE), lambda j: (0, jnp.minimum(j, split - 1))),
            pl.BlockSpec((wide.shape[0], CAP, TILE), lambda j: (0, 0, jnp.maximum(j - split, 0))),
        ],
        out_specs=pl.BlockSpec((tok, TILE), lambda j: (0, j)),
        out_shape=jax.ShapeDtypeStruct((tok, width), BF),
    )(table, ring, wide)


def over_loc(a):
    return lax.all_to_all(a, "loc", split_axis=0, concat_axis=0, tiled=True)


def body(tokens, grad_out, expert_ids, route_weight, gate_weight, up_weight, down_weight):
    groups = lax.axis_size("grp")
    locs = lax.axis_size("loc")
    here = lax.axis_index("grp").astype(jnp.int32)[None]
    experts = locs // 2
    width = tokens.shape[1]
    buf = experts * CAP
    span = locs * CAP
    ring_cols = 3072
    wide_cols = width - ring_cols

    w_gate, w_up, w_down = gate_weight[0], up_weight[0], down_weight[0]
    ff = w_gate.shape[1]

    table, xg_send, g_send = dispatch(expert_ids, route_weight, tokens, grad_out, experts)

    xg = over_loc(xg_send.reshape(locs, 2 * CAP, width))
    g_ring = lax.all_gather(g_send, "grp", axis=0, tiled=False)
    x_rows = lax.all_gather(take_tokens(xg), "grp", axis=0, tiled=True)
    g_rest = over_loc(regroup(here, g_ring).reshape(locs, 2 * (groups - 1) * CAP, width // 2))
    g_rest = g_rest.reshape(locs * 2 * (groups - 1) * CAP, width // 2)
    xg_rows = xg.reshape(locs * 2 * CAP, width)

    pre_gate, pre_up, own = pre(x_rows, w_gate, w_up, xg_rows, w_down)
    gate_x, up_x, gate_l, up_l, outer_own, outer_rest = deltas(
        here,
        g_rest,
        w_down,
        pre_gate.reshape(groups, span, ff),
        pre_up.reshape(groups, span, ff),
        own.reshape(locs, 2 * CAP, ff),
    )
    rows = groups * span
    gate_x, up_x = gate_x.reshape(rows, ff), up_x.reshape(rows, ff)

    part_ring = row_part(gate_l.reshape(rows, ff), up_l.reshape(rows, ff), w_gate, w_up, 0, ring_cols)
    part_ring, gate_x, up_x = lax.optimization_barrier((part_ring, gate_x, up_x))
    home_ring = over_loc(part_ring.reshape(locs, groups * CAP, ring_cols))
    part_wide = row_part(gate_x, up_x, w_gate, w_up, ring_cols, wide_cols)
    reduced = lax.psum_scatter(
        part_wide.reshape(groups, span, wide_cols), "grp", scatter_dimension=0, tiled=True
    )

    part_wide, gate_x, up_x, outer_own, outer_rest = lax.optimization_barrier(
        (part_wide, gate_x, up_x, outer_own, outer_rest)
    )
    gate_grad, up_grad = row_grads(x_rows, gate_x, up_x)
    down_grad = down(outer_own.reshape(locs * 2 * CAP, ff), xg_rows, outer_rest, g_rest)
    home_ring, gate_grad, up_grad, down_grad = lax.optimization_barrier(
        (home_ring, gate_grad, up_grad, down_grad)
    )

    folded = fold(here, home_ring.reshape(2, experts, groups * CAP, ring_cols))
    ring = lax.psum_scatter(folded, "grp", scatter_dimension=0, tiled=True)
    home_wide = over_loc(reduced.reshape(locs, CAP, wide_cols))
    tokens_grad = combine(table, ring.reshape(buf, ring_cols), home_wide)
    return (tokens_grad, gate_grad[None], up_grad[None], down_grad[None])


def solution(mesh):
    in_specs = (
        P(("grp", "loc"), None),
        P(("grp", "loc"), None),
        P(("grp", "loc"), None),
        P(("grp", "loc"), None),
        P("loc", None, "grp"),
        P("loc", None, "grp"),
        P("loc", "grp", None),
    )
    out_specs = (
        P(("grp", "loc"), None),
        P("loc", None, "grp"),
        P("loc", None, "grp"),
        P("loc", "grp", None),
    )
    return jax.shard_map(body, mesh=mesh, in_specs=in_specs, out_specs=out_specs, check_vma=False)
```

```python
import functools

import jax
import jax.numpy as jnp
from jax import lax
from jax.experimental import pallas as pl
from jax.experimental.pallas import tpu as pltpu
from jax.sharding import PartitionSpec as P

CAP = 4
BF = jnp.bfloat16
F32 = jnp.float32
TILE = 512


def contract_rows(left, right):
    return lax.dot_general(left, right, (((0,), (0,)), ((), ())), preferred_element_type=F32)


def contract_cols(left, right):
    return lax.dot_general(left, right, (((1,), (1,)), ((), ())), preferred_element_type=F32)


def whole(shape):
    return pl.BlockSpec(shape, lambda *_: (0,) * len(shape))


def call(kernel, name, flops, nbytes, mib=56, **kwargs):
    return pl.pallas_call(
        kernel,
        name=name,
        compiler_params=pltpu.CompilerParams(vmem_limit_bytes=mib << 20),
        cost_estimate=pl.CostEstimate(flops=flops, bytes_accessed=nbytes, transcendentals=0),
        **kwargs,
    )


def dispatch_kernel(ids_ref, w_ref, tl_ref, th_ref, gl_ref, gh_ref, table_ref, xg_ref, ring_ref, pick):
    topk, tok = ids_ref.shape
    experts = xg_ref.shape[1]
    buf = table_ref.shape[0]
    unit = 2 * CAP
    step = pl.program_id(0)

    def tables(count, per_expert):
        slot_row = lax.broadcasted_iota(jnp.int32, (count, tok), 0)
        expert = lax.div(slot_row, per_expert)
        weights = w_ref[...].astype(F32)
        chosen = jnp.zeros((count, tok), F32)
        weight = jnp.zeros((count, tok), F32)
        for k in range(topk):
            hit = ids_ref[k : k + 1, :] == expert
            chosen = jnp.where(hit, 1.0, chosen)
            weight = jnp.where(hit, weights[k : k + 1, :], weight)
        before = lax.broadcasted_iota(jnp.int32, (tok, tok), 0)
        after = lax.broadcasted_iota(jnp.int32, (tok, tok), 1)
        earlier = jnp.where(before < after, 1.0, 0.0).astype(BF)
        slot = jnp.dot(chosen.astype(BF), earlier, preferred_element_type=F32)
        mine = (chosen > 0.5) & (slot == lax.rem(slot_row, CAP).astype(F32))
        return jnp.where(mine, 1.0, 0.0), jnp.where(mine, weight, 0.0), slot_row

    @pl.when(step == 0)
    def _():
        table, weighted, slot_row = tables(experts * unit, unit)
        low = lax.rem(slot_row, unit) < CAP
        pick[0] = jnp.where(low, table, 0.0).astype(BF)
        pick[1] = jnp.where(low, 0.0, table).astype(BF)
        pick[2] = jnp.where(low, weighted, 0.0).astype(BF)
        pick[3] = jnp.where(low, 0.0, weighted).astype(BF)

    def rows(first, low_ref, high_ref):
        total = jnp.dot(pick[first], low_ref[...], preferred_element_type=F32)
        total += jnp.dot(pick[first + 1], high_ref[...], preferred_element_type=F32)
        return total.astype(BF)

    def put(value):
        value = value.reshape(experts, unit, value.shape[1])
        xg_ref[0] = value
        xg_ref[1] = value

    last = pl.num_programs(0) - 1

    @pl.when(step < last)
    def _():
        put(rows(0, tl_ref, th_ref))

    @pl.when(step == last)
    def _():
        put(rows(2, gl_ref, gh_ref))
        table_ref[...] = tables(buf, CAP)[0].astype(BF)

    @pl.when(step < last - 1)
    def _():
        ring_ref[...] = rows(2, gl_ref, gh_ref)


def dispatch(ids, weights, tokens, grad_out, experts):
    tok, width = tokens.shape
    buf = experts * CAP
    unit = 2 * CAP
    half = width // 2
    steps = half // TILE + 1
    parts = steps - 2
    g_low = lambda j: (0, jnp.where(j < parts, j + 2, 0))
    g_high = lambda j: (0, jnp.where(j < parts, j + 2 + parts, 1))
    return call(
        dispatch_kernel,
        "dispatch",
        8 * tok * buf * 2 * width,
        2 * width * (2 * tok + 4 * buf),
        grid=(steps,),
        in_specs=[
            whole(ids.shape),
            whole(weights.shape),
            pl.BlockSpec((tok, TILE), lambda j: (0, jnp.minimum(j, steps - 2))),
            pl.BlockSpec((tok, TILE), lambda j: (0, steps - 1 + jnp.minimum(j, steps - 2))),
            pl.BlockSpec((tok, TILE), g_low),
            pl.BlockSpec((tok, TILE), g_high),
        ],
        out_specs=[
            whole((buf, tok)),
            pl.BlockSpec((2, experts, unit, TILE), lambda j: (0, 0, 0, j)),
            pl.BlockSpec((experts * unit, TILE), lambda j: (0, jnp.minimum(j, parts - 1))),
        ],
        out_shape=[
            jax.ShapeDtypeStruct((buf, tok), BF),
            jax.ShapeDtypeStruct((2, experts, unit, half + TILE), BF),
            jax.ShapeDtypeStruct((experts * unit, half - TILE), BF),
        ],
        scratch_shapes=[pltpu.VMEM((4, experts * unit, tok), BF)],
    )(ids, weights, tokens, tokens, grad_out, grad_out)


def regroup_kernel(own_ref, next_ref, far_top_ref, far_low_ref, prev_ref, out_ref):
    _, experts, depth, tile = out_ref.shape
    unit = 2 * CAP
    mid = experts // 2

    def rows(ref):
        return ref[...].reshape(ref.shape[0] // unit, unit, tile)

    for h in range(2):
        out_ref[h, :, :unit, :] = rows(own_ref)
        out_ref[h, :, unit : 2 * unit, :] = rows(next_ref)
        out_ref[h, :mid, 2 * unit : 3 * unit, :] = rows(far_top_ref)
        out_ref[h, mid:, 2 * unit : 3 * unit, :] = rows(far_low_ref)
        out_ref[h, :, 3 * unit :, :] = rows(prev_ref)


def regroup(blocks):
    count, cols = blocks[0].shape
    unit = 2 * CAP
    experts = count // unit
    return call(
        regroup_kernel,
        "regroup",
        0,
        24 * count * cols,
        grid=(cols // TILE,),
        in_specs=[pl.BlockSpec((b.shape[0], TILE), lambda j: (0, j)) for b in blocks],
        out_specs=pl.BlockSpec((2, experts, 4 * unit, TILE), lambda j: (0, 0, 0, j)),
        out_shape=jax.ShapeDtypeStruct((2, experts, 4 * unit, cols), BF),
    )(*blocks)


def pre_kernel(x_ref, gl_ref, gh_ref, ul_ref, uh_ref, dl_ref, dh_ref, slope_ref, swish_ref, part_ref, outer_ref, acc):
    step = pl.program_id(0)
    last = pl.num_programs(0) - 1

    @pl.when(step == 0)
    def _():
        acc[...] = jnp.zeros_like(acc)

    @pl.when(step < last)
    def _():
        weights = jnp.concatenate([gl_ref[...], gh_ref[...], ul_ref[...], uh_ref[...]], axis=1)
        acc[...] += jnp.dot(x_ref[...], weights, preferred_element_type=F32)

    @pl.when(step == last)
    def _():
        count, ff = swish_ref.shape
        locs = count // CAP
        weights = jnp.concatenate([dl_ref[...], dh_ref[...]], axis=0)

        def fold_halves(value):
            value = value.reshape(locs, 2 * CAP, 2 * ff)
            return (value[:, :CAP, :ff] + value[:, CAP:, ff:]).reshape(count, ff)

        gate = fold_halves(acc[:, : 2 * ff])
        up = fold_halves(acc[:, 2 * ff :])
        part_ref[...] = fold_halves(contract_cols(x_ref[...], weights))
        sig = 1.0 / (1.0 + jnp.exp(-gate))
        swish = gate * sig
        slope_ref[...] = up * sig * (1.0 + gate * (1.0 - sig))
        swish_ref[...] = swish
        outer_ref[...] = swish * up


def pre(block, w_gate, w_up, w_down):
    rows, cols = block.shape
    ff = w_gate.shape[1]
    steps = cols // TILE
    count = rows // 2
    low = pl.BlockSpec((TILE, ff), lambda j: (jnp.minimum(j, steps - 2), 0))
    high = pl.BlockSpec((TILE, ff), lambda j: (steps - 1 + jnp.minimum(j, steps - 2), 0))
    return call(
        pre_kernel,
        "pre",
        8 * rows * cols * ff,
        2 * cols * (rows + 4 * ff),
        mib=16,
        grid=(steps,),
        in_specs=[
            pl.BlockSpec((rows, TILE), lambda j: (0, j)),
            low,
            high,
            low,
            high,
            pl.BlockSpec((ff, TILE), lambda j: (0, 0)),
            pl.BlockSpec((ff, TILE), lambda j: (0, 1)),
        ],
        out_specs=[whole((count, ff))] * 4,
        out_shape=[jax.ShapeDtypeStruct((count, ff), F32)] * 4,
        scratch_shapes=[pltpu.VMEM((rows, 4 * ff), F32)],
    )(block, w_gate, w_gate, w_up, w_up, w_down, w_down)


def delta_kernel(here_ref, g_ref, low_ref, high_ref, *refs):
    slopes, swishes, parts = refs[:5], refs[5:10], refs[10:15]
    gx_ref, ux_ref, gl_ref, ul_ref, acc = refs[15:]
    groups, span, ff = gx_ref.shape
    locs = span // CAP
    unit = 2 * CAP

    @pl.when(pl.program_id(0) == 0)
    def _():
        acc[...] = jnp.zeros_like(acc)

    both = jnp.concatenate([low_ref[...], high_ref[...]], axis=0)
    acc[...] += contract_cols(g_ref[...], both)

    @pl.when(pl.program_id(0) == pl.num_programs(0) - 1)
    def _():
        def block(refs, step):
            own, after, top, bottom, before = refs
            if step == 2:
                return jnp.concatenate([top[...], bottom[...]], axis=0)
            return (own, after, None, before)[step][...]

        halves = acc[...].reshape(locs, groups * unit, 2 * ff)
        for step in range(groups):
            group = lax.rem(here_ref[0] + step, groups)
            first = step * unit
            hidden = (
                halves[:, first : first + CAP, :ff] + halves[:, first + CAP : first + unit, ff:]
            ).reshape(span, ff) + block(parts, step)
            gate = hidden * block(slopes, step)
            up = hidden * block(swishes, step)
            gx_ref[group] = gate.astype(BF)
            ux_ref[group] = up.astype(BF)
            gl_ref[:, step * CAP : (step + 1) * CAP, :] = gate.reshape(locs, CAP, ff).astype(BF)
            ul_ref[:, step * CAP : (step + 1) * CAP, :] = up.reshape(locs, CAP, ff).astype(BF)


def deltas(here, g_rows, w_down, slopes, swishes, parts):
    rows, cols = g_rows.shape
    ff = w_down.shape[0]
    groups = 4
    span = rows // 2 // groups
    locs = span // CAP
    steps = cols // TILE
    small = lambda *shape: jax.ShapeDtypeStruct(shape, BF)
    outs = [
        small(groups, span, ff),
        small(groups, span, ff),
        small(locs, groups * CAP, ff),
        small(locs, groups * CAP, ff),
    ]
    blocks = [*slopes, *swishes, *parts]
    return call(
        delta_kernel,
        "deltas",
        4 * rows * cols * ff,
        2 * cols * (rows + 2 * ff) + 16 * groups * span * ff,
        grid_spec=pltpu.PrefetchScalarGridSpec(
            num_scalar_prefetch=1,
            grid=(steps,),
            in_specs=[
                pl.BlockSpec((rows, TILE), lambda j, _: (0, j)),
                pl.BlockSpec((ff, TILE), lambda j, _: (0, j + 2)),
                pl.BlockSpec((ff, TILE), lambda j, _: (0, j + 2 + steps)),
                *[whole(b.shape) for b in blocks],
            ],
            out_specs=[whole(o.shape) for o in outs],
            scratch_shapes=[pltpu.VMEM((rows, 2 * ff), F32)],
        ),
        out_shape=outs,
    )(here, g_rows, w_down, w_down, *blocks)


def row_part_kernel(gd_ref, ud_ref, wg_ref, wu_ref, out_ref):
    total = contract_cols(gd_ref[...], wg_ref[...]) + contract_cols(ud_ref[...], wu_ref[...])
    out_ref[...] = total.astype(BF)


def row_part(gate_delta, up_delta, w_gate, w_up, first, count):
    rows, ff = gate_delta.shape
    skip = first // TILE
    return call(
        row_part_kernel,
        "row_part",
        4 * rows * ff * count,
        2 * count * (rows + 2 * ff),
        grid=(count // TILE,),
        in_specs=[
            whole((rows, ff)),
            whole((rows, ff)),
            pl.BlockSpec((TILE, ff), lambda j: (j + skip, 0)),
            pl.BlockSpec((TILE, ff), lambda j: (j + skip, 0)),
        ],
        out_specs=pl.BlockSpec((rows, TILE), lambda j: (0, j)),
        out_shape=jax.ShapeDtypeStruct((rows, count), BF),
    )(gate_delta, up_delta, w_gate, w_up)


def row_grads_kernel(here_ref, gx_ref, ux_ref, own_ref, next_ref, top_ref, bottom_ref, prev_ref, gate_ref, up_ref, wide):
    groups, span, ff = gx_ref.shape
    locs = span // CAP
    rows = 2 * span

    @pl.when(pl.program_id(0) == 0)
    def _():
        zero = jnp.zeros((locs, CAP, ff), F32)
        for step in range(groups):
            group = lax.rem(here_ref[0] + step, groups)
            gate = gx_ref[group].astype(F32).reshape(locs, CAP, ff)
            up = ux_ref[group].astype(F32).reshape(locs, CAP, ff)
            low = jnp.concatenate([gate, zero, up, zero], axis=2)
            high = jnp.concatenate([zero, gate, zero, up], axis=2)
            both = jnp.concatenate([low, high], axis=1)
            wide[step] = both.reshape(rows, 4 * ff).astype(BF)

    total = contract_rows(own_ref[...], wide[0]) + contract_rows(next_ref[...], wide[1])
    total += contract_rows(top_ref[...], wide[2, :span]) + contract_rows(bottom_ref[...], wide[2, span:])
    total += contract_rows(prev_ref[...], wide[3])
    total = total.astype(BF)
    gate_ref[0] = total[:, :ff]
    gate_ref[1] = total[:, ff : 2 * ff]
    up_ref[0] = total[:, 2 * ff : 3 * ff]
    up_ref[1] = total[:, 3 * ff :]


def row_grads(here, gate_x, up_x, blocks):
    groups, span, ff = gate_x.shape
    half = blocks[0].shape[1] - TILE
    out = jax.ShapeDtypeStruct((2, half, ff), BF)
    gate, up = call(
        row_grads_kernel,
        "row_grads",
        16 * groups * span * half * ff,
        4 * half * (groups * span + 2 * ff),
        grid_spec=pltpu.PrefetchScalarGridSpec(
            num_scalar_prefetch=1,
            grid=(half // TILE,),
            in_specs=[
                whole(gate_x.shape),
                whole(up_x.shape),
                *[pl.BlockSpec((b.shape[0], TILE), lambda j, _: (0, j)) for b in blocks],
            ],
            out_specs=[pl.BlockSpec((2, TILE, ff), lambda j, _: (0, j, 0))] * 2,
            scratch_shapes=[pltpu.VMEM((groups, 2 * span, 4 * ff), BF)],
        ),
        out_shape=[out, out],
    )(here, gate_x, up_x, *blocks)
    return gate.reshape(2 * half, ff), up.reshape(2 * half, ff)


def down_kernel(g_ref, *refs):
    outers, blocks, out_ref, wide = refs[:5], refs[5:10], refs[10], refs[11]
    span, ff = outers[0].shape
    locs = span // CAP
    unit = 2 * CAP
    step = pl.program_id(0)
    tile = g_ref.shape[1]

    def spread(outer):
        rows = outer.reshape(outer.shape[0] // CAP, CAP, ff)
        zero = jnp.zeros_like(rows)
        low = jnp.concatenate([rows, zero], axis=2)
        high = jnp.concatenate([zero, rows], axis=2)
        return jnp.concatenate([low, high], axis=1)

    def put(total, low, high):
        total = total.astype(BF)
        out_ref[:, pl.ds(pl.multiple_of(low, tile), tile)] = total[:ff]
        out_ref[:, pl.ds(pl.multiple_of(high, tile), tile)] = total[ff:]

    @pl.when(step == 0)
    def _():
        own, after, top, bottom, before = [r[...] for r in outers]
        ordered = [own, after, jnp.concatenate([top, bottom], axis=0), before]
        for k, outer in enumerate(ordered):
            wide[:, k * unit : (k + 1) * unit, :] = spread(outer).astype(BF)
        total = jnp.zeros((2 * ff, tile), F32)
        for outer, block in zip(outers, blocks):
            rows = 2 * outer.shape[0]
            total += contract_rows(spread(outer[...]).reshape(rows, 2 * ff).astype(BF), block[...])
        put(total, 0, tile)

    rows = wide[...].reshape(g_ref.shape[0], 2 * ff)
    first = (step + 2) * tile
    put(contract_rows(rows, g_ref[...]), first, first + pl.num_programs(0) * tile)


def down(g_rows, outers, blocks):
    rows, cols = g_rows.shape
    ff = outers[0].shape[1]
    steps = cols // TILE
    last = blocks[0].shape[1] // TILE - 1
    locs = outers[0].shape[0] // CAP
    width = 2 * (cols + TILE)
    return call(
        down_kernel,
        "down",
        4 * rows * (cols + TILE) * ff,
        2 * (cols + TILE) * (rows + 2 * ff),
        grid=(steps,),
        in_specs=[
            pl.BlockSpec((rows, TILE), lambda j: (0, j)),
            *[whole(o.shape) for o in outers],
            *[pl.BlockSpec((b.shape[0], TILE), lambda j: (0, last)) for b in blocks],
        ],
        out_specs=whole((ff, width)),
        out_shape=jax.ShapeDtypeStruct((ff, width), BF),
        scratch_shapes=[pltpu.VMEM((locs, rows // locs, 2 * ff), BF)],
    )(g_rows, *outers, *blocks)


def fold_kernel(here_ref, in_ref, out_ref):
    _, experts, depth, tile = in_ref.shape
    groups = depth // CAP
    total = in_ref[0].astype(F32) + in_ref[1].astype(F32)
    for step in range(groups):
        part = total[:, step * CAP : (step + 1) * CAP, :]
        group = lax.rem(here_ref[0] + step, groups)
        out_ref[group] = part.reshape(experts * CAP, tile).astype(BF)


def fold(here, home):
    _, experts, depth, width = home.shape
    groups = depth // CAP
    return call(
        fold_kernel,
        "fold",
        experts * depth * width,
        6 * experts * depth * width,
        mib=20,
        grid_spec=pltpu.PrefetchScalarGridSpec(
            num_scalar_prefetch=1,
            grid=(width // TILE,),
            in_specs=[pl.BlockSpec((2, experts, depth, TILE), lambda j, _: (0, 0, 0, j))],
            out_specs=pl.BlockSpec((groups, experts * CAP, TILE), lambda j, _: (0, 0, j)),
        ),
        out_shape=jax.ShapeDtypeStruct((groups, experts * CAP, width), BF),
    )(here, home)


def combine_kernel(split, table_ref, ring_ref, wide_ref, out_ref):
    table = table_ref[...]

    @pl.when(pl.program_id(0) < split)
    def _():
        out_ref[...] = contract_rows(table, ring_ref[...]).astype(BF)

    @pl.when(pl.program_id(0) >= split)
    def _():
        count, _, tile = wide_ref.shape
        rows = wide_ref[...].astype(F32).reshape(count * CAP, tile).astype(BF)
        both = jnp.concatenate([table, table], axis=0)
        out_ref[...] = contract_rows(both, rows).astype(BF)


def combine(table, ring, wide):
    buf, tok = table.shape
    width = ring.shape[1] + wide.shape[2]
    split = ring.shape[1] // TILE
    return call(
        functools.partial(combine_kernel, split),
        "combine",
        2 * tok * buf * width,
        2 * width * (tok + 2 * buf),
        mib=20,
        grid=(width // TILE,),
        in_specs=[
            whole((buf, tok)),
            pl.BlockSpec((buf, TILE), lambda j: (0, jnp.minimum(j, split - 1))),
            pl.BlockSpec((wide.shape[0], CAP, TILE), lambda j: (0, 0, jnp.maximum(j - split, 0))),
        ],
        out_specs=pl.BlockSpec((tok, TILE), lambda j: (0, j)),
        out_shape=jax.ShapeDtypeStruct((tok, width), BF),
    )(table, ring, wide)


def over_loc(a):
    return lax.all_to_all(a, "loc", split_axis=0, concat_axis=0, tiled=True)


def ring_gather(own):
    groups = lax.axis_size("grp")
    up = [(i, (i + 1) % groups) for i in range(groups)]
    down_ring = [(i, (i - 1) % groups) for i in range(groups)]
    mid = own.shape[0] // 2
    before = lax.ppermute(own, "grp", up)
    after = lax.ppermute(own, "grp", down_ring)
    top = lax.ppermute(before[:mid], "grp", up)
    bottom = lax.ppermute(after[mid:], "grp", down_ring)
    return [own, after, top, bottom, before]


def body(tokens, grad_out, expert_ids, route_weight, gate_weight, up_weight, down_weight):
    groups = lax.axis_size("grp")
    locs = lax.axis_size("loc")
    here = lax.axis_index("grp").astype(jnp.int32)[None]
    experts = locs // 2
    width = tokens.shape[1]
    buf = experts * CAP
    span = locs * CAP
    unit = 2 * CAP
    ring_cols = 3072
    wide_cols = width - ring_cols

    w_gate, w_up, w_down = gate_weight[0], up_weight[0], down_weight[0]
    ff = w_gate.shape[1]

    table, xg_send, g_send = dispatch(expert_ids.T, route_weight.T, tokens, grad_out, experts)

    xg = over_loc(xg_send.reshape(locs, unit, xg_send.shape[3]))
    g_out = regroup(ring_gather(g_send))
    g_rows = over_loc(g_out.reshape(locs, groups * unit, g_out.shape[3]))
    g_rows = g_rows.reshape(locs * groups * unit, g_out.shape[3])
    blocks = ring_gather(xg.reshape(locs * unit, xg.shape[2]))

    slopes, swishes, parts, outers = zip(*[pre(b, w_gate, w_up, w_down) for b in blocks])
    gate_x, up_x, gate_l, up_l = deltas(here, g_rows, w_down, slopes, swishes, parts)
    rows = groups * span

    part_ring = row_part(gate_l.reshape(rows, ff), up_l.reshape(rows, ff), w_gate, w_up, 0, ring_cols)
    part_ring, gate_x, up_x = lax.optimization_barrier((part_ring, gate_x, up_x))
    home_ring = over_loc(part_ring.reshape(locs, groups * CAP, ring_cols))
    part_wide = row_part(
        gate_x.reshape(rows, ff), up_x.reshape(rows, ff), w_gate, w_up, ring_cols, wide_cols
    )
    reduced = lax.psum_scatter(
        part_wide.reshape(groups, span, wide_cols), "grp", scatter_dimension=0, tiled=True
    )

    part_wide, gate_x, up_x, outers = lax.optimization_barrier((part_wide, gate_x, up_x, outers))
    gate_grad, up_grad = row_grads(here, gate_x, up_x, blocks)
    down_grad = down(g_rows, outers, blocks)
    home_ring, gate_grad, up_grad, down_grad = lax.optimization_barrier(
        (home_ring, gate_grad, up_grad, down_grad)
    )

    folded = fold(here, home_ring.reshape(2, experts, groups * CAP, ring_cols))
    ring = lax.psum_scatter(folded, "grp", scatter_dimension=0, tiled=True)
    home_wide = over_loc(reduced.reshape(locs, CAP, wide_cols))
    tokens_grad = combine(table, ring.reshape(buf, ring_cols), home_wide)
    return (tokens_grad, gate_grad[None], up_grad[None], down_grad[None])


def solution(mesh):
    in_specs = (
        P(("grp", "loc"), None),
        P(("grp", "loc"), None),
        P(("grp", "loc"), None),
        P(("grp", "loc"), None),
        P("loc", None, "grp"),
        P("loc", None, "grp"),
        P("loc", "grp", None),
    )
    out_specs = (
        P(("grp", "loc"), None),
        P("loc", None, "grp"),
        P("loc", None, "grp"),
        P("loc", "grp", None),
    )
    return jax.shard_map(body, mesh=mesh, in_specs=in_specs, out_specs=out_specs, check_vma=False)
```

```python
import functools

import jax
import jax.numpy as jnp
from jax import lax
from jax.experimental import pallas as pl
from jax.experimental.pallas import tpu as pltpu
from jax.sharding import PartitionSpec as P

CAP = 4
BF = jnp.bfloat16
F32 = jnp.float32
TILE = 512
ANY = pl.BlockSpec(memory_space=pl.ANY)
VMEM = pl.BlockSpec(memory_space=pltpu.VMEM)


def contract_rows(left, right):
    return lax.dot_general(left, right, (((0,), (0,)), ((), ())), preferred_element_type=F32)


def contract_cols(left, right):
    return lax.dot_general(left, right, (((1,), (1,)), ((), ())), preferred_element_type=F32)


def whole(shape):
    return pl.BlockSpec(shape, lambda *_: (0,) * len(shape))


def call(kernel, name, flops, nbytes, mib=56, **kwargs):
    return pl.pallas_call(
        kernel,
        name=name,
        compiler_params=pltpu.CompilerParams(vmem_limit_bytes=mib << 20),
        cost_estimate=pl.CostEstimate(flops=flops, bytes_accessed=nbytes, transcendentals=0),
        **kwargs,
    )


def dispatch_gradient_kernel(ids_ref, w_ref, g_ref, table_ref, pick_ref, share_ref, ring_ref, held, sem):
    load = pltpu.make_async_copy(g_ref, held, sem.at[0])
    load.start()
    topk, tok = ids_ref.shape
    buf = table_ref.shape[0]
    unit = 2 * CAP
    share = share_ref.shape[1]
    cols = ring_ref.shape[1]

    def tables(count, per_expert):
        slot_row = lax.broadcasted_iota(jnp.int32, (count, tok), 0)
        expert = lax.div(slot_row, per_expert)
        weights = w_ref[...].astype(F32)
        chosen = jnp.zeros((count, tok), F32)
        weight = jnp.zeros((count, tok), F32)
        for k in range(topk):
            hit = ids_ref[k : k + 1, :] == expert
            chosen = jnp.where(hit, 1.0, chosen)
            weight = jnp.where(hit, weights[k : k + 1, :], weight)
        before = lax.broadcasted_iota(jnp.int32, (tok, tok), 0)
        after = lax.broadcasted_iota(jnp.int32, (tok, tok), 1)
        earlier = jnp.where(before < after, 1.0, 0.0).astype(BF)
        slot = jnp.dot(chosen.astype(BF), earlier, preferred_element_type=F32)
        mine = (chosen > 0.5) & (slot == lax.rem(slot_row, CAP).astype(F32))
        return jnp.where(mine, 1.0, 0.0), jnp.where(mine, weight, 0.0), slot_row

    table_ref[...] = tables(buf, CAP)[0].astype(BF)
    table, weighted, slot_row = tables(2 * buf, unit)
    low = lax.rem(slot_row, unit) < CAP
    pick_ref[0] = jnp.where(low, table, 0.0).astype(BF)
    pick_ref[1] = jnp.where(low, 0.0, table).astype(BF)
    both = jnp.concatenate(
        [jnp.where(low, weighted, 0.0).astype(BF), jnp.where(low, 0.0, weighted).astype(BF)], axis=1
    )
    load.wait()

    def rows(first, second, count):
        parts = jnp.concatenate(
            [held[:, first : first + count], held[:, second : second + count]], axis=0
        )
        return jnp.dot(both, parts, preferred_element_type=F32).astype(BF)

    share_ref[...] = rows(0, share, share)
    for first in range(0, cols, TILE):
        start = 2 * share + first
        ring_ref[:, first : first + TILE] = rows(start, start + cols, TILE)


def dispatch_gradient(ids, weights, grad_out, experts, share):
    tok, width = grad_out.shape
    buf = experts * CAP
    small = lambda *shape: jax.ShapeDtypeStruct(shape, BF)
    return call(
        dispatch_gradient_kernel,
        "dispatch_gradient",
        4 * tok * buf * width,
        2 * width * (tok + buf),
        in_specs=[VMEM, VMEM, ANY],
        out_specs=[VMEM] * 4,
        out_shape=[
            small(buf, tok),
            small(2, 2 * buf, tok),
            small(2 * buf, share),
            small(2 * buf, width // 2 - share),
        ],
        scratch_shapes=[pltpu.VMEM((tok, width), BF), pltpu.SemaphoreType.DMA((1,))],
    )(ids, weights, grad_out)


def dispatch_token_kernel(pick_ref, share_ref, t_ref, out_ref, held, staged, sem):
    load = pltpu.make_async_copy(t_ref, held, sem.at[0])
    load.start()
    _, experts, unit, cols = out_ref.shape
    share = share_ref.shape[1]
    half = cols - share
    both = jnp.concatenate([pick_ref[0], pick_ref[1]], axis=1)
    staged[:, :, half:] = share_ref[...].reshape(experts, unit, share)
    load.wait()
    for first in range(0, half, TILE):
        parts = jnp.concatenate(
            [held[:, first : first + TILE], held[:, half + first : half + first + TILE]], axis=0
        )
        rows = jnp.dot(both, parts, preferred_element_type=F32).astype(BF)
        staged[:, :, first : first + TILE] = rows.reshape(experts, unit, TILE)
    stores = [pltpu.make_async_copy(staged, out_ref.at[h], sem.at[1 + h]) for h in range(2)]
    for store in stores:
        store.start()
    for store in stores:
        store.wait()


def dispatch_token(pick, share, tokens, experts):
    tok, width = tokens.shape
    unit = 2 * CAP
    cols = width // 2 + share.shape[1]
    return call(
        dispatch_token_kernel,
        "dispatch_token",
        4 * tok * experts * CAP * width,
        2 * width * (tok + 2 * experts * CAP),
        in_specs=[VMEM, VMEM, ANY],
        out_specs=ANY,
        out_shape=jax.ShapeDtypeStruct((2, experts, unit, cols), BF),
        scratch_shapes=[
            pltpu.VMEM((tok, width), BF),
            pltpu.VMEM((experts, unit, cols), BF),
            pltpu.SemaphoreType.DMA((3,)),
        ],
    )(pick, share, tokens)


def regroup_kernel(own_ref, next_ref, top_ref, bottom_ref, prev_ref, out_ref, sem):
    unit = own_ref.shape[1]
    mid = top_ref.shape[0]
    copies = []
    for h in range(2):
        places = [
            (own_ref, out_ref.at[h, :, :unit, :]),
            (next_ref, out_ref.at[h, :, unit : 2 * unit, :]),
            (top_ref, out_ref.at[h, :mid, 2 * unit : 3 * unit, :]),
            (bottom_ref, out_ref.at[h, mid:, 2 * unit : 3 * unit, :]),
            (prev_ref, out_ref.at[h, :, 3 * unit :, :]),
        ]
        for source, target in places:
            copies.append(pltpu.make_async_copy(source, target, sem.at[len(copies)]))
    for copy in copies:
        copy.start()
    for copy in copies:
        copy.wait()


def regroup(blocks):
    count, cols = blocks[0].shape
    unit = 2 * CAP
    experts = count // unit
    return call(
        regroup_kernel,
        "regroup",
        0,
        24 * count * cols,
        in_specs=[ANY] * 5,
        out_specs=ANY,
        out_shape=jax.ShapeDtypeStruct((2, experts, 4 * unit, cols), BF),
        scratch_shapes=[pltpu.SemaphoreType.DMA((10,))],
    )(*[b.reshape(b.shape[0] // unit, unit, cols) for b in blocks])


def pre_kernel(x_ref, wg_ref, wu_ref, wd_ref, slope_ref, swish_ref, part_ref, outer_ref, x, w, d, acc, sem):
    rows, cols = x.shape
    ff = w.shape[2] // 4
    count = rows // 2
    share = d.shape[1]
    half = cols - share
    steps = half // TILE
    weights = []
    for k, ref in enumerate((wg_ref, wu_ref)):
        for h in range(2):
            lane = (2 * k + h) * ff
            for t in range(steps):
                source = ref.at[h * half + t * TILE : h * half + (t + 1) * TILE, :]
                weights.append((t, source, w.at[t, :, lane : lane + ff]))
    copies = [[] for _ in range(steps + 1)]
    index = 0
    for t in range(steps):
        window = slice(t * TILE, (t + 1) * TILE)
        copies[t].append(pltpu.make_async_copy(x_ref.at[:, window], x.at[:, window], sem.at[index]))
        index += 1
        for step, source, target in weights:
            if step == t:
                copies[t].append(pltpu.make_async_copy(source, target, sem.at[index]))
                index += 1
    copies[steps].append(pltpu.make_async_copy(x_ref.at[:, half:], x.at[:, half:], sem.at[index]))
    for h in range(2):
        source = wd_ref.at[:, h * share : (h + 1) * share]
        target = d.at[h * ff : (h + 1) * ff, :]
        copies[steps].append(pltpu.make_async_copy(source, target, sem.at[index + 1 + h]))
    for group in copies:
        for copy in group:
            copy.start()
    for t in range(steps):
        for copy in copies[t]:
            copy.wait()
        value = jnp.dot(x[:, t * TILE : (t + 1) * TILE], w[t], preferred_element_type=F32)
        if t == 0:
            acc[...] = value
        else:
            acc[...] += value
    for copy in copies[steps]:
        copy.wait()

    def fold_halves(value):
        value = value.reshape(rows // (2 * CAP), 2 * CAP, 2 * ff)
        return (value[:, :CAP, :ff] + value[:, CAP:, ff:]).reshape(part_ref.shape)

    part_ref[...] = fold_halves(contract_cols(x[:, half:], d[...]))
    gate = fold_halves(acc[:, : 2 * ff])
    up = fold_halves(acc[:, 2 * ff :])
    sig = 1.0 / (1.0 + jnp.exp(-gate))
    swish = gate * sig
    slope_ref[...] = up * sig * (1.0 + gate * (1.0 - sig))
    swish_ref[...] = swish
    outer_ref[...] = swish * up


def pre(block, w_gate, w_up, w_down, groups, share):
    rows, cols = block.shape
    ff = w_gate.shape[1]
    steps = (cols - share) // TILE
    span = rows // 2 // groups
    return call(
        pre_kernel,
        "pre",
        8 * rows * cols * ff,
        2 * cols * (rows + 4 * ff),
        in_specs=[ANY] * 4,
        out_specs=[VMEM] * 4,
        out_shape=[jax.ShapeDtypeStruct((groups, span, ff), F32)] * 4,
        scratch_shapes=[
            pltpu.VMEM((rows, cols), BF),
            pltpu.VMEM((steps, TILE, 4 * ff), BF),
            pltpu.VMEM((2 * ff, share), BF),
            pltpu.VMEM((rows, 4 * ff), F32),
            pltpu.SemaphoreType.DMA((5 * steps + 3,)),
        ],
    )(block, w_gate, w_up, w_down)


def back_kernel(
    here_ref, g_ref, wd_ref, wg_ref, wu_ref, slope_ref, swish_ref, part_ref,
    gx_ref, ux_ref, ring_ref, wide_ref, g, d, w, near, far, staged, sem,
):
    groups, span, ff = gx_ref.shape
    locs = span // CAP
    unit = 2 * CAP
    rows, cols = g.shape
    first_col = wd_ref.shape[1] - 2 * cols
    chunk = 2 * TILE
    tile = cols // 4
    loads = []
    for t in range(4):
        window = slice(t * tile, (t + 1) * tile)
        group = [pltpu.make_async_copy(g_ref.at[:, window], g.at[:, window], sem.at[3 * t])]
        for h in range(2):
            start = first_col + h * cols + t * tile
            source = wd_ref.at[:, start : start + tile]
            target = d.at[h * ff : (h + 1) * ff, window]
            group.append(pltpu.make_async_copy(source, target, sem.at[3 * t + 1 + h]))
        loads.append(group)
    loads.append(
        [
            pltpu.make_async_copy(ref, w.at[:, k * ff : (k + 1) * ff], sem.at[12 + k])
            for k, ref in enumerate((wg_ref, wu_ref))
        ]
    )
    for group in loads:
        for load in group:
            load.start()
    total = None
    for t in range(4):
        for load in loads[t]:
            load.wait()
        window = slice(t * tile, (t + 1) * tile)
        value = contract_cols(g[:, window], d[:, window])
        total = value if total is None else total + value
    halves = total.reshape(locs, groups * unit, 2 * ff)
    for step in range(groups):
        group = lax.rem(here_ref[0] + step, groups)
        first = step * unit
        hidden = (
            halves[:, first : first + CAP, :ff] + halves[:, first + CAP : first + unit, ff:]
        ).reshape(span, ff) + part_ref[group]
        gate = hidden * slope_ref[group]
        up = hidden * swish_ref[group]
        gx_ref[group] = gate.astype(BF)
        ux_ref[group] = up.astype(BF)
        both = jnp.concatenate([gate, up], axis=1)
        far[group] = both.astype(BF)
        near[:, step * CAP : (step + 1) * CAP, :] = both.reshape(locs, CAP, 2 * ff).astype(BF)
    for load in loads[4]:
        load.wait()
    ring_cols = ring_ref.shape[1]
    stores = []
    for c in range(w.shape[0] // chunk):
        first = c * chunk
        window = slice(first, first + chunk)
        left = near[...] if first < ring_cols else far[...]
        value = contract_cols(left.reshape(groups * span, 2 * ff), w[window, :])
        staged[:, window] = value.astype(BF)
        if first < ring_cols:
            target = ring_ref.at[:, window]
        else:
            target = wide_ref.at[:, first - ring_cols : first - ring_cols + chunk]
        stores.append(pltpu.make_async_copy(staged.at[:, window], target, sem.at[14 + c]))
        stores[-1].start()
    for store in stores:
        store.wait()


def back(here, g_rows, w_down, w_gate, w_up, slope, swish, part, ring_cols):
    rows, cols = g_rows.shape
    groups, span, ff = slope.shape
    width = w_gate.shape[0]
    small = lambda *shape: jax.ShapeDtypeStruct(shape, BF)
    return call(
        back_kernel,
        "back",
        4 * rows * cols * ff + 4 * groups * span * ff * width,
        2 * (rows * cols + 3 * width * ff + groups * span * width),
        in_specs=[pl.BlockSpec(memory_space=pltpu.SMEM), ANY, ANY, ANY, ANY, VMEM, VMEM, VMEM],
        out_specs=[VMEM, VMEM, ANY, ANY],
        out_shape=[
            small(groups, span, ff),
            small(groups, span, ff),
            small(groups * span, ring_cols),
            small(groups * span, width - ring_cols),
        ],
        scratch_shapes=[
            pltpu.VMEM((rows, cols), BF),
            pltpu.VMEM((2 * ff, cols), BF),
            pltpu.VMEM((width, 2 * ff), BF),
            pltpu.VMEM((span // CAP, groups * CAP, 2 * ff), BF),
            pltpu.VMEM((groups, span, 2 * ff), BF),
            pltpu.VMEM((groups * span, width), BF),
            pltpu.SemaphoreType.DMA((14 + width // (2 * TILE),)),
        ],
    )(here, g_rows, w_down, w_gate, w_up, slope, swish, part)


def row_grads_kernel(gx_ref, ux_ref, x_ref, gate_ref, up_ref, wide):
    groups, span, ff = gx_ref.shape
    locs = span // CAP

    @pl.when(pl.program_id(0) == 0)
    def _():
        zero = jnp.zeros((locs, CAP, ff), F32)
        for group in range(groups):
            gate = gx_ref[group].astype(F32).reshape(locs, CAP, ff)
            up = ux_ref[group].astype(F32).reshape(locs, CAP, ff)
            low = jnp.concatenate([gate, zero, up, zero], axis=2)
            high = jnp.concatenate([zero, gate, zero, up], axis=2)
            both = jnp.concatenate([low, high], axis=1).reshape(2 * span, 4 * ff)
            wide[2 * span * group : 2 * span * (group + 1), :] = both.astype(BF)

    total = contract_rows(x_ref[...], wide[...]).astype(BF)
    gate_ref[0] = total[:, :ff]
    gate_ref[1] = total[:, ff : 2 * ff]
    up_ref[0] = total[:, 2 * ff : 3 * ff]
    up_ref[1] = total[:, 3 * ff :]


def row_grads(gate_x, up_x, x_rows, share):
    groups, span, ff = gate_x.shape
    rows, cols = x_rows.shape
    half = cols - share
    out = jax.ShapeDtypeStruct((2, half, ff), BF)
    gate, up = call(
        row_grads_kernel,
        "row_grads",
        8 * rows * half * ff,
        2 * half * (rows + 4 * ff),
        grid=(half // TILE,),
        in_specs=[
            whole(gate_x.shape),
            whole(up_x.shape),
            pl.BlockSpec((rows, TILE), lambda j: (0, j)),
        ],
        out_specs=[pl.BlockSpec((2, TILE, ff), lambda j: (0, j, 0))] * 2,
        out_shape=[out, out],
        scratch_shapes=[pltpu.VMEM((rows, 4 * ff), BF)],
    )(gate_x, up_x, x_rows)
    return gate.reshape(2 * half, ff), up.reshape(2 * half, ff)


def down_kernel(here_ref, outer_ref, x_ref, g_ref, out_ref, wide):
    groups, span, ff = outer_ref.shape
    locs = span // CAP
    unit = 2 * CAP
    step = pl.program_id(0)
    tile = g_ref.shape[1]
    share = x_ref.shape[1]

    def spread(outer):
        rows = outer.reshape(locs, CAP, ff)
        zero = jnp.zeros_like(rows)
        low = jnp.concatenate([rows, zero], axis=2)
        high = jnp.concatenate([zero, rows], axis=2)
        return jnp.concatenate([low, high], axis=1)

    @pl.when(step == 0)
    def _():
        rows = []
        for k in range(groups):
            other = outer_ref[lax.rem(here_ref[0] + k, groups)]
            wide[:, k * unit : (k + 1) * unit, :] = spread(other).astype(BF)
            rows.append(spread(outer_ref[k]).reshape(2 * span, 2 * ff).astype(BF))
        total = contract_rows(jnp.concatenate(rows, axis=0), x_ref[...]).astype(BF)
        out_ref[:, :share] = total[:ff]
        out_ref[:, share : 2 * share] = total[ff:]

    rows = wide[...].reshape(g_ref.shape[0], 2 * ff)
    total = contract_rows(rows, g_ref[...]).astype(BF)
    low = 2 * share + step * tile
    high = low + pl.num_programs(0) * tile
    out_ref[:, pl.ds(pl.multiple_of(low, 128), tile)] = total[:ff]
    out_ref[:, pl.ds(pl.multiple_of(high, 128), tile)] = total[ff:]


def down(here, outer, x_rows, g_rows, share):
    rows, cols = g_rows.shape
    groups, span, ff = outer.shape
    width = 2 * (cols + share)
    last = x_rows.shape[1] // share - 1
    return call(
        down_kernel,
        "down",
        4 * rows * (cols + share) * ff,
        2 * (cols + share) * (rows + 2 * ff),
        grid_spec=pltpu.PrefetchScalarGridSpec(
            num_scalar_prefetch=1,
            grid=(cols // TILE,),
            in_specs=[
                whole(outer.shape),
                pl.BlockSpec((rows, share), lambda j, _: (0, last)),
                pl.BlockSpec((rows, TILE), lambda j, _: (0, j)),
            ],
            out_specs=whole((ff, width)),
            scratch_shapes=[pltpu.VMEM((span // CAP, 2 * groups * CAP, 2 * ff), BF)],
        ),
        out_shape=jax.ShapeDtypeStruct((ff, width), BF),
    )(here, outer, x_rows, g_rows)


def fold_kernel(here_ref, in_ref, out_ref):
    _, experts, depth, tile = in_ref.shape
    groups = depth // CAP
    total = in_ref[0].astype(F32) + in_ref[1].astype(F32)
    for step in range(groups):
        part = total[:, step * CAP : (step + 1) * CAP, :]
        group = lax.rem(here_ref[0] + step, groups)
        out_ref[group] = part.reshape(experts * CAP, tile).astype(BF)


def fold(here, home):
    _, experts, depth, width = home.shape
    groups = depth // CAP
    return call(
        fold_kernel,
        "fold",
        experts * depth * width,
        6 * experts * depth * width,
        mib=20,
        grid_spec=pltpu.PrefetchScalarGridSpec(
            num_scalar_prefetch=1,
            grid=(width // (2 * TILE),),
            in_specs=[pl.BlockSpec((2, experts, depth, 2 * TILE), lambda j, _: (0, 0, 0, j))],
            out_specs=pl.BlockSpec((groups, experts * CAP, 2 * TILE), lambda j, _: (0, 0, j)),
        ),
        out_shape=jax.ShapeDtypeStruct((groups, experts * CAP, width), BF),
    )(here, home)


def combine_kernel(split, table_ref, ring_ref, wide_ref, out_ref):
    table = table_ref[...]

    @pl.when(pl.program_id(0) < split)
    def _():
        out_ref[...] = contract_rows(table, ring_ref[...]).astype(BF)

    @pl.when(pl.program_id(0) >= split)
    def _():
        count, _, tile = wide_ref.shape
        rows = wide_ref[...].astype(F32).reshape(count * CAP, tile).astype(BF)
        both = jnp.concatenate([table, table], axis=0)
        out_ref[...] = contract_rows(both, rows).astype(BF)


def combine(table, ring, wide):
    buf, tok = table.shape
    width = ring.shape[1] + wide.shape[2]
    tile = 2 * TILE
    split = ring.shape[1] // tile
    return call(
        functools.partial(combine_kernel, split),
        "combine",
        2 * tok * buf * width,
        2 * width * (tok + 2 * buf),
        mib=20,
        grid=(width // tile,),
        in_specs=[
            whole((buf, tok)),
            pl.BlockSpec((buf, tile), lambda j: (0, jnp.minimum(j, split - 1))),
            pl.BlockSpec((wide.shape[0], CAP, tile), lambda j: (0, 0, jnp.maximum(j - split, 0))),
        ],
        out_specs=pl.BlockSpec((tok, tile), lambda j: (0, j)),
        out_shape=jax.ShapeDtypeStruct((tok, width), BF),
    )(table, ring, wide)


def over_loc(a):
    return lax.all_to_all(a, "loc", split_axis=0, concat_axis=0, tiled=True)


def ring_gather(own):
    groups = lax.axis_size("grp")
    up = [(i, (i + 1) % groups) for i in range(groups)]
    down_ring = [(i, (i - 1) % groups) for i in range(groups)]
    mid = own.shape[0] // 2
    before = lax.ppermute(own, "grp", up)
    after = lax.ppermute(own, "grp", down_ring)
    top = lax.ppermute(before[:mid], "grp", up)
    bottom = lax.ppermute(after[mid:], "grp", down_ring)
    return [own, after, top, bottom, before]


def body(tokens, grad_out, expert_ids, route_weight, gate_weight, up_weight, down_weight):
    groups = lax.axis_size("grp")
    locs = lax.axis_size("loc")
    here = lax.axis_index("grp").astype(jnp.int32)[None]
    experts = locs // 2
    width = tokens.shape[1]
    buf = experts * CAP
    span = locs * CAP
    unit = 2 * CAP
    ring_cols = 3072
    wide_cols = width - ring_cols

    share = TILE

    w_gate, w_up, w_down = gate_weight[0], up_weight[0], down_weight[0]

    table, pick, g_share, g_send = dispatch_gradient(
        expert_ids.T, route_weight.T, grad_out, experts, share
    )
    g_blocks = ring_gather(g_send)
    xg_send = dispatch_token(pick, g_share, tokens, experts)
    xg = over_loc(xg_send.reshape(locs, unit, xg_send.shape[3]))
    xg, *g_blocks = lax.optimization_barrier((xg, *g_blocks))
    g_out = regroup(g_blocks)
    g_rows = over_loc(g_out.reshape(locs, groups * unit, g_out.shape[3]))
    g_rows = g_rows.reshape(locs * groups * unit, g_out.shape[3])
    x_rows = lax.all_gather(xg.reshape(locs * unit, xg.shape[2]), "grp", axis=0, tiled=True)

    slope, swish, part, outer = pre(x_rows, w_gate, w_up, w_down, groups, share)
    gate_x, up_x, part_ring, part_wide = back(
        here, g_rows, w_down, w_gate, w_up, slope, swish, part, ring_cols
    )

    home_ring = over_loc(part_ring.reshape(locs, groups * CAP, ring_cols))
    reduced = lax.psum_scatter(
        part_wide.reshape(groups, span, wide_cols), "grp", scatter_dimension=0, tiled=True
    )
    gate_grad, up_grad = row_grads(gate_x, up_x, x_rows, share)
    outer, gate_x = lax.optimization_barrier((outer, gate_x))
    down_grad = down(here, outer, x_rows, g_rows, share)
    home_ring, gate_grad, up_grad, down_grad = lax.optimization_barrier(
        (home_ring, gate_grad, up_grad, down_grad)
    )

    folded = fold(here, home_ring.reshape(2, experts, groups * CAP, ring_cols))
    ring = lax.psum_scatter(folded, "grp", scatter_dimension=0, tiled=True)
    home_wide = over_loc(reduced.reshape(locs, CAP, wide_cols))
    tokens_grad = combine(table, ring.reshape(buf, ring_cols), home_wide)
    return (tokens_grad, gate_grad[None], up_grad[None], down_grad[None])


def solution(mesh):
    in_specs = (
        P(("grp", "loc"), None),
        P(("grp", "loc"), None),
        P(("grp", "loc"), None),
        P(("grp", "loc"), None),
        P("loc", None, "grp"),
        P("loc", None, "grp"),
        P("loc", "grp", None),
    )
    out_specs = (
        P(("grp", "loc"), None),
        P("loc", None, "grp"),
        P("loc", None, "grp"),
        P("loc", "grp", None),
    )
    return jax.shard_map(body, mesh=mesh, in_specs=in_specs, out_specs=out_specs, check_vma=False)
```

```python
import functools

import jax
import jax.numpy as jnp
from jax import lax
from jax.experimental import pallas as pl
from jax.experimental.pallas import tpu as pltpu
from jax.sharding import PartitionSpec as P

CAP = 4
BF = jnp.bfloat16
F32 = jnp.float32
TILE = 512
ANY = pl.BlockSpec(memory_space=pl.ANY)
VMEM = pl.BlockSpec(memory_space=pltpu.VMEM)


def contract_rows(left, right):
    return lax.dot_general(left, right, (((0,), (0,)), ((), ())), preferred_element_type=F32)


def contract_cols(left, right):
    return lax.dot_general(left, right, (((1,), (1,)), ((), ())), preferred_element_type=F32)


def whole(shape):
    return pl.BlockSpec(shape, lambda *_: (0,) * len(shape))


def call(kernel, name, flops, nbytes, mib=56, **kwargs):
    return pl.pallas_call(
        kernel,
        name=name,
        compiler_params=pltpu.CompilerParams(vmem_limit_bytes=mib << 20),
        cost_estimate=pl.CostEstimate(flops=flops, bytes_accessed=nbytes, transcendentals=0),
        **kwargs,
    )


def dispatch_gradient_kernel(ids_ref, w_ref, g_ref, table_ref, pick_ref, share_ref, ring_ref, held, sem):
    load = pltpu.make_async_copy(g_ref, held, sem.at[0])
    load.start()
    topk, tok = ids_ref.shape
    buf = table_ref.shape[0]
    unit = 2 * CAP
    share = share_ref.shape[1]
    cols = ring_ref.shape[1]

    def tables(count, per_expert):
        slot_row = lax.broadcasted_iota(jnp.int32, (count, tok), 0)
        expert = lax.div(slot_row, per_expert)
        weights = w_ref[...].astype(F32)
        chosen = jnp.zeros((count, tok), F32)
        weight = jnp.zeros((count, tok), F32)
        for k in range(topk):
            hit = ids_ref[k : k + 1, :] == expert
            chosen = jnp.where(hit, 1.0, chosen)
            weight = jnp.where(hit, weights[k : k + 1, :], weight)
        before = lax.broadcasted_iota(jnp.int32, (tok, tok), 0)
        after = lax.broadcasted_iota(jnp.int32, (tok, tok), 1)
        earlier = jnp.where(before < after, 1.0, 0.0).astype(BF)
        slot = jnp.dot(chosen.astype(BF), earlier, preferred_element_type=F32)
        mine = (chosen > 0.5) & (slot == lax.rem(slot_row, CAP).astype(F32))
        return jnp.where(mine, 1.0, 0.0), jnp.where(mine, weight, 0.0), slot_row

    table_ref[...] = tables(buf, CAP)[0].astype(BF)
    table, weighted, slot_row = tables(2 * buf, unit)
    low = lax.rem(slot_row, unit) < CAP
    pick_ref[0] = jnp.where(low, table, 0.0).astype(BF)
    pick_ref[1] = jnp.where(low, 0.0, table).astype(BF)
    both = jnp.concatenate(
        [jnp.where(low, weighted, 0.0).astype(BF), jnp.where(low, 0.0, weighted).astype(BF)], axis=1
    )
    load.wait()

    def rows(first, second, count):
        parts = jnp.concatenate(
            [held[:, first : first + count], held[:, second : second + count]], axis=0
        )
        return jnp.dot(both, parts, preferred_element_type=F32).astype(BF)

    share_ref[...] = rows(0, share, share)
    for first in range(0, cols, TILE):
        start = 2 * share + first
        ring_ref[:, first : first + TILE] = rows(start, start + cols, TILE)


def dispatch_gradient(ids, weights, grad_out, experts, share):
    tok, width = grad_out.shape
    buf = experts * CAP
    small = lambda *shape: jax.ShapeDtypeStruct(shape, BF)
    return call(
        dispatch_gradient_kernel,
        "dispatch_gradient",
        4 * tok * buf * width,
        2 * width * (tok + buf),
        in_specs=[VMEM, VMEM, ANY],
        out_specs=[VMEM] * 4,
        out_shape=[
            small(buf, tok),
            small(2, 2 * buf, tok),
            small(2 * buf, share),
            small(2 * buf, width // 2 - share),
        ],
        scratch_shapes=[pltpu.VMEM((tok, width), BF), pltpu.SemaphoreType.DMA((1,))],
    )(ids, weights, grad_out)


def dispatch_token_kernel(pick_ref, share_ref, t_ref, out_ref, held, staged, sem):
    load = pltpu.make_async_copy(t_ref, held, sem.at[0])
    load.start()
    _, experts, unit, cols = out_ref.shape
    share = share_ref.shape[1]
    half = cols - share
    both = jnp.concatenate([pick_ref[0], pick_ref[1]], axis=1)
    staged[:, :, half:] = share_ref[...].reshape(experts, unit, share)
    load.wait()
    for first in range(0, half, TILE):
        parts = jnp.concatenate(
            [held[:, first : first + TILE], held[:, half + first : half + first + TILE]], axis=0
        )
        rows = jnp.dot(both, parts, preferred_element_type=F32).astype(BF)
        staged[:, :, first : first + TILE] = rows.reshape(experts, unit, TILE)
    stores = [pltpu.make_async_copy(staged, out_ref.at[h], sem.at[1 + h]) for h in range(2)]
    for store in stores:
        store.start()
    for store in stores:
        store.wait()


def dispatch_token(pick, share, tokens, experts):
    tok, width = tokens.shape
    unit = 2 * CAP
    cols = width // 2 + share.shape[1]
    return call(
        dispatch_token_kernel,
        "dispatch_token",
        4 * tok * experts * CAP * width,
        2 * width * (tok + 2 * experts * CAP),
        in_specs=[VMEM, VMEM, ANY],
        out_specs=ANY,
        out_shape=jax.ShapeDtypeStruct((2, experts, unit, cols), BF),
        scratch_shapes=[
            pltpu.VMEM((tok, width), BF),
            pltpu.VMEM((experts, unit, cols), BF),
            pltpu.SemaphoreType.DMA((3,)),
        ],
    )(pick, share, tokens)


def regroup_kernel(in_ref, out_ref, held, sem):
    groups, experts, unit, _ = in_ref.shape
    parts = 4
    size = experts // parts
    loads, stores = [], []
    for p in range(parts):
        window = slice(p * size, (p + 1) * size)
        for y in range(groups):
            source = in_ref.at[y, window, :, :]
            target = held.at[window, y * unit : (y + 1) * unit, :]
            loads.append(pltpu.make_async_copy(source, target, sem.at[p * groups + y]))
            loads[-1].start()
    for p in range(parts):
        window = slice(p * size, (p + 1) * size)
        for y in range(groups):
            loads[p * groups + y].wait()
        for h in range(2):
            index = parts * groups + 2 * p + h
            stores.append(pltpu.make_async_copy(held.at[window], out_ref.at[h, window], sem.at[index]))
            stores[-1].start()
    for store in stores:
        store.wait()


def regroup(rows):
    groups, experts, unit, cols = rows.shape
    return call(
        regroup_kernel,
        "regroup",
        0,
        6 * groups * experts * unit * cols,
        in_specs=[ANY],
        out_specs=ANY,
        out_shape=jax.ShapeDtypeStruct((2, experts, groups * unit, cols), BF),
        scratch_shapes=[
            pltpu.VMEM((experts, groups * unit, cols), BF),
            pltpu.SemaphoreType.DMA((4 * groups + 8,)),
        ],
    )(rows)


def pre_kernel(x_ref, wg_ref, wu_ref, wd_ref, slope_ref, swish_ref, part_ref, outer_ref, x, w, d, acc, sem):
    rows, cols = x.shape
    ff = w.shape[2] // 4
    count = rows // 2
    share = d.shape[1]
    half = cols - share
    steps = half // TILE
    weights = []
    for k, ref in enumerate((wg_ref, wu_ref)):
        for h in range(2):
            lane = (2 * k + h) * ff
            for t in range(steps):
                source = ref.at[h * half + t * TILE : h * half + (t + 1) * TILE, :]
                weights.append((t, source, w.at[t, :, lane : lane + ff]))
    copies = [[] for _ in range(steps + 1)]
    index = 0
    for t in range(steps):
        window = slice(t * TILE, (t + 1) * TILE)
        copies[t].append(pltpu.make_async_copy(x_ref.at[:, window], x.at[:, window], sem.at[index]))
        index += 1
        for step, source, target in weights:
            if step == t:
                copies[t].append(pltpu.make_async_copy(source, target, sem.at[index]))
                index += 1
    copies[steps].append(pltpu.make_async_copy(x_ref.at[:, half:], x.at[:, half:], sem.at[index]))
    for h in range(2):
        source = wd_ref.at[:, h * share : (h + 1) * share]
        target = d.at[h * ff : (h + 1) * ff, :]
        copies[steps].append(pltpu.make_async_copy(source, target, sem.at[index + 1 + h]))
    for group in copies:
        for copy in group:
            copy.start()
    for t in range(steps):
        for copy in copies[t]:
            copy.wait()
        value = jnp.dot(x[:, t * TILE : (t + 1) * TILE], w[t], preferred_element_type=F32)
        if t == 0:
            acc[...] = value
        else:
            acc[...] += value
    for copy in copies[steps]:
        copy.wait()

    def fold_halves(value):
        value = value.reshape(rows // (2 * CAP), 2 * CAP, 2 * ff)
        return (value[:, :CAP, :ff] + value[:, CAP:, ff:]).reshape(part_ref.shape)

    part_ref[...] = fold_halves(contract_cols(x[:, half:], d[...]))
    gate = fold_halves(acc[:, : 2 * ff])
    up = fold_halves(acc[:, 2 * ff :])
    sig = 1.0 / (1.0 + jnp.exp(-gate))
    swish = gate * sig
    slope_ref[...] = up * sig * (1.0 + gate * (1.0 - sig))
    swish_ref[...] = swish
    outer_ref[...] = swish * up


def pre(block, w_gate, w_up, w_down, groups, share):
    rows, cols = block.shape
    ff = w_gate.shape[1]
    steps = (cols - share) // TILE
    span = rows // 2 // groups
    return call(
        pre_kernel,
        "pre",
        8 * rows * cols * ff,
        2 * cols * (rows + 4 * ff),
        in_specs=[ANY] * 4,
        out_specs=[VMEM] * 4,
        out_shape=[jax.ShapeDtypeStruct((groups, span, ff), F32)] * 4,
        scratch_shapes=[
            pltpu.VMEM((rows, cols), BF),
            pltpu.VMEM((steps, TILE, 4 * ff), BF),
            pltpu.VMEM((2 * ff, share), BF),
            pltpu.VMEM((rows, 4 * ff), F32),
            pltpu.SemaphoreType.DMA((5 * steps + 3,)),
        ],
    )(block, w_gate, w_up, w_down)


def hidden_kernel(
    g_ref, wd_ref, wg_ref, wu_ref, slope_ref, swish_ref, part_ref,
    gx_ref, ux_ref, near_ref, wide_ref, g, d, w, far, staged, sem,
):
    groups, span, ff = gx_ref.shape
    locs = span // CAP
    unit = 2 * CAP
    cols = g.shape[1]
    wide_cols = wide_ref.shape[1]
    first_col = wd_ref.shape[1] - 2 * cols
    first_row = wg_ref.shape[0] - wide_cols
    chunk = 2 * TILE
    tile = cols // 4
    loads = []
    for t in range(4):
        window = slice(t * tile, (t + 1) * tile)
        group = [pltpu.make_async_copy(g_ref.at[:, window], g.at[:, window], sem.at[3 * t])]
        for h in range(2):
            start = first_col + h * cols + t * tile
            source = wd_ref.at[:, start : start + tile]
            target = d.at[h * ff : (h + 1) * ff, window]
            group.append(pltpu.make_async_copy(source, target, sem.at[3 * t + 1 + h]))
        loads.append(group)
    group = []
    for k, ref in enumerate((wg_ref, wu_ref)):
        source = ref.at[first_row : first_row + wide_cols, :]
        group.append(pltpu.make_async_copy(source, w.at[:, k * ff : (k + 1) * ff], sem.at[12 + k]))
    loads.append(group)
    for group in loads:
        for load in group:
            load.start()
    total = None
    for t in range(4):
        for load in loads[t]:
            load.wait()
        window = slice(t * tile, (t + 1) * tile)
        value = contract_cols(g[:, window], d[:, window])
        total = value if total is None else total + value
    halves = total.reshape(locs, groups * unit, 2 * ff)
    for group in range(groups):
        first = group * unit
        hidden = (
            halves[:, first : first + CAP, :ff] + halves[:, first + CAP : first + unit, ff:]
        ).reshape(span, ff) + part_ref[group]
        gate = hidden * slope_ref[group]
        up = hidden * swish_ref[group]
        gx_ref[group] = gate.astype(BF)
        ux_ref[group] = up.astype(BF)
        both = jnp.concatenate([gate, up], axis=1)
        far[group] = both.astype(BF)
        near_ref[:, group * CAP : (group + 1) * CAP, :] = both.reshape(locs, CAP, 2 * ff).astype(BF)
    for load in loads[4]:
        load.wait()
    left = far[...].reshape(groups * span, 2 * ff)
    stores = []
    for c in range(wide_cols // chunk):
        window = slice(c * chunk, (c + 1) * chunk)
        staged[:, window] = contract_cols(left, w[window, :]).astype(BF)
        target = wide_ref.at[:, window]
        stores.append(pltpu.make_async_copy(staged.at[:, window], target, sem.at[14 + c]))
        stores[-1].start()
    for store in stores:
        store.wait()


def hidden(g_rows, w_down, w_gate, w_up, slope, swish, part, wide_cols):
    rows, cols = g_rows.shape
    groups, span, ff = slope.shape
    small = lambda *shape: jax.ShapeDtypeStruct(shape, BF)
    return call(
        hidden_kernel,
        "hidden",
        4 * rows * cols * ff + 4 * groups * span * ff * wide_cols,
        2 * (rows * cols + 3 * wide_cols * ff + groups * span * wide_cols),
        in_specs=[ANY, ANY, ANY, ANY, VMEM, VMEM, VMEM],
        out_specs=[VMEM, VMEM, VMEM, ANY],
        out_shape=[
            small(groups, span, ff),
            small(groups, span, ff),
            small(span // CAP, groups * CAP, 2 * ff),
            small(groups * span, wide_cols),
        ],
        scratch_shapes=[
            pltpu.VMEM((rows, cols), BF),
            pltpu.VMEM((2 * ff, cols), BF),
            pltpu.VMEM((wide_cols, 2 * ff), BF),
            pltpu.VMEM((groups, span, 2 * ff), BF),
            pltpu.VMEM((groups * span, wide_cols), BF),
            pltpu.SemaphoreType.DMA((14 + wide_cols // (2 * TILE),)),
        ],
    )(g_rows, w_down, w_gate, w_up, slope, swish, part)


def ring_part_kernel(near_ref, wg_ref, wu_ref, out_ref, w, staged, sem):
    rows, ring_cols = out_ref.shape
    ff = wg_ref.shape[1]
    loads = []
    for k, ref in enumerate((wg_ref, wu_ref)):
        target = w.at[:, k * ff : (k + 1) * ff]
        loads.append(pltpu.make_async_copy(ref.at[:ring_cols, :], target, sem.at[k]))
        loads[-1].start()
    for load in loads:
        load.wait()
    left = near_ref[...].reshape(rows, 2 * ff)
    stores = []
    for c in range(ring_cols // TILE):
        window = slice(c * TILE, (c + 1) * TILE)
        staged[:, window] = contract_cols(left, w[window, :]).astype(BF)
        target = out_ref.at[:, window]
        stores.append(pltpu.make_async_copy(staged.at[:, window], target, sem.at[2 + c]))
        stores[-1].start()
    for store in stores:
        store.wait()


def ring_part(near, w_gate, w_up, ring_cols):
    locs, depth, double = near.shape
    rows = locs * depth
    return call(
        ring_part_kernel,
        "ring_part",
        2 * rows * double * ring_cols,
        2 * ring_cols * (rows + double),
        in_specs=[VMEM, ANY, ANY],
        out_specs=ANY,
        out_shape=jax.ShapeDtypeStruct((rows, ring_cols), BF),
        scratch_shapes=[
            pltpu.VMEM((ring_cols, double), BF),
            pltpu.VMEM((rows, ring_cols), BF),
            pltpu.SemaphoreType.DMA((2 + ring_cols // TILE,)),
        ],
    )(near, w_gate, w_up)


def row_grads_kernel(gx_ref, ux_ref, x_ref, gate_ref, up_ref, wide):
    groups, span, ff = gx_ref.shape
    locs = span // CAP

    @pl.when(pl.program_id(0) == 0)
    def _():
        zero = jnp.zeros((locs, CAP, ff), F32)
        for group in range(groups):
            gate = gx_ref[group].astype(F32).reshape(locs, CAP, ff)
            up = ux_ref[group].astype(F32).reshape(locs, CAP, ff)
            low = jnp.concatenate([gate, zero, up, zero], axis=2)
            high = jnp.concatenate([zero, gate, zero, up], axis=2)
            both = jnp.concatenate([low, high], axis=1).reshape(2 * span, 4 * ff)
            wide[2 * span * group : 2 * span * (group + 1), :] = both.astype(BF)

    total = contract_rows(x_ref[...], wide[...]).astype(BF)
    gate_ref[0] = total[:, :ff]
    gate_ref[1] = total[:, ff : 2 * ff]
    up_ref[0] = total[:, 2 * ff : 3 * ff]
    up_ref[1] = total[:, 3 * ff :]


def row_grads(gate_x, up_x, x_rows, share):
    groups, span, ff = gate_x.shape
    rows, cols = x_rows.shape
    half = cols - share
    out = jax.ShapeDtypeStruct((2, half, ff), BF)
    gate, up = call(
        row_grads_kernel,
        "row_grads",
        8 * rows * half * ff,
        2 * half * (rows + 4 * ff),
        grid=(half // TILE,),
        in_specs=[
            whole(gate_x.shape),
            whole(up_x.shape),
            pl.BlockSpec((rows, TILE), lambda j: (0, j)),
        ],
        out_specs=[pl.BlockSpec((2, TILE, ff), lambda j: (0, j, 0))] * 2,
        out_shape=[out, out],
        scratch_shapes=[pltpu.VMEM((rows, 4 * ff), BF)],
    )(gate_x, up_x, x_rows)
    return gate.reshape(2 * half, ff), up.reshape(2 * half, ff)


def down_kernel(outer_ref, x_ref, g_ref, out_ref, wide):
    groups, span, ff = outer_ref.shape
    locs = span // CAP
    unit = 2 * CAP
    step = pl.program_id(0)
    tile = g_ref.shape[1]
    share = x_ref.shape[1]

    def spread(outer):
        rows = outer.reshape(locs, CAP, ff)
        zero = jnp.zeros_like(rows)
        low = jnp.concatenate([rows, zero], axis=2)
        high = jnp.concatenate([zero, rows], axis=2)
        return jnp.concatenate([low, high], axis=1)

    @pl.when(step == 0)
    def _():
        rows = []
        for k in range(groups):
            block = spread(outer_ref[k]).astype(BF)
            wide[:, k * unit : (k + 1) * unit, :] = block
            rows.append(block.reshape(2 * span, 2 * ff))
        total = contract_rows(jnp.concatenate(rows, axis=0), x_ref[...]).astype(BF)
        out_ref[:, :share] = total[:ff]
        out_ref[:, share : 2 * share] = total[ff:]

    rows = wide[...].reshape(g_ref.shape[0], 2 * ff)
    total = contract_rows(rows, g_ref[...]).astype(BF)
    low = 2 * share + step * tile
    high = low + pl.num_programs(0) * tile
    out_ref[:, pl.ds(pl.multiple_of(low, 128), tile)] = total[:ff]
    out_ref[:, pl.ds(pl.multiple_of(high, 128), tile)] = total[ff:]


def down(outer, x_rows, g_rows, share):
    rows, cols = g_rows.shape
    groups, span, ff = outer.shape
    width = 2 * (cols + share)
    last = x_rows.shape[1] // share - 1
    return call(
        down_kernel,
        "down",
        4 * rows * (cols + share) * ff,
        2 * (cols + share) * (rows + 2 * ff),
        grid=(cols // TILE,),
        in_specs=[
            whole(outer.shape),
            pl.BlockSpec((rows, share), lambda j: (0, last)),
            pl.BlockSpec((rows, TILE), lambda j: (0, j)),
        ],
        out_specs=whole((ff, width)),
        out_shape=jax.ShapeDtypeStruct((ff, width), BF),
        scratch_shapes=[pltpu.VMEM((span // CAP, 2 * groups * CAP, 2 * ff), BF)],
    )(outer, x_rows, g_rows)


def fold_kernel(in_ref, out_ref):
    _, experts, depth, tile = in_ref.shape
    groups = depth // CAP
    total = in_ref[0].astype(F32) + in_ref[1].astype(F32)
    for step in range(groups):
        part = total[:, step * CAP : (step + 1) * CAP, :]
        out_ref[step] = part.reshape(experts * CAP, tile).astype(BF)


def fold(home):
    _, experts, depth, width = home.shape
    groups = depth // CAP
    tile = 2 * TILE
    return call(
        fold_kernel,
        "fold",
        experts * depth * width,
        6 * experts * depth * width,
        mib=20,
        grid=(width // tile,),
        in_specs=[pl.BlockSpec((2, experts, depth, tile), lambda j: (0, 0, 0, j))],
        out_specs=pl.BlockSpec((groups, experts * CAP, tile), lambda j: (0, 0, j)),
        out_shape=jax.ShapeDtypeStruct((groups, experts * CAP, width), BF),
    )(home)


def combine_kernel(split, table_ref, ring_ref, wide_ref, out_ref):
    table = table_ref[...]

    @pl.when(pl.program_id(0) < split)
    def _():
        out_ref[...] = contract_rows(table, ring_ref[...]).astype(BF)

    @pl.when(pl.program_id(0) >= split)
    def _():
        count, _, tile = wide_ref.shape
        rows = wide_ref[...].astype(F32).reshape(count * CAP, tile).astype(BF)
        both = jnp.concatenate([table, table], axis=0)
        out_ref[...] = contract_rows(both, rows).astype(BF)


def combine(table, ring, wide):
    buf, tok = table.shape
    width = ring.shape[1] + wide.shape[2]
    tile = 2 * TILE
    split = ring.shape[1] // tile
    return call(
        functools.partial(combine_kernel, split),
        "combine",
        2 * tok * buf * width,
        2 * width * (tok + 2 * buf),
        mib=20,
        grid=(width // tile,),
        in_specs=[
            whole((buf, tok)),
            pl.BlockSpec((buf, tile), lambda j: (0, jnp.minimum(j, split - 1))),
            pl.BlockSpec((wide.shape[0], CAP, tile), lambda j: (0, 0, jnp.maximum(j - split, 0))),
        ],
        out_specs=pl.BlockSpec((tok, tile), lambda j: (0, j)),
        out_shape=jax.ShapeDtypeStruct((tok, width), BF),
    )(table, ring, wide)


def over_loc(a):
    return lax.all_to_all(a, "loc", split_axis=0, concat_axis=0, tiled=True)


def body(tokens, grad_out, expert_ids, route_weight, gate_weight, up_weight, down_weight):
    groups = lax.axis_size("grp")
    locs = lax.axis_size("loc")
    experts = locs // 2
    width = tokens.shape[1]
    buf = experts * CAP
    span = locs * CAP
    unit = 2 * CAP
    ring_cols = 3072
    wide_cols = width - ring_cols

    share = TILE

    w_gate, w_up, w_down = gate_weight[0], up_weight[0], down_weight[0]

    table, pick, g_share, g_send = dispatch_gradient(
        expert_ids.T, route_weight.T, grad_out, experts, share
    )
    g_ring = lax.all_gather(g_send, "grp", axis=0, tiled=True)
    xg_send = dispatch_token(pick, g_share, tokens, experts)
    xg = over_loc(xg_send.reshape(locs, unit, xg_send.shape[3]))
    x_rows = lax.all_gather(xg.reshape(locs * unit, xg.shape[2]), "grp", axis=0, tiled=True)
    g_out = regroup(g_ring.reshape(groups, experts, unit, g_ring.shape[1]))
    g_rows = over_loc(g_out.reshape(locs, groups * unit, g_out.shape[3]))
    g_rows = g_rows.reshape(locs * groups * unit, g_out.shape[3])

    slope, swish, part, outer = pre(x_rows, w_gate, w_up, w_down, groups, share)
    gate_x, up_x, near, part_wide = hidden(g_rows, w_down, w_gate, w_up, slope, swish, part, wide_cols)
    part_wide, near = lax.optimization_barrier((part_wide, near))
    part_ring = ring_part(near, w_gate, w_up, ring_cols)

    home_ring = over_loc(part_ring.reshape(locs, groups * CAP, ring_cols))
    reduced = lax.psum_scatter(
        part_wide.reshape(groups, span, wide_cols), "grp", scatter_dimension=0, tiled=True
    )
    part_ring, gate_x, up_x, outer = lax.optimization_barrier((part_ring, gate_x, up_x, outer))
    gate_grad, up_grad = row_grads(gate_x, up_x, x_rows, share)
    down_grad = down(outer, x_rows, g_rows, share)
    home_ring, gate_grad, up_grad, down_grad = lax.optimization_barrier(
        (home_ring, gate_grad, up_grad, down_grad)
    )

    folded = fold(home_ring.reshape(2, experts, groups * CAP, ring_cols))
    ring = lax.psum_scatter(folded, "grp", scatter_dimension=0, tiled=True)
    home_wide = over_loc(reduced.reshape(locs, CAP, wide_cols))
    tokens_grad = combine(table, ring.reshape(buf, ring_cols), home_wide)
    return (tokens_grad, gate_grad[None], up_grad[None], down_grad[None])


def solution(mesh):
    in_specs = (
        P(("grp", "loc"), None),
        P(("grp", "loc"), None),
        P(("grp", "loc"), None),
        P(("grp", "loc"), None),
        P("loc", None, "grp"),
        P("loc", None, "grp"),
        P("loc", "grp", None),
    )
    out_specs = (
        P(("grp", "loc"), None),
        P("loc", None, "grp"),
        P("loc", None, "grp"),
        P("loc", "grp", None),
    )
    return jax.shard_map(body, mesh=mesh, in_specs=in_specs, out_specs=out_specs, check_vma=False)
```

```python
import functools

import jax
import jax.numpy as jnp
from jax import lax
from jax.experimental import pallas as pl
from jax.experimental.pallas import tpu as pltpu
from jax.sharding import PartitionSpec as P

CAP = 4
BF = jnp.bfloat16
F32 = jnp.float32
TILE = 512
ANY = pl.BlockSpec(memory_space=pl.ANY)
VMEM = pl.BlockSpec(memory_space=pltpu.VMEM)


def contract_rows(left, right):
    return lax.dot_general(left, right, (((0,), (0,)), ((), ())), preferred_element_type=F32)


def contract_cols(left, right):
    return lax.dot_general(left, right, (((1,), (1,)), ((), ())), preferred_element_type=F32)


def whole(shape):
    return pl.BlockSpec(shape, lambda *_: (0,) * len(shape))


def call(kernel, name, flops, nbytes, mib=56, **kwargs):
    return pl.pallas_call(
        kernel,
        name=name,
        compiler_params=pltpu.CompilerParams(vmem_limit_bytes=mib << 20),
        cost_estimate=pl.CostEstimate(flops=flops, bytes_accessed=nbytes, transcendentals=0),
        **kwargs,
    )


def dispatch_gradient_kernel(ids_ref, w_ref, g_ref, table_ref, pick_ref, share_ref, ring_ref, held, sem):
    load = pltpu.make_async_copy(g_ref, held, sem.at[0])
    load.start()
    topk, tok = ids_ref.shape
    buf = table_ref.shape[0]
    unit = 2 * CAP
    share = share_ref.shape[1]
    cols = ring_ref.shape[1]

    def tables(count, per_expert):
        slot_row = lax.broadcasted_iota(jnp.int32, (count, tok), 0)
        expert = lax.div(slot_row, per_expert)
        weights = w_ref[...].astype(F32)
        chosen = jnp.zeros((count, tok), F32)
        weight = jnp.zeros((count, tok), F32)
        for k in range(topk):
            hit = ids_ref[k : k + 1, :] == expert
            chosen = jnp.where(hit, 1.0, chosen)
            weight = jnp.where(hit, weights[k : k + 1, :], weight)
        before = lax.broadcasted_iota(jnp.int32, (tok, tok), 0)
        after = lax.broadcasted_iota(jnp.int32, (tok, tok), 1)
        earlier = jnp.where(before < after, 1.0, 0.0).astype(BF)
        slot = jnp.dot(chosen.astype(BF), earlier, preferred_element_type=F32)
        mine = (chosen > 0.5) & (slot == lax.rem(slot_row, CAP).astype(F32))
        return jnp.where(mine, 1.0, 0.0), jnp.where(mine, weight, 0.0), slot_row

    table_ref[...] = tables(buf, CAP)[0].astype(BF)
    table, weighted, slot_row = tables(2 * buf, unit)
    low = lax.rem(slot_row, unit) < CAP
    pick_ref[0] = jnp.where(low, table, 0.0).astype(BF)
    pick_ref[1] = jnp.where(low, 0.0, table).astype(BF)
    both = jnp.concatenate(
        [jnp.where(low, weighted, 0.0).astype(BF), jnp.where(low, 0.0, weighted).astype(BF)], axis=1
    )
    load.wait()

    def rows(first, second, count):
        parts = jnp.concatenate(
            [held[:, first : first + count], held[:, second : second + count]], axis=0
        )
        return jnp.dot(both, parts, preferred_element_type=F32).astype(BF)

    share_ref[...] = rows(0, share, share)
    part = TILE // 2
    for first in range(0, cols, part):
        start = 2 * share + first
        ring_ref[:, first : first + part] = rows(start, start + cols, part)


def dispatch_gradient(ids, weights, grad_out, experts, share):
    tok, width = grad_out.shape
    buf = experts * CAP
    small = lambda *shape: jax.ShapeDtypeStruct(shape, BF)
    return call(
        dispatch_gradient_kernel,
        "dispatch_gradient",
        4 * tok * buf * width,
        2 * width * (tok + buf),
        in_specs=[VMEM, VMEM, ANY],
        out_specs=[VMEM] * 4,
        out_shape=[
            small(buf, tok),
            small(2, 2 * buf, tok),
            small(2 * buf, share),
            small(2 * buf, width // 2 - share),
        ],
        scratch_shapes=[pltpu.VMEM((tok, width), BF), pltpu.SemaphoreType.DMA((1,))],
    )(ids, weights, grad_out)


def dispatch_token_kernel(pick_ref, share_ref, t_ref, out_ref, held, staged, sem):
    load = pltpu.make_async_copy(t_ref, held, sem.at[0])
    load.start()
    _, experts, unit, cols = out_ref.shape
    share = share_ref.shape[1]
    half = cols - share
    both = jnp.concatenate([pick_ref[0], pick_ref[1]], axis=1)
    staged[:, :, half:] = share_ref[...].reshape(experts, unit, share)
    load.wait()
    for first in range(0, half, TILE):
        parts = jnp.concatenate(
            [held[:, first : first + TILE], held[:, half + first : half + first + TILE]], axis=0
        )
        rows = jnp.dot(both, parts, preferred_element_type=F32).astype(BF)
        staged[:, :, first : first + TILE] = rows.reshape(experts, unit, TILE)
    stores = [pltpu.make_async_copy(staged, out_ref.at[h], sem.at[1 + h]) for h in range(2)]
    for store in stores:
        store.start()
    for store in stores:
        store.wait()


def dispatch_token(pick, share, tokens, experts):
    tok, width = tokens.shape
    unit = 2 * CAP
    cols = width // 2 + share.shape[1]
    return call(
        dispatch_token_kernel,
        "dispatch_token",
        4 * tok * experts * CAP * width,
        2 * width * (tok + 2 * experts * CAP),
        in_specs=[VMEM, VMEM, ANY],
        out_specs=ANY,
        out_shape=jax.ShapeDtypeStruct((2, experts, unit, cols), BF),
        scratch_shapes=[
            pltpu.VMEM((tok, width), BF),
            pltpu.VMEM((experts, unit, cols), BF),
            pltpu.SemaphoreType.DMA((3,)),
        ],
    )(pick, share, tokens)


def regroup_kernel(own_ref, next_ref, top_ref, bottom_ref, prev_ref, out_ref, held, sem):
    experts, unit, _ = own_ref.shape
    parts = 4
    size = experts // parts
    loads, stores = [], []
    for p in range(parts):
        window = slice(p * size, (p + 1) * size)
        if p < parts // 2:
            far = top_ref.at[window]
        else:
            far = bottom_ref.at[p * size - experts // 2 : (p + 1) * size - experts // 2]
        sources = [own_ref.at[window], next_ref.at[window], far, prev_ref.at[window]]
        for k, source in enumerate(sources):
            target = held.at[window, k * unit : (k + 1) * unit, :]
            loads.append(pltpu.make_async_copy(source, target, sem.at[p * 4 + k]))
            loads[-1].start()
    for p in range(parts):
        window = slice(p * size, (p + 1) * size)
        for k in range(4):
            loads[p * 4 + k].wait()
        for h in range(2):
            index = parts * 4 + 2 * p + h
            stores.append(pltpu.make_async_copy(held.at[window], out_ref.at[h, window], sem.at[index]))
            stores[-1].start()
    for store in stores:
        store.wait()


def regroup(blocks):
    count, cols = blocks[0].shape
    unit = 2 * CAP
    experts = count // unit
    return call(
        regroup_kernel,
        "regroup",
        0,
        24 * count * cols,
        in_specs=[ANY] * 5,
        out_specs=ANY,
        out_shape=jax.ShapeDtypeStruct((2, experts, 4 * unit, cols), BF),
        scratch_shapes=[
            pltpu.VMEM((experts, 4 * unit, cols), BF),
            pltpu.SemaphoreType.DMA((24,)),
        ],
    )(*[b.reshape(b.shape[0] // unit, unit, cols) for b in blocks])


def pre_kernel(count, *refs):
    x_refs = refs[:count]
    wg_ref, wu_ref, wd_ref, slope_ref, swish_ref, part_ref, outer_ref, x, w, d, acc, sem = refs[count:]
    rows, cols = x.shape
    ff = w.shape[2] // 4
    share = d.shape[1]
    half = cols - share
    steps = half // TILE
    copies = [[] for _ in range(steps + 1)]
    index = 0

    def add(step, source, target):
        nonlocal index
        copies[step].append(pltpu.make_async_copy(source, target, sem.at[index]))
        index += 1

    for t in range(steps + 1):
        window = slice(t * TILE, (t + 1) * TILE) if t < steps else slice(half, cols)
        at = 0
        for ref in x_refs:
            add(t, ref.at[:, window], x.at[at : at + ref.shape[0], window])
            at += ref.shape[0]
        if t < steps:
            for k, ref in enumerate((wg_ref, wu_ref)):
                for h in range(2):
                    lane = (2 * k + h) * ff
                    source = ref.at[h * half + t * TILE : h * half + (t + 1) * TILE, :]
                    add(t, source, w.at[t, :, lane : lane + ff])
        else:
            for h in range(2):
                source = wd_ref.at[:, h * share : (h + 1) * share]
                add(t, source, d.at[h * ff : (h + 1) * ff, :])
    for group in copies:
        for copy in group:
            copy.start()
    for t in range(steps):
        for copy in copies[t]:
            copy.wait()
        value = jnp.dot(x[:, t * TILE : (t + 1) * TILE], w[t], preferred_element_type=F32)
        if t == 0:
            acc[...] = value
        else:
            acc[...] += value
    for copy in copies[steps]:
        copy.wait()

    def fold_halves(value):
        value = value.reshape(rows // (2 * CAP), 2 * CAP, 2 * ff)
        return (value[:, :CAP, :ff] + value[:, CAP:, ff:]).reshape(rows // 2, ff)

    part_ref[...] = fold_halves(contract_cols(x[:, half:], d[...]))
    gate = fold_halves(acc[:, : 2 * ff])
    up = fold_halves(acc[:, 2 * ff :])
    sig = 1.0 / (1.0 + jnp.exp(-gate))
    swish = gate * sig
    slope_ref[...] = up * sig * (1.0 + gate * (1.0 - sig))
    swish_ref[...] = swish
    outer_ref[...] = swish * up


def pre(blocks, w_gate, w_up, w_down, share):
    cols = blocks[0].shape[1]
    rows = sum(b.shape[0] for b in blocks)
    ff = w_gate.shape[1]
    steps = (cols - share) // TILE
    copies = (len(blocks) + 4) * steps + len(blocks) + 2
    return call(
        functools.partial(pre_kernel, len(blocks)),
        "pre",
        8 * rows * cols * ff,
        2 * cols * (rows + 4 * ff),
        in_specs=[ANY] * (len(blocks) + 3),
        out_specs=[VMEM] * 4,
        out_shape=[jax.ShapeDtypeStruct((rows // 2, ff), F32)] * 4,
        scratch_shapes=[
            pltpu.VMEM((rows, cols), BF),
            pltpu.VMEM((steps, TILE, 4 * ff), BF),
            pltpu.VMEM((2 * ff, share), BF),
            pltpu.VMEM((rows, 4 * ff), F32),
            pltpu.SemaphoreType.DMA((copies,)),
        ],
    )(*blocks, w_gate, w_up, w_down)


def load_weights(wg_ref, wu_ref, w, first, sem, index):
    count = w.shape[0]
    ff = wg_ref.shape[1]
    copies = []
    for k, ref in enumerate((wg_ref, wu_ref)):
        source = ref.at[first : first + count, :]
        target = w.at[:, k * ff : (k + 1) * ff]
        copies.append(pltpu.make_async_copy(source, target, sem.at[index + k]))
    return copies


def start_all(copies):
    for copy in copies:
        copy.start()


def wait_all(copies):
    for copy in copies:
        copy.wait()


def hidden_kernel(
    g_ref, wd_ref, wg_ref, wu_ref, *refs
):
    own, side, far = refs[0:3], refs[3:6], refs[6:9]
    gu_ref, near_ref, top_ref, bottom_ref, g, d, w, small, staged, sem = refs[9:]
    groups, span, double = gu_ref.shape
    ff = double // 2
    locs = span // CAP
    unit = 2 * CAP
    cols = g.shape[1]
    wide_cols = top_ref.shape[1]
    first_col = wd_ref.shape[1] - 2 * cols
    steps = 2
    tile = cols // steps
    loads = []
    for t in range(steps):
        window = slice(t * tile, (t + 1) * tile)
        loads.append(pltpu.make_async_copy(g_ref.at[:, window], g.at[:, window], sem.at[3 * t]))
        for h in range(2):
            start = first_col + h * cols + t * tile
            source = wd_ref.at[:, start : start + tile]
            target = d.at[h * ff : (h + 1) * ff, window]
            loads.append(pltpu.make_async_copy(source, target, sem.at[3 * t + 1 + h]))
    more = []
    index = 3 * steps
    for k in range(3):
        places = [(own[k], 0), (side[k].at[:span], 1), (far[k], 2), (side[k].at[span:], 3)]
        for source, group in places:
            more.append(pltpu.make_async_copy(source, small.at[k, group], sem.at[index]))
            index += 1
    weights = load_weights(wg_ref, wu_ref, w, wg_ref.shape[0] - wide_cols, sem, index)
    start_all(loads)
    start_all(more)
    start_all(weights)
    total = None
    for t in range(steps):
        wait_all(loads[3 * t : 3 * t + 3])
        window = slice(t * tile, (t + 1) * tile)
        value = contract_cols(g[:, window], d[:, window])
        total = value if total is None else total + value
    wait_all(more)
    halves = total.reshape(locs, groups * unit, double)
    for group in range(groups):
        first = group * unit
        hidden = (
            halves[:, first : first + CAP, :ff] + halves[:, first + CAP : first + unit, ff:]
        ).reshape(span, ff) + small[2, group]
        gate = hidden * small[0, group]
        up = hidden * small[1, group]
        both = jnp.concatenate([gate, up], axis=1)
        gu_ref[group] = both.astype(BF)
        near_ref[:, group * CAP : (group + 1) * CAP, :] = both.reshape(locs, CAP, double).astype(BF)
    wait_all(weights)
    staged[...] = contract_cols(gu_ref[2], w[...]).astype(BF)
    stores = [
        pltpu.make_async_copy(staged.at[: span // 2], top_ref, sem.at[index + 2]),
        pltpu.make_async_copy(staged.at[span // 2 :], bottom_ref, sem.at[index + 3]),
    ]
    start_all(stores)
    wait_all(stores)


def hidden(g_rows, w_down, w_gate, w_up, own, side, far, wide_cols):
    rows, cols = g_rows.shape
    span, ff = own[0].shape
    groups = rows // 2 // span
    small = lambda *shape: jax.ShapeDtypeStruct(shape, BF)
    return call(
        hidden_kernel,
        "hidden",
        4 * rows * cols * ff + 4 * span * ff * wide_cols,
        2 * (rows * cols + 2 * wide_cols * ff + span * wide_cols),
        in_specs=[ANY] * 13,
        out_specs=[VMEM, VMEM, ANY, ANY],
        out_shape=[
            small(groups, span, 2 * ff),
            small(span // CAP, groups * CAP, 2 * ff),
            small(span // 2, wide_cols),
            small(span // 2, wide_cols),
        ],
        scratch_shapes=[
            pltpu.VMEM((rows, cols), BF),
            pltpu.VMEM((2 * ff, cols), BF),
            pltpu.VMEM((wide_cols, 2 * ff), BF),
            pltpu.VMEM((3, groups, span, ff), F32),
            pltpu.VMEM((span, wide_cols), BF),
            pltpu.SemaphoreType.DMA((6 + 12 + 4,)),
        ],
    )(g_rows, w_down, w_gate, w_up, *own, *side, *far)


def ring_part_kernel(near_ref, wg_ref, wu_ref, out_ref, w, staged, sem):
    rows, ring_cols = out_ref.shape
    loads = load_weights(wg_ref, wu_ref, w, 0, sem, 0)
    start_all(loads)
    wait_all(loads)
    left = near_ref[...].reshape(rows, w.shape[1])
    stores = []
    for c in range(ring_cols // TILE):
        window = slice(c * TILE, (c + 1) * TILE)
        staged[:, window] = contract_cols(left, w[window, :]).astype(BF)
        target = out_ref.at[:, window]
        stores.append(pltpu.make_async_copy(staged.at[:, window], target, sem.at[2 + c]))
        stores[-1].start()
    wait_all(stores)


def ring_part(near, w_gate, w_up, ring_cols):
    locs, depth, double = near.shape
    rows = locs * depth
    return call(
        ring_part_kernel,
        "ring_part",
        2 * rows * double * ring_cols,
        2 * ring_cols * (rows + double),
        in_specs=[VMEM, ANY, ANY],
        out_specs=ANY,
        out_shape=jax.ShapeDtypeStruct((rows, ring_cols), BF),
        scratch_shapes=[
            pltpu.VMEM((ring_cols, double), BF),
            pltpu.VMEM((rows, ring_cols), BF),
            pltpu.SemaphoreType.DMA((2 + ring_cols // TILE,)),
        ],
    )(near, w_gate, w_up)


def side_kernel(gu_ref, wg_ref, wu_ref, top_ref, bottom_ref, next_ref, prev_ref, own_ref, w, held, staged, sem):
    _, span, double = gu_ref.shape
    wide_cols = next_ref.shape[1]
    weights = load_weights(wg_ref, wu_ref, w, wg_ref.shape[0] - wide_cols, sem, 0)
    came = [
        pltpu.make_async_copy(top_ref, held.at[0], sem.at[2]),
        pltpu.make_async_copy(bottom_ref, held.at[1], sem.at[3]),
    ]
    start_all(weights)
    start_all(came)
    wait_all(weights)
    wait_all(came)
    left = jnp.concatenate([gu_ref[1], gu_ref[3], gu_ref[0]], axis=0)
    mid = span // 2
    stores = []
    for c in range(wide_cols // TILE):
        window = slice(c * TILE, (c + 1) * TILE)
        value = contract_cols(left, w[window, :])
        top = held[0, :, window].astype(F32)
        bottom = held[1, :, window].astype(F32)
        staged[0, :mid, window] = (value[:mid] + top).astype(BF)
        staged[0, mid:, window] = value[mid:span].astype(BF)
        staged[1, :mid, window] = value[span : span + mid].astype(BF)
        staged[1, mid:, window] = (value[span + mid : 2 * span] + bottom).astype(BF)
        staged[2, :, window] = value[2 * span :].astype(BF)
        for k, ref in enumerate((next_ref, prev_ref, own_ref)):
            copy = pltpu.make_async_copy(
                staged.at[k, :, window], ref.at[:, window], sem.at[4 + 3 * c + k]
            )
            copy.start()
            stores.append(copy)
    wait_all(stores)


def side_part(gu, w_gate, w_up, top, bottom):
    _, span, double = gu.shape
    wide_cols = top.shape[1]
    return call(
        side_kernel,
        "side_part",
        6 * span * double * wide_cols,
        2 * wide_cols * (4 * span + double),
        in_specs=[VMEM, ANY, ANY, ANY, ANY],
        out_specs=[ANY] * 3,
        out_shape=[jax.ShapeDtypeStruct((span, wide_cols), BF)] * 3,
        scratch_shapes=[
            pltpu.VMEM((wide_cols, double), BF),
            pltpu.VMEM((2, span // 2, wide_cols), BF),
            pltpu.VMEM((3, span, wide_cols), BF),
            pltpu.SemaphoreType.DMA((4 + 3 * (wide_cols // TILE),)),
        ],
    )(gu, w_gate, w_up, top, bottom)


def sum_kernel(a_ref, b_ref, c_ref, out_ref, held, staged, sem):
    locs, _, cols = out_ref.shape
    steps = cols // TILE
    loads, stores = [], []
    for t in range(steps):
        window = slice(t * TILE, (t + 1) * TILE)
        for k, ref in enumerate((a_ref, b_ref, c_ref)):
            loads.append(
                pltpu.make_async_copy(ref.at[:, window], held.at[k, :, window], sem.at[4 * t + k])
            )
    start_all(loads)
    for t in range(steps):
        wait_all(loads[3 * t : 3 * t + 3])
        window = slice(t * TILE, (t + 1) * TILE)
        total = sum(held[k, :, window].astype(F32) for k in range(3))
        staged[:, :, window] = total.reshape(locs, CAP, TILE).astype(BF)
        source = staged.at[:, :, window]
        stores.append(pltpu.make_async_copy(source, out_ref.at[:, :, window], sem.at[4 * t + 3]))
        stores[-1].start()
    wait_all(stores)


def sum_blocks(a, b, c):
    rows, cols = a.shape
    return call(
        sum_kernel,
        "sum_blocks",
        2 * rows * cols,
        8 * rows * cols,
        in_specs=[ANY] * 3,
        out_specs=ANY,
        out_shape=jax.ShapeDtypeStruct((rows // CAP, CAP, cols), BF),
        scratch_shapes=[
            pltpu.VMEM((3, rows, cols), BF),
            pltpu.VMEM((rows // CAP, CAP, cols), BF),
            pltpu.SemaphoreType.DMA((4 * (cols // TILE),)),
        ],
    )(a, b, c)


def row_grads_kernel(gu_ref, own_ref, next_ref, top_ref, bottom_ref, prev_ref, gate_ref, up_ref, wide):
    groups, span, double = gu_ref.shape
    ff = double // 2
    locs = span // CAP

    @pl.when(pl.program_id(0) == 0)
    def _():
        zero = jnp.zeros((locs, CAP, ff), F32)
        for group in range(groups):
            both = gu_ref[group].astype(F32).reshape(locs, CAP, double)
            gate, up = both[:, :, :ff], both[:, :, ff:]
            low = jnp.concatenate([gate, zero, up, zero], axis=2)
            high = jnp.concatenate([zero, gate, zero, up], axis=2)
            both = jnp.concatenate([low, high], axis=1).reshape(2 * span, 4 * ff)
            wide[2 * span * group : 2 * span * (group + 1), :] = both.astype(BF)

    x = jnp.concatenate(
        [own_ref[...], next_ref[...], top_ref[...], bottom_ref[...], prev_ref[...]], axis=0
    )
    total = contract_rows(x, wide[...]).astype(BF)
    gate_ref[0] = total[:, :ff]
    gate_ref[1] = total[:, ff : 2 * ff]
    up_ref[0] = total[:, 2 * ff : 3 * ff]
    up_ref[1] = total[:, 3 * ff :]


def row_grads(gu, blocks, share):
    groups, span, double = gu.shape
    ff = double // 2
    rows = 2 * groups * span
    half = blocks[0].shape[1] - share
    out = jax.ShapeDtypeStruct((2, half, ff), BF)
    gate, up = call(
        row_grads_kernel,
        "row_grads",
        8 * rows * half * ff,
        2 * half * (rows + 4 * ff),
        grid=(half // TILE,),
        in_specs=[
            whole(gu.shape),
            *[pl.BlockSpec((b.shape[0], TILE), lambda j: (0, j)) for b in blocks],
        ],
        out_specs=[pl.BlockSpec((2, TILE, ff), lambda j: (0, j, 0))] * 2,
        out_shape=[out, out],
        scratch_shapes=[pltpu.VMEM((rows, 4 * ff), BF)],
    )(gu, *blocks)
    return gate.reshape(2 * half, ff), up.reshape(2 * half, ff)


def down_kernel(g_ref, *refs):
    outers, blocks = refs[:3], refs[3:8]
    out_ref, wide, held, sem = refs[8:]
    own, side, far = outers
    span, ff = own.shape
    locs = span // CAP
    unit = 2 * CAP
    step = pl.program_id(0)
    tile = g_ref.shape[1]
    share = held.shape[1]

    def spread(outer):
        rows = outer.reshape(locs, CAP, ff)
        zero = jnp.zeros_like(rows)
        low = jnp.concatenate([rows, zero], axis=2)
        high = jnp.concatenate([zero, rows], axis=2)
        return jnp.concatenate([low, high], axis=1)

    @pl.when(step == 0)
    def _():
        copies = []
        at = 0
        for k, ref in enumerate(blocks):
            source = ref.at[:, ref.shape[1] - share :]
            copies.append(
                pltpu.make_async_copy(source, held.at[at : at + ref.shape[0], :], sem.at[k])
            )
            at += ref.shape[0]
        start_all(copies)
        rows = []
        for k, outer in enumerate((own[...], side[:span], far[...], side[span:])):
            block = spread(outer).astype(BF)
            wide[:, k * unit : (k + 1) * unit, :] = block
            rows.append(block.reshape(2 * span, 2 * ff))
        wait_all(copies)
        total = contract_rows(jnp.concatenate(rows, axis=0), held[...]).astype(BF)
        out_ref[:, :share] = total[:ff]
        out_ref[:, share : 2 * share] = total[ff:]

    rows = wide[...].reshape(g_ref.shape[0], 2 * ff)
    total = contract_rows(rows, g_ref[...]).astype(BF)
    low = 2 * share + step * tile
    high = low + pl.num_programs(0) * tile
    out_ref[:, pl.ds(pl.multiple_of(low, 128), tile)] = total[:ff]
    out_ref[:, pl.ds(pl.multiple_of(high, 128), tile)] = total[ff:]


def down(outers, blocks, g_rows, share):
    rows, cols = g_rows.shape
    span, ff = outers[0].shape
    width = 2 * (cols + share)
    tile = TILE if cols % TILE == 0 else TILE // 2
    return call(
        down_kernel,
        "down",
        4 * rows * (cols + share) * ff,
        2 * (cols + share) * (rows + 2 * ff),
        grid=(cols // tile,),
        in_specs=[
            pl.BlockSpec((rows, tile), lambda j: (0, j)),
            *[whole(o.shape) for o in outers],
            *[ANY] * 5,
        ],
        out_specs=whole((ff, width)),
        out_shape=jax.ShapeDtypeStruct((ff, width), BF),
        scratch_shapes=[
            pltpu.VMEM((span // CAP, rows * CAP // span, 2 * ff), BF),
            pltpu.VMEM((rows, share), BF),
            pltpu.SemaphoreType.DMA((5,)),
        ],
    )(g_rows, *outers, *blocks)


def fold_kernel(in_ref, top_ref, bottom_ref, rest_ref):
    _, experts, depth, tile = in_ref.shape
    total = in_ref[0].astype(F32) + in_ref[1].astype(F32)
    at = 0
    for step in range(depth // CAP):
        part = total[:, step * CAP : (step + 1) * CAP, :].reshape(experts * CAP, tile).astype(BF)
        if step == 2:
            top_ref[...] = part[: experts * CAP // 2]
            bottom_ref[...] = part[experts * CAP // 2 :]
        else:
            rest_ref[at] = part
            at += 1


def fold(home):
    _, experts, depth, width = home.shape
    buf = experts * CAP
    tile = TILE
    return call(
        fold_kernel,
        "fold",
        experts * depth * width,
        6 * experts * depth * width,
        mib=20,
        grid=(width // tile,),
        in_specs=[pl.BlockSpec((2, experts, depth, tile), lambda j: (0, 0, 0, j))],
        out_specs=[
            pl.BlockSpec((buf // 2, tile), lambda j: (0, j)),
            pl.BlockSpec((buf // 2, tile), lambda j: (0, j)),
            pl.BlockSpec((3, buf, tile), lambda j: (0, 0, j)),
        ],
        out_shape=[
            jax.ShapeDtypeStruct((buf // 2, width), BF),
            jax.ShapeDtypeStruct((buf // 2, width), BF),
            jax.ShapeDtypeStruct((3, buf, width), BF),
        ],
    )(home)


def add_kernel(rest_ref, top_ref, bottom_ref, next_ref, prev_ref):
    mid = top_ref.shape[0]
    next_ref[:mid] = (rest_ref[1, :mid].astype(F32) + top_ref[...].astype(F32)).astype(BF)
    next_ref[mid:] = rest_ref[1, mid:]
    prev_ref[:mid] = rest_ref[2, :mid]
    prev_ref[mid:] = (rest_ref[2, mid:].astype(F32) + bottom_ref[...].astype(F32)).astype(BF)


def add_far(rest, top, bottom):
    _, buf, cols = rest.shape
    return call(
        add_kernel,
        "add_far",
        buf * cols,
        10 * buf * cols,
        mib=20,
        in_specs=[VMEM] * 3,
        out_specs=[VMEM] * 2,
        out_shape=[jax.ShapeDtypeStruct((buf, cols), BF)] * 2,
    )(rest, top, bottom)


def combine_kernel(split, table_ref, own_ref, left_ref, right_ref, wide_ref, out_ref):
    table = table_ref[...]

    @pl.when(pl.program_id(0) < split)
    def _():
        rows = jnp.concatenate([own_ref[...], left_ref[...], right_ref[...]], axis=0)
        thrice = jnp.concatenate([table] * 3, axis=0)
        out_ref[...] = contract_rows(thrice, rows).astype(BF)

    @pl.when(pl.program_id(0) >= split)
    def _():
        count, _, tile = wide_ref.shape
        rows = wide_ref[...].astype(F32).reshape(count * CAP, tile).astype(BF)
        both = jnp.concatenate([table, table], axis=0)
        out_ref[...] = contract_rows(both, rows).astype(BF)


def combine(table, rest, left, right, wide):
    buf, tok = table.shape
    width = left.shape[1] + wide.shape[2]
    tile = TILE
    split = left.shape[1] // tile
    block = pl.BlockSpec((buf, tile), lambda j: (0, jnp.minimum(j, split - 1)))
    return call(
        functools.partial(combine_kernel, split),
        "combine",
        2 * tok * buf * width,
        2 * width * (tok + 2 * buf),
        mib=20,
        grid=(width // tile,),
        in_specs=[
            whole((buf, tok)),
            pl.BlockSpec((None, buf, tile), lambda j: (0, 0, jnp.minimum(j, split - 1))),
            block,
            block,
            pl.BlockSpec((wide.shape[0], CAP, tile), lambda j: (0, 0, jnp.maximum(j - split, 0))),
        ],
        out_specs=pl.BlockSpec((tok, tile), lambda j: (0, j)),
        out_shape=jax.ShapeDtypeStruct((tok, width), BF),
    )(table, rest, left, right, wide)


def over_loc(a):
    return lax.all_to_all(a, "loc", split_axis=0, concat_axis=0, tiled=True)


def shift(a, step):
    groups = lax.axis_size("grp")
    return lax.ppermute(a, "grp", [(i, (i + step) % groups) for i in range(groups)])


def ring_gather(own):
    mid = own.shape[0] // 2
    before, after = shift(own, 1), shift(own, -1)
    return [own, after, shift(before[:mid], 1), shift(after[mid:], -1), before]


def body(tokens, grad_out, expert_ids, route_weight, gate_weight, up_weight, down_weight):
    groups = lax.axis_size("grp")
    locs = lax.axis_size("loc")
    experts = locs // 2
    width = tokens.shape[1]
    buf = experts * CAP
    unit = 2 * CAP
    share = 768
    ring_cols = 2560
    wide_cols = width - ring_cols

    w_gate, w_up, w_down = gate_weight[0], up_weight[0], down_weight[0]

    table, pick, g_share, g_send = dispatch_gradient(
        expert_ids.T, route_weight.T, grad_out, experts, share
    )
    g_blocks = ring_gather(g_send)
    xg_send = dispatch_token(pick, g_share, tokens, experts)
    xg = over_loc(xg_send.reshape(locs, unit, xg_send.shape[3]))
    xg, *g_blocks = lax.optimization_barrier((xg, *g_blocks))
    blocks = ring_gather(xg.reshape(locs * unit, xg.shape[2]))
    g_out = regroup(g_blocks)
    g_rows = over_loc(g_out.reshape(locs, groups * unit, g_out.shape[3]))
    g_rows = g_rows.reshape(locs * groups * unit, g_out.shape[3])

    own, after, top, bottom, before = blocks
    *pre_own, outer_own = pre([own], w_gate, w_up, w_down, share)
    *pre_side, outer_side = pre([after, before], w_gate, w_up, w_down, share)
    *pre_far, outer_far = pre([top, bottom], w_gate, w_up, w_down, share)
    gu, near, far_top, far_bottom = hidden(
        g_rows, w_down, w_gate, w_up, pre_own, pre_side, pre_far, wide_cols
    )

    came_top, came_bottom = shift(far_top, 1), shift(far_bottom, -1)
    part_ring = ring_part(near, w_gate, w_up, ring_cols)
    part_ring, gu = lax.optimization_barrier((part_ring, gu))
    home_ring = over_loc(part_ring.reshape(locs, groups * CAP, ring_cols))
    part_next, part_prev, part_own = side_part(gu, w_gate, w_up, came_top, came_bottom)
    from_before, from_after = shift(part_next, 1), shift(part_prev, -1)

    outers = (outer_own, outer_side, outer_far)
    part_own, gu, outers = lax.optimization_barrier((part_own, gu, outers))
    gate_grad, up_grad = row_grads(gu, blocks, share)
    down_grad = down(outers, blocks, g_rows, share)
    part_own, gate_grad, up_grad, down_grad = lax.optimization_barrier(
        (part_own, gate_grad, up_grad, down_grad)
    )
    home_wide = over_loc(sum_blocks(part_own, from_before, from_after))

    fold_top, fold_bottom, rest = fold(home_ring.reshape(2, experts, groups * CAP, ring_cols))
    fold_next, fold_prev = add_far(rest, shift(fold_top, 1), shift(fold_bottom, -1))
    tokens_grad = combine(table, rest, shift(fold_next, 1), shift(fold_prev, -1), home_wide)
    return (tokens_grad, gate_grad[None], up_grad[None], down_grad[None])


def solution(mesh):
    in_specs = (
        P(("grp", "loc"), None),
        P(("grp", "loc"), None),
        P(("grp", "loc"), None),
        P(("grp", "loc"), None),
        P("loc", None, "grp"),
        P("loc", None, "grp"),
        P("loc", "grp", None),
    )
    out_specs = (
        P(("grp", "loc"), None),
        P("loc", None, "grp"),
        P("loc", None, "grp"),
        P("loc", "grp", None),
    )
    return jax.shard_map(body, mesh=mesh, in_specs=in_specs, out_specs=out_specs, check_vma=False)
```

```python
import functools

import jax
import jax.numpy as jnp
from jax import lax
from jax.experimental import pallas as pl
from jax.experimental.pallas import tpu as pltpu
from jax.sharding import PartitionSpec as P

CAP = 4
BF = jnp.bfloat16
F32 = jnp.float32
TILE = 512
ANY = pl.BlockSpec(memory_space=pl.ANY)
VMEM = pl.BlockSpec(memory_space=pltpu.VMEM)


def contract_rows(left, right):
    return lax.dot_general(left, right, (((0,), (0,)), ((), ())), preferred_element_type=F32)


def contract_cols(left, right):
    return lax.dot_general(left, right, (((1,), (1,)), ((), ())), preferred_element_type=F32)


def whole(shape):
    return pl.BlockSpec(shape, lambda *_: (0,) * len(shape))


def call(kernel, name, flops, nbytes, mib=56, **kwargs):
    return pl.pallas_call(
        kernel,
        name=name,
        compiler_params=pltpu.CompilerParams(vmem_limit_bytes=mib << 20),
        cost_estimate=pl.CostEstimate(flops=flops, bytes_accessed=nbytes, transcendentals=0),
        **kwargs,
    )


def dispatch_gradient_kernel(ids_ref, w_ref, g_ref, table_ref, pick_ref, share_ref, ring_ref, held, sem):
    load = pltpu.make_async_copy(g_ref, held, sem.at[0])
    load.start()
    topk, tok = ids_ref.shape
    buf = table_ref.shape[0]
    unit = 2 * CAP
    share = share_ref.shape[1]
    cols = ring_ref.shape[1]

    def tables(count, per_expert):
        slot_row = lax.broadcasted_iota(jnp.int32, (count, tok), 0)
        expert = lax.div(slot_row, per_expert)
        weights = w_ref[...].astype(F32)
        chosen = jnp.zeros((count, tok), F32)
        weight = jnp.zeros((count, tok), F32)
        for k in range(topk):
            hit = ids_ref[k : k + 1, :] == expert
            chosen = jnp.where(hit, 1.0, chosen)
            weight = jnp.where(hit, weights[k : k + 1, :], weight)
        before = lax.broadcasted_iota(jnp.int32, (tok, tok), 0)
        after = lax.broadcasted_iota(jnp.int32, (tok, tok), 1)
        earlier = jnp.where(before < after, 1.0, 0.0).astype(BF)
        slot = jnp.dot(chosen.astype(BF), earlier, preferred_element_type=F32)
        mine = (chosen > 0.5) & (slot == lax.rem(slot_row, CAP).astype(F32))
        return jnp.where(mine, 1.0, 0.0), jnp.where(mine, weight, 0.0), slot_row

    table_ref[...] = tables(buf, CAP)[0].astype(BF)
    table, weighted, slot_row = tables(2 * buf, unit)
    low = lax.rem(slot_row, unit) < CAP
    pick_ref[0] = jnp.where(low, table, 0.0).astype(BF)
    pick_ref[1] = jnp.where(low, 0.0, table).astype(BF)
    both = jnp.concatenate(
        [jnp.where(low, weighted, 0.0).astype(BF), jnp.where(low, 0.0, weighted).astype(BF)], axis=1
    )
    load.wait()

    def rows(first, second, count):
        parts = jnp.concatenate(
            [held[:, first : first + count], held[:, second : second + count]], axis=0
        )
        return jnp.dot(both, parts, preferred_element_type=F32).astype(BF)

    share_ref[...] = rows(0, share, share)
    part = TILE // 2
    for first in range(0, cols, part):
        start = 2 * share + first
        ring_ref[:, first : first + part] = rows(start, start + cols, part)


def dispatch_gradient(ids, weights, grad_out, experts, share):
    tok, width = grad_out.shape
    buf = experts * CAP
    small = lambda *shape: jax.ShapeDtypeStruct(shape, BF)
    return call(
        dispatch_gradient_kernel,
        "dispatch_gradient",
        4 * tok * buf * width,
        2 * width * (tok + buf),
        in_specs=[VMEM, VMEM, ANY],
        out_specs=[VMEM] * 4,
        out_shape=[
            small(buf, tok),
            small(2, 2 * buf, tok),
            small(2 * buf, share),
            small(2 * buf, width // 2 - share),
        ],
        scratch_shapes=[pltpu.VMEM((tok, width), BF), pltpu.SemaphoreType.DMA((1,))],
    )(ids, weights, grad_out)


def dispatch_token_kernel(pick_ref, share_ref, t_ref, out_ref, held, staged, sem):
    load = pltpu.make_async_copy(t_ref, held, sem.at[0])
    load.start()
    _, experts, unit, cols = out_ref.shape
    share = share_ref.shape[1]
    half = cols - share
    both = jnp.concatenate([pick_ref[0], pick_ref[1]], axis=1)
    staged[:, :, half:] = share_ref[...].reshape(experts, unit, share)
    load.wait()
    for first in range(0, half, TILE):
        parts = jnp.concatenate(
            [held[:, first : first + TILE], held[:, half + first : half + first + TILE]], axis=0
        )
        rows = jnp.dot(both, parts, preferred_element_type=F32).astype(BF)
        staged[:, :, first : first + TILE] = rows.reshape(experts, unit, TILE)
    stores = [pltpu.make_async_copy(staged, out_ref.at[h], sem.at[1 + h]) for h in range(2)]
    for store in stores:
        store.start()
    for store in stores:
        store.wait()


def dispatch_token(pick, share, tokens, experts):
    tok, width = tokens.shape
    unit = 2 * CAP
    cols = width // 2 + share.shape[1]
    return call(
        dispatch_token_kernel,
        "dispatch_token",
        4 * tok * experts * CAP * width,
        2 * width * (tok + 2 * experts * CAP),
        in_specs=[VMEM, VMEM, ANY],
        out_specs=ANY,
        out_shape=jax.ShapeDtypeStruct((2, experts, unit, cols), BF),
        scratch_shapes=[
            pltpu.VMEM((tok, width), BF),
            pltpu.VMEM((experts, unit, cols), BF),
            pltpu.SemaphoreType.DMA((3,)),
        ],
    )(pick, share, tokens)


def regroup_kernel(own_ref, next_ref, top_ref, bottom_ref, prev_ref, out_ref, held, sem):
    experts, unit, _ = own_ref.shape
    parts = 4
    size = experts // parts
    loads, stores = [], []
    for p in range(parts):
        window = slice(p * size, (p + 1) * size)
        if p < parts // 2:
            far = top_ref.at[window]
        else:
            far = bottom_ref.at[p * size - experts // 2 : (p + 1) * size - experts // 2]
        sources = [own_ref.at[window], next_ref.at[window], far, prev_ref.at[window]]
        for k, source in enumerate(sources):
            target = held.at[window, k * unit : (k + 1) * unit, :]
            loads.append(pltpu.make_async_copy(source, target, sem.at[p * 4 + k]))
            loads[-1].start()
    for p in range(parts):
        window = slice(p * size, (p + 1) * size)
        for k in range(4):
            loads[p * 4 + k].wait()
        for h in range(2):
            index = parts * 4 + 2 * p + h
            stores.append(pltpu.make_async_copy(held.at[window], out_ref.at[h, window], sem.at[index]))
            stores[-1].start()
    for store in stores:
        store.wait()


def regroup(blocks):
    count, cols = blocks[0].shape
    unit = 2 * CAP
    experts = count // unit
    return call(
        regroup_kernel,
        "regroup",
        0,
        24 * count * cols,
        in_specs=[ANY] * 5,
        out_specs=ANY,
        out_shape=jax.ShapeDtypeStruct((2, experts, 4 * unit, cols), BF),
        scratch_shapes=[
            pltpu.VMEM((experts, 4 * unit, cols), BF),
            pltpu.SemaphoreType.DMA((24,)),
        ],
    )(*[b.reshape(b.shape[0] // unit, unit, cols) for b in blocks])


def pre_kernel(count, *refs):
    x_refs = refs[:count]
    wg_ref, wu_ref, wd_ref, slope_ref, swish_ref, part_ref, outer_ref, x, w, d, acc, sem = refs[count:]
    rows, cols = x.shape
    ff = w.shape[2] // 4
    share = d.shape[1]
    half = cols - share
    steps = half // TILE
    copies = [[] for _ in range(steps + 1)]
    index = 0

    def add(step, source, target):
        nonlocal index
        copies[step].append(pltpu.make_async_copy(source, target, sem.at[index]))
        index += 1

    for t in range(steps + 1):
        window = slice(t * TILE, (t + 1) * TILE) if t < steps else slice(half, cols)
        at = 0
        for ref in x_refs:
            add(t, ref.at[:, window], x.at[at : at + ref.shape[0], window])
            at += ref.shape[0]
        if t < steps:
            for k, ref in enumerate((wg_ref, wu_ref)):
                for h in range(2):
                    lane = (2 * k + h) * ff
                    source = ref.at[h * half + t * TILE : h * half + (t + 1) * TILE, :]
                    add(t, source, w.at[t, :, lane : lane + ff])
        else:
            for h in range(2):
                source = wd_ref.at[:, h * share : (h + 1) * share]
                add(t, source, d.at[h * ff : (h + 1) * ff, :])
    for group in copies:
        for copy in group:
            copy.start()
    for t in range(steps):
        for copy in copies[t]:
            copy.wait()
        value = jnp.dot(x[:, t * TILE : (t + 1) * TILE], w[t], preferred_element_type=F32)
        if t == 0:
            acc[...] = value
        else:
            acc[...] += value
    for copy in copies[steps]:
        copy.wait()

    def fold_halves(value):
        value = value.reshape(rows // (2 * CAP), 2 * CAP, 2 * ff)
        return (value[:, :CAP, :ff] + value[:, CAP:, ff:]).reshape(rows // 2, ff)

    part_ref[...] = fold_halves(contract_cols(x[:, half:], d[...]))
    gate = fold_halves(acc[:, : 2 * ff])
    up = fold_halves(acc[:, 2 * ff :])
    sig = 1.0 / (1.0 + jnp.exp(-gate))
    swish = gate * sig
    slope_ref[...] = up * sig * (1.0 + gate * (1.0 - sig))
    swish_ref[...] = swish
    outer_ref[...] = swish * up


def pre(blocks, w_gate, w_up, w_down, share):
    cols = blocks[0].shape[1]
    rows = sum(b.shape[0] for b in blocks)
    ff = w_gate.shape[1]
    steps = (cols - share) // TILE
    copies = (len(blocks) + 4) * steps + len(blocks) + 2
    return call(
        functools.partial(pre_kernel, len(blocks)),
        "pre",
        8 * rows * cols * ff,
        2 * cols * (rows + 4 * ff),
        in_specs=[ANY] * (len(blocks) + 3),
        out_specs=[VMEM] * 4,
        out_shape=[jax.ShapeDtypeStruct((rows // 2, ff), F32)] * 4,
        scratch_shapes=[
            pltpu.VMEM((rows, cols), BF),
            pltpu.VMEM((steps, TILE, 4 * ff), BF),
            pltpu.VMEM((2 * ff, share), BF),
            pltpu.VMEM((rows, 4 * ff), F32),
            pltpu.SemaphoreType.DMA((copies,)),
        ],
    )(*blocks, w_gate, w_up, w_down)


def load_weights(wg_ref, wu_ref, w, first, sem, index):
    count = w.shape[0]
    ff = wg_ref.shape[1]
    copies = []
    for k, ref in enumerate((wg_ref, wu_ref)):
        source = ref.at[first : first + count, :]
        target = w.at[:, k * ff : (k + 1) * ff]
        copies.append(pltpu.make_async_copy(source, target, sem.at[index + k]))
    return copies


def start_all(copies):
    for copy in copies:
        copy.start()


def wait_all(copies):
    for copy in copies:
        copy.wait()


def hidden_kernel(
    g_ref, wd_ref, wg_ref, wu_ref, *refs
):
    own, side, far = refs[0:3], refs[3:6], refs[6:9]
    gu_ref, near_ref, top_ref, bottom_ref, g, d, w, small, staged, sem = refs[9:]
    groups, span, double = gu_ref.shape
    ff = double // 2
    locs = span // CAP
    unit = 2 * CAP
    cols = g.shape[1]
    wide_cols = top_ref.shape[1]
    first_col = wd_ref.shape[1] - 2 * cols
    steps = 2
    tile = cols // steps
    loads = []
    for t in range(steps):
        window = slice(t * tile, (t + 1) * tile)
        loads.append(pltpu.make_async_copy(g_ref.at[:, window], g.at[:, window], sem.at[3 * t]))
        for h in range(2):
            start = first_col + h * cols + t * tile
            source = wd_ref.at[:, start : start + tile]
            target = d.at[h * ff : (h + 1) * ff, window]
            loads.append(pltpu.make_async_copy(source, target, sem.at[3 * t + 1 + h]))
    more = []
    index = 3 * steps
    for k in range(3):
        places = [(own[k], 0), (side[k].at[:span], 1), (far[k], 2), (side[k].at[span:], 3)]
        for source, group in places:
            more.append(pltpu.make_async_copy(source, small.at[k, group], sem.at[index]))
            index += 1
    weights = load_weights(wg_ref, wu_ref, w, wg_ref.shape[0] - wide_cols, sem, index)
    start_all(loads)
    start_all(more)
    start_all(weights)
    total = None
    for t in range(steps):
        wait_all(loads[3 * t : 3 * t + 3])
        window = slice(t * tile, (t + 1) * tile)
        value = contract_cols(g[:, window], d[:, window])
        total = value if total is None else total + value
    wait_all(more)
    halves = total.reshape(locs, groups * unit, double)
    for group in range(groups):
        first = group * unit
        hidden = (
            halves[:, first : first + CAP, :ff] + halves[:, first + CAP : first + unit, ff:]
        ).reshape(span, ff) + small[2, group]
        gate = hidden * small[0, group]
        up = hidden * small[1, group]
        both = jnp.concatenate([gate, up], axis=1)
        gu_ref[group] = both.astype(BF)
        near_ref[:, group * CAP : (group + 1) * CAP, :] = both.reshape(locs, CAP, double).astype(BF)
    wait_all(weights)
    staged[...] = contract_cols(gu_ref[2], w[...]).astype(BF)
    stores = [
        pltpu.make_async_copy(staged.at[: span // 2], top_ref, sem.at[index + 2]),
        pltpu.make_async_copy(staged.at[span // 2 :], bottom_ref, sem.at[index + 3]),
    ]
    start_all(stores)
    wait_all(stores)


def hidden(g_rows, w_down, w_gate, w_up, own, side, far, wide_cols):
    rows, cols = g_rows.shape
    span, ff = own[0].shape
    groups = rows // 2 // span
    small = lambda *shape: jax.ShapeDtypeStruct(shape, BF)
    return call(
        hidden_kernel,
        "hidden",
        4 * rows * cols * ff + 4 * span * ff * wide_cols,
        2 * (rows * cols + 2 * wide_cols * ff + span * wide_cols),
        in_specs=[ANY] * 13,
        out_specs=[VMEM, VMEM, ANY, ANY],
        out_shape=[
            small(groups, span, 2 * ff),
            small(span // CAP, groups * CAP, 2 * ff),
            small(span // 2, wide_cols),
            small(span // 2, wide_cols),
        ],
        scratch_shapes=[
            pltpu.VMEM((rows, cols), BF),
            pltpu.VMEM((2 * ff, cols), BF),
            pltpu.VMEM((wide_cols, 2 * ff), BF),
            pltpu.VMEM((3, groups, span, ff), F32),
            pltpu.VMEM((span, wide_cols), BF),
            pltpu.SemaphoreType.DMA((6 + 12 + 4,)),
        ],
    )(g_rows, w_down, w_gate, w_up, *own, *side, *far)


def ring_part_kernel(near_ref, wg_ref, wu_ref, out_ref, w, staged, sem):
    rows, ring_cols = out_ref.shape
    loads = load_weights(wg_ref, wu_ref, w, 0, sem, 0)
    start_all(loads)
    wait_all(loads)
    left = near_ref[...].reshape(rows, w.shape[1])
    stores = []
    for c in range(ring_cols // TILE):
        window = slice(c * TILE, (c + 1) * TILE)
        staged[:, window] = contract_cols(left, w[window, :]).astype(BF)
        target = out_ref.at[:, window]
        stores.append(pltpu.make_async_copy(staged.at[:, window], target, sem.at[2 + c]))
        stores[-1].start()
    wait_all(stores)


def ring_part(near, w_gate, w_up, ring_cols):
    locs, depth, double = near.shape
    rows = locs * depth
    return call(
        ring_part_kernel,
        "ring_part",
        2 * rows * double * ring_cols,
        2 * ring_cols * (rows + double),
        in_specs=[VMEM, ANY, ANY],
        out_specs=ANY,
        out_shape=jax.ShapeDtypeStruct((rows, ring_cols), BF),
        scratch_shapes=[
            pltpu.VMEM((ring_cols, double), BF),
            pltpu.VMEM((rows, ring_cols), BF),
            pltpu.SemaphoreType.DMA((2 + ring_cols // TILE,)),
        ],
    )(near, w_gate, w_up)


def side_kernel(gu_ref, wg_ref, wu_ref, top_ref, bottom_ref, next_ref, prev_ref, own_ref, w, held, staged, sem):
    _, span, double = gu_ref.shape
    wide_cols = next_ref.shape[1]
    weights = load_weights(wg_ref, wu_ref, w, wg_ref.shape[0] - wide_cols, sem, 0)
    came = [
        pltpu.make_async_copy(top_ref, held.at[0], sem.at[2]),
        pltpu.make_async_copy(bottom_ref, held.at[1], sem.at[3]),
    ]
    start_all(weights)
    start_all(came)
    wait_all(weights)
    wait_all(came)
    left = jnp.concatenate([gu_ref[1], gu_ref[3], gu_ref[0]], axis=0)
    mid = span // 2
    stores = []
    for c in range(wide_cols // TILE):
        window = slice(c * TILE, (c + 1) * TILE)
        value = contract_cols(left, w[window, :])
        top = held[0, :, window].astype(F32)
        bottom = held[1, :, window].astype(F32)
        staged[0, :mid, window] = (value[:mid] + top).astype(BF)
        staged[0, mid:, window] = value[mid:span].astype(BF)
        staged[1, :mid, window] = value[span : span + mid].astype(BF)
        staged[1, mid:, window] = (value[span + mid : 2 * span] + bottom).astype(BF)
        staged[2, :, window] = value[2 * span :].astype(BF)
        for k, ref in enumerate((next_ref, prev_ref, own_ref)):
            copy = pltpu.make_async_copy(
                staged.at[k, :, window], ref.at[:, window], sem.at[4 + 3 * c + k]
            )
            copy.start()
            stores.append(copy)
    wait_all(stores)


def side_part(gu, w_gate, w_up, top, bottom):
    _, span, double = gu.shape
    wide_cols = top.shape[1]
    return call(
        side_kernel,
        "side_part",
        6 * span * double * wide_cols,
        2 * wide_cols * (4 * span + double),
        mib=24,
        in_specs=[VMEM, ANY, ANY, ANY, ANY],
        out_specs=[ANY] * 3,
        out_shape=[jax.ShapeDtypeStruct((span, wide_cols), BF)] * 3,
        scratch_shapes=[
            pltpu.VMEM((wide_cols, double), BF),
            pltpu.VMEM((2, span // 2, wide_cols), BF),
            pltpu.VMEM((3, span, wide_cols), BF),
            pltpu.SemaphoreType.DMA((4 + 3 * (wide_cols // TILE),)),
        ],
    )(gu, w_gate, w_up, top, bottom)


def sum_kernel(a_ref, b_ref, c_ref, out_ref, held, staged, sem):
    locs, _, cols = out_ref.shape
    steps = cols // TILE
    loads, stores = [], []
    for t in range(steps):
        window = slice(t * TILE, (t + 1) * TILE)
        for k, ref in enumerate((a_ref, b_ref, c_ref)):
            loads.append(
                pltpu.make_async_copy(ref.at[:, window], held.at[k, :, window], sem.at[4 * t + k])
            )
    start_all(loads)
    for t in range(steps):
        wait_all(loads[3 * t : 3 * t + 3])
        window = slice(t * TILE, (t + 1) * TILE)
        total = sum(held[k, :, window].astype(F32) for k in range(3))
        staged[:, :, window] = total.reshape(locs, CAP, TILE).astype(BF)
        source = staged.at[:, :, window]
        stores.append(pltpu.make_async_copy(source, out_ref.at[:, :, window], sem.at[4 * t + 3]))
        stores[-1].start()
    wait_all(stores)


def sum_blocks(a, b, c):
    rows, cols = a.shape
    return call(
        sum_kernel,
        "sum_blocks",
        2 * rows * cols,
        8 * rows * cols,
        mib=24,
        in_specs=[ANY] * 3,
        out_specs=ANY,
        out_shape=jax.ShapeDtypeStruct((rows // CAP, CAP, cols), BF),
        scratch_shapes=[
            pltpu.VMEM((3, rows, cols), BF),
            pltpu.VMEM((rows // CAP, CAP, cols), BF),
            pltpu.SemaphoreType.DMA((4 * (cols // TILE),)),
        ],
    )(a, b, c)


def row_grads_kernel(gu_ref, own_ref, next_ref, top_ref, bottom_ref, prev_ref, gate_ref, up_ref, wide):
    groups, span, double = gu_ref.shape
    ff = double // 2
    locs = span // CAP

    @pl.when(pl.program_id(0) == 0)
    def _():
        zero = jnp.zeros((locs, CAP, ff), F32)
        for group in range(groups):
            both = gu_ref[group].astype(F32).reshape(locs, CAP, double)
            gate, up = both[:, :, :ff], both[:, :, ff:]
            low = jnp.concatenate([gate, zero, up, zero], axis=2)
            high = jnp.concatenate([zero, gate, zero, up], axis=2)
            both = jnp.concatenate([low, high], axis=1).reshape(2 * span, 4 * ff)
            wide[2 * span * group : 2 * span * (group + 1), :] = both.astype(BF)

    x = jnp.concatenate(
        [own_ref[...], next_ref[...], top_ref[...], bottom_ref[...], prev_ref[...]], axis=0
    )
    total = contract_rows(x, wide[...]).astype(BF)
    gate_ref[0] = total[:, :ff]
    gate_ref[1] = total[:, ff : 2 * ff]
    up_ref[0] = total[:, 2 * ff : 3 * ff]
    up_ref[1] = total[:, 3 * ff :]


def row_grads(gu, blocks, share):
    groups, span, double = gu.shape
    ff = double // 2
    rows = 2 * groups * span
    half = blocks[0].shape[1] - share
    out = jax.ShapeDtypeStruct((2, half, ff), BF)
    gate, up = call(
        row_grads_kernel,
        "row_grads",
        8 * rows * half * ff,
        2 * half * (rows + 4 * ff),
        grid=(half // TILE,),
        in_specs=[
            whole(gu.shape),
            *[pl.BlockSpec((b.shape[0], TILE), lambda j: (0, j)) for b in blocks],
        ],
        out_specs=[pl.BlockSpec((2, TILE, ff), lambda j: (0, j, 0))] * 2,
        out_shape=[out, out],
        scratch_shapes=[pltpu.VMEM((rows, 4 * ff), BF)],
    )(gu, *blocks)
    return gate.reshape(2 * half, ff), up.reshape(2 * half, ff)


def down_kernel(g_ref, *refs):
    outers, blocks = refs[:3], refs[3:8]
    out_ref, wide, held, sem = refs[8:]
    own, side, far = outers
    span, ff = own.shape
    locs = span // CAP
    unit = 2 * CAP
    step = pl.program_id(0)
    tile = g_ref.shape[1]
    share = held.shape[1]

    def spread(outer):
        rows = outer.reshape(locs, CAP, ff)
        zero = jnp.zeros_like(rows)
        low = jnp.concatenate([rows, zero], axis=2)
        high = jnp.concatenate([zero, rows], axis=2)
        return jnp.concatenate([low, high], axis=1)

    @pl.when(step == 0)
    def _():
        copies = []
        at = 0
        for k, ref in enumerate(blocks):
            source = ref.at[:, ref.shape[1] - share :]
            copies.append(
                pltpu.make_async_copy(source, held.at[at : at + ref.shape[0], :], sem.at[k])
            )
            at += ref.shape[0]
        start_all(copies)
        rows = []
        for k, outer in enumerate((own[...], side[:span], far[...], side[span:])):
            block = spread(outer).astype(BF)
            wide[:, k * unit : (k + 1) * unit, :] = block
            rows.append(block.reshape(2 * span, 2 * ff))
        wait_all(copies)
        total = contract_rows(jnp.concatenate(rows, axis=0), held[...]).astype(BF)
        out_ref[:, :share] = total[:ff]
        out_ref[:, share : 2 * share] = total[ff:]

    rows = wide[...].reshape(g_ref.shape[0], 2 * ff)
    total = contract_rows(rows, g_ref[...]).astype(BF)
    low = 2 * share + step * tile
    high = low + pl.num_programs(0) * tile
    out_ref[:, pl.ds(pl.multiple_of(low, 128), tile)] = total[:ff]
    out_ref[:, pl.ds(pl.multiple_of(high, 128), tile)] = total[ff:]


def down(outers, blocks, g_rows, share):
    rows, cols = g_rows.shape
    span, ff = outers[0].shape
    width = 2 * (cols + share)
    tile = TILE if cols % TILE == 0 else TILE // 2
    return call(
        down_kernel,
        "down",
        4 * rows * (cols + share) * ff,
        2 * (cols + share) * (rows + 2 * ff),
        grid=(cols // tile,),
        in_specs=[
            pl.BlockSpec((rows, tile), lambda j: (0, j)),
            *[whole(o.shape) for o in outers],
            *[ANY] * 5,
        ],
        out_specs=whole((ff, width)),
        out_shape=jax.ShapeDtypeStruct((ff, width), BF),
        scratch_shapes=[
            pltpu.VMEM((span // CAP, rows * CAP // span, 2 * ff), BF),
            pltpu.VMEM((rows, share), BF),
            pltpu.SemaphoreType.DMA((5,)),
        ],
    )(g_rows, *outers, *blocks)


def fold_kernel(in_ref, top_ref, bottom_ref, rest_ref):
    _, experts, depth, tile = in_ref.shape
    total = in_ref[0].astype(F32) + in_ref[1].astype(F32)
    at = 0
    for step in range(depth // CAP):
        part = total[:, step * CAP : (step + 1) * CAP, :].reshape(experts * CAP, tile).astype(BF)
        if step == 2:
            top_ref[...] = part[: experts * CAP // 2]
            bottom_ref[...] = part[experts * CAP // 2 :]
        else:
            rest_ref[at] = part
            at += 1


def fold(home):
    _, experts, depth, width = home.shape
    buf = experts * CAP
    tile = TILE
    return call(
        fold_kernel,
        "fold",
        experts * depth * width,
        6 * experts * depth * width,
        mib=20,
        grid=(width // tile,),
        in_specs=[pl.BlockSpec((2, experts, depth, tile), lambda j: (0, 0, 0, j))],
        out_specs=[
            pl.BlockSpec((buf // 2, tile), lambda j: (0, j)),
            pl.BlockSpec((buf // 2, tile), lambda j: (0, j)),
            pl.BlockSpec((3, buf, tile), lambda j: (0, 0, j)),
        ],
        out_shape=[
            jax.ShapeDtypeStruct((buf // 2, width), BF),
            jax.ShapeDtypeStruct((buf // 2, width), BF),
            jax.ShapeDtypeStruct((3, buf, width), BF),
        ],
    )(home)


def add_kernel(rest_ref, top_ref, bottom_ref, next_ref, prev_ref):
    mid = top_ref.shape[0]
    next_ref[:mid] = (rest_ref[1, :mid].astype(F32) + top_ref[...].astype(F32)).astype(BF)
    next_ref[mid:] = rest_ref[1, mid:]
    prev_ref[:mid] = rest_ref[2, :mid]
    prev_ref[mid:] = (rest_ref[2, mid:].astype(F32) + bottom_ref[...].astype(F32)).astype(BF)


def add_far(rest, top, bottom):
    _, buf, cols = rest.shape
    return call(
        add_kernel,
        "add_far",
        buf * cols,
        10 * buf * cols,
        mib=20,
        in_specs=[VMEM] * 3,
        out_specs=[VMEM] * 2,
        out_shape=[jax.ShapeDtypeStruct((buf, cols), BF)] * 2,
    )(rest, top, bottom)


def combine_kernel(table_ref, rest_ref, left_ref, right_ref, wide_ref, out_ref, ring, wide, staged, sem):
    buf = table_ref.shape[0]
    ring_cols = ring.shape[1]
    locs, _, wide_cols = wide.shape
    loads, stores = [], []

    def add(source, target):
        loads.append(pltpu.make_async_copy(source, target, sem.at[len(loads)]))

    for k, ref in enumerate((rest_ref.at[0], left_ref, right_ref)):
        add(ref, ring.at[k * buf : (k + 1) * buf, :])
    for first in range(0, wide_cols, TILE):
        window = slice(first, first + TILE)
        add(wide_ref.at[:, :, window], wide.at[:, :, window])
    start_all(loads)
    table = table_ref[...]
    twice = jnp.concatenate([table] * 2, axis=0)
    thrice = jnp.concatenate([table] * 3, axis=0)
    wait_all(loads[:3])
    for t in range((ring_cols + wide_cols) // TILE):
        window = slice(t * TILE, (t + 1) * TILE)
        first = t * TILE - ring_cols
        if first < 0:
            total = contract_rows(thrice, ring[:, window])
        else:
            loads[3 + first // TILE].wait()
            rows = wide[:, :, first : first + TILE].astype(F32).reshape(locs * CAP, TILE).astype(BF)
            total = contract_rows(twice, rows)
        staged[:, window] = total.astype(BF)
        target = out_ref.at[:, window]
        index = len(loads) + len(stores)
        stores.append(pltpu.make_async_copy(staged.at[:, window], target, sem.at[index]))
        stores[-1].start()
    wait_all(stores)


def combine(table, rest, left, right, wide):
    buf, tok = table.shape
    ring_cols, wide_cols = left.shape[1], wide.shape[2]
    width = ring_cols + wide_cols
    return call(
        combine_kernel,
        "combine",
        2 * tok * buf * width,
        2 * width * (tok + 2 * buf),
        mib=24,
        in_specs=[VMEM, ANY, ANY, ANY, ANY],
        out_specs=ANY,
        out_shape=jax.ShapeDtypeStruct((tok, width), BF),
        scratch_shapes=[
            pltpu.VMEM((3 * buf, ring_cols), BF),
            pltpu.VMEM((wide.shape[0], CAP, wide_cols), BF),
            pltpu.VMEM((tok, width), BF),
            pltpu.SemaphoreType.DMA((3 + wide_cols // TILE + width // TILE,)),
        ],
    )(table, rest, left, right, wide)


def over_loc(a):
    return lax.all_to_all(a, "loc", split_axis=0, concat_axis=0, tiled=True)


def shift(a, step):
    groups = lax.axis_size("grp")
    return lax.ppermute(a, "grp", [(i, (i + step) % groups) for i in range(groups)])


def ring_gather(own):
    mid = own.shape[0] // 2
    before, after = shift(own, 1), shift(own, -1)
    return [own, after, shift(before[:mid], 1), shift(after[mid:], -1), before]


def body(tokens, grad_out, expert_ids, route_weight, gate_weight, up_weight, down_weight):
    groups = lax.axis_size("grp")
    locs = lax.axis_size("loc")
    experts = locs // 2
    width = tokens.shape[1]
    buf = experts * CAP
    unit = 2 * CAP
    share = 512
    ring_cols = 3584
    wide_cols = width - ring_cols

    w_gate, w_up, w_down = gate_weight[0], up_weight[0], down_weight[0]

    table, pick, g_share, g_send = dispatch_gradient(
        expert_ids.T, route_weight.T, grad_out, experts, share
    )
    g_blocks = ring_gather(g_send)
    xg_send = dispatch_token(pick, g_share, tokens, experts)
    xg = over_loc(xg_send.reshape(locs, unit, xg_send.shape[3]))
    xg, *g_blocks = lax.optimization_barrier((xg, *g_blocks))
    blocks = ring_gather(xg.reshape(locs * unit, xg.shape[2]))
    g_out = regroup(g_blocks)
    g_rows = over_loc(g_out.reshape(locs, groups * unit, g_out.shape[3]))
    g_rows = g_rows.reshape(locs * groups * unit, g_out.shape[3])

    own, after, top, bottom, before = blocks
    *pre_own, outer_own = pre([own], w_gate, w_up, w_down, share)
    *pre_side, outer_side = pre([after, before], w_gate, w_up, w_down, share)
    *pre_far, outer_far = pre([top, bottom], w_gate, w_up, w_down, share)
    gu, near, far_top, far_bottom = hidden(
        g_rows, w_down, w_gate, w_up, pre_own, pre_side, pre_far, wide_cols
    )

    came_top, came_bottom = shift(far_top, 1), shift(far_bottom, -1)
    part_ring = ring_part(near, w_gate, w_up, ring_cols)
    part_ring, gu = lax.optimization_barrier((part_ring, gu))
    home_ring = over_loc(part_ring.reshape(locs, groups * CAP, ring_cols))
    part_next, part_prev, part_own = side_part(gu, w_gate, w_up, came_top, came_bottom)
    from_before, from_after = shift(part_next, 1), shift(part_prev, -1)

    outers = (outer_own, outer_side, outer_far)
    part_own, gu, outers = lax.optimization_barrier((part_own, gu, outers))
    gate_grad, up_grad = row_grads(gu, blocks, share)
    down_grad = down(outers, blocks, g_rows, share)
    part_own, gate_grad, up_grad, down_grad = lax.optimization_barrier(
        (part_own, gate_grad, up_grad, down_grad)
    )
    home_wide = over_loc(sum_blocks(part_own, from_before, from_after))

    fold_top, fold_bottom, rest = fold(home_ring.reshape(2, experts, groups * CAP, ring_cols))
    fold_next, fold_prev = add_far(rest, shift(fold_top, 1), shift(fold_bottom, -1))
    tokens_grad = combine(table, rest, shift(fold_next, 1), shift(fold_prev, -1), home_wide)
    return (tokens_grad, gate_grad[None], up_grad[None], down_grad[None])


def solution(mesh):
    in_specs = (
        P(("grp", "loc"), None),
        P(("grp", "loc"), None),
        P(("grp", "loc"), None),
        P(("grp", "loc"), None),
        P("loc", None, "grp"),
        P("loc", None, "grp"),
        P("loc", "grp", None),
    )
    out_specs = (
        P(("grp", "loc"), None),
        P("loc", None, "grp"),
        P("loc", None, "grp"),
        P("loc", "grp", None),
    )
    return jax.shard_map(body, mesh=mesh, in_specs=in_specs, out_specs=out_specs, check_vma=False)
```

```python
import functools

import jax
import jax.numpy as jnp
from jax import lax
from jax.experimental import pallas as pl
from jax.experimental.pallas import tpu as pltpu
from jax.sharding import PartitionSpec as P

CAP = 4
BF = jnp.bfloat16
F32 = jnp.float32
TILE = 512
ANY = pl.BlockSpec(memory_space=pl.ANY)
VMEM = pl.BlockSpec(memory_space=pltpu.VMEM)


def contract_rows(left, right):
    return lax.dot_general(left, right, (((0,), (0,)), ((), ())), preferred_element_type=F32)


def contract_cols(left, right):
    return lax.dot_general(left, right, (((1,), (1,)), ((), ())), preferred_element_type=F32)


def whole(shape):
    return pl.BlockSpec(shape, lambda *_: (0,) * len(shape))


def call(kernel, name, flops, nbytes, mib=56, **kwargs):
    return pl.pallas_call(
        kernel,
        name=name,
        compiler_params=pltpu.CompilerParams(vmem_limit_bytes=mib << 20),
        cost_estimate=pl.CostEstimate(flops=flops, bytes_accessed=nbytes, transcendentals=0),
        **kwargs,
    )


def dispatch_gradient_kernel(ids_ref, w_ref, g_ref, table_ref, pick_ref, share_ref, ring_ref, held, sem):
    load = pltpu.make_async_copy(g_ref, held, sem.at[0])
    load.start()
    topk, tok = ids_ref.shape
    buf = table_ref.shape[0]
    unit = 2 * CAP
    share = share_ref.shape[1]
    cols = ring_ref.shape[1]

    def tables(count, per_expert):
        slot_row = lax.broadcasted_iota(jnp.int32, (count, tok), 0)
        expert = lax.div(slot_row, per_expert)
        weights = w_ref[...].astype(F32)
        chosen = jnp.zeros((count, tok), F32)
        weight = jnp.zeros((count, tok), F32)
        for k in range(topk):
            hit = ids_ref[k : k + 1, :] == expert
            chosen = jnp.where(hit, 1.0, chosen)
            weight = jnp.where(hit, weights[k : k + 1, :], weight)
        before = lax.broadcasted_iota(jnp.int32, (tok, tok), 0)
        after = lax.broadcasted_iota(jnp.int32, (tok, tok), 1)
        earlier = jnp.where(before < after, 1.0, 0.0).astype(BF)
        slot = jnp.dot(chosen.astype(BF), earlier, preferred_element_type=F32)
        mine = (chosen > 0.5) & (slot == lax.rem(slot_row, CAP).astype(F32))
        return jnp.where(mine, 1.0, 0.0), jnp.where(mine, weight, 0.0), slot_row

    table_ref[...] = tables(buf, CAP)[0].astype(BF)
    table, weighted, slot_row = tables(2 * buf, unit)
    low = lax.rem(slot_row, unit) < CAP
    pick_ref[0] = jnp.where(low, table, 0.0).astype(BF)
    pick_ref[1] = jnp.where(low, 0.0, table).astype(BF)
    both = jnp.concatenate(
        [jnp.where(low, weighted, 0.0).astype(BF), jnp.where(low, 0.0, weighted).astype(BF)], axis=1
    )
    load.wait()

    def rows(first, second, count):
        parts = jnp.concatenate(
            [held[:, first : first + count], held[:, second : second + count]], axis=0
        )
        return jnp.dot(both, parts, preferred_element_type=F32).astype(BF)

    share_ref[...] = rows(0, share, share)
    part = TILE // 2
    for first in range(0, cols, part):
        start = 2 * share + first
        ring_ref[:, first : first + part] = rows(start, start + cols, part)


def dispatch_gradient(ids, weights, grad_out, experts, share):
    tok, width = grad_out.shape
    buf = experts * CAP
    small = lambda *shape: jax.ShapeDtypeStruct(shape, BF)
    return call(
        dispatch_gradient_kernel,
        "dispatch_gradient",
        4 * tok * buf * width,
        2 * width * (tok + buf),
        in_specs=[VMEM, VMEM, ANY],
        out_specs=[VMEM] * 4,
        out_shape=[
            small(buf, tok),
            small(2, 2 * buf, tok),
            small(2 * buf, share),
            small(2 * buf, width // 2 - share),
        ],
        scratch_shapes=[pltpu.VMEM((tok, width), BF), pltpu.SemaphoreType.DMA((1,))],
    )(ids, weights, grad_out)


def dispatch_token_kernel(pick_ref, share_ref, t_ref, out_ref, held, staged, sem):
    load = pltpu.make_async_copy(t_ref, held, sem.at[0])
    load.start()
    _, experts, unit, cols = out_ref.shape
    share = share_ref.shape[1]
    half = cols - share
    both = jnp.concatenate([pick_ref[0], pick_ref[1]], axis=1)
    staged[:, :, half:] = share_ref[...].reshape(experts, unit, share)
    load.wait()
    for first in range(0, half, TILE):
        parts = jnp.concatenate(
            [held[:, first : first + TILE], held[:, half + first : half + first + TILE]], axis=0
        )
        rows = jnp.dot(both, parts, preferred_element_type=F32).astype(BF)
        staged[:, :, first : first + TILE] = rows.reshape(experts, unit, TILE)
    stores = [pltpu.make_async_copy(staged, out_ref.at[h], sem.at[1 + h]) for h in range(2)]
    for store in stores:
        store.start()
    for store in stores:
        store.wait()


def dispatch_token(pick, share, tokens, experts):
    tok, width = tokens.shape
    unit = 2 * CAP
    cols = width // 2 + share.shape[1]
    return call(
        dispatch_token_kernel,
        "dispatch_token",
        4 * tok * experts * CAP * width,
        2 * width * (tok + 2 * experts * CAP),
        in_specs=[VMEM, VMEM, ANY],
        out_specs=ANY,
        out_shape=jax.ShapeDtypeStruct((2, experts, unit, cols), BF),
        scratch_shapes=[
            pltpu.VMEM((tok, width), BF),
            pltpu.VMEM((experts, unit, cols), BF),
            pltpu.SemaphoreType.DMA((3,)),
        ],
    )(pick, share, tokens)


def regroup_kernel(own_ref, next_ref, top_ref, bottom_ref, prev_ref, out_ref, held, sem):
    experts, unit, _ = own_ref.shape
    parts = 4
    size = experts // parts
    loads, stores = [], []
    for p in range(parts):
        window = slice(p * size, (p + 1) * size)
        if p < parts // 2:
            far = top_ref.at[window]
        else:
            far = bottom_ref.at[p * size - experts // 2 : (p + 1) * size - experts // 2]
        sources = [own_ref.at[window], next_ref.at[window], far, prev_ref.at[window]]
        for k, source in enumerate(sources):
            target = held.at[window, k * unit : (k + 1) * unit, :]
            loads.append(pltpu.make_async_copy(source, target, sem.at[p * 4 + k]))
            loads[-1].start()
    for p in range(parts):
        window = slice(p * size, (p + 1) * size)
        for k in range(4):
            loads[p * 4 + k].wait()
        for h in range(2):
            index = parts * 4 + 2 * p + h
            stores.append(pltpu.make_async_copy(held.at[window], out_ref.at[h, window], sem.at[index]))
            stores[-1].start()
    for store in stores:
        store.wait()


def regroup(blocks):
    count, cols = blocks[0].shape
    unit = 2 * CAP
    experts = count // unit
    return call(
        regroup_kernel,
        "regroup",
        0,
        24 * count * cols,
        in_specs=[ANY] * 5,
        out_specs=ANY,
        out_shape=jax.ShapeDtypeStruct((2, experts, 4 * unit, cols), BF),
        scratch_shapes=[
            pltpu.VMEM((experts, 4 * unit, cols), BF),
            pltpu.SemaphoreType.DMA((24,)),
        ],
    )(*[b.reshape(b.shape[0] // unit, unit, cols) for b in blocks])


def pre_kernel(count, *refs):
    x_refs = refs[:count]
    wg_ref, wu_ref, wd_ref, slope_ref, swish_ref, part_ref, outer_ref, x, w, d, acc, sem = refs[count:]
    rows, cols = x.shape
    ff = w.shape[2] // 4
    share = d.shape[1]
    half = cols - share
    steps = half // TILE
    copies = [[] for _ in range(steps + 1)]
    index = 0

    def add(step, source, target):
        nonlocal index
        copies[step].append(pltpu.make_async_copy(source, target, sem.at[index]))
        index += 1

    for t in range(steps + 1):
        window = slice(t * TILE, (t + 1) * TILE) if t < steps else slice(half, cols)
        at = 0
        for ref in x_refs:
            add(t, ref.at[:, window], x.at[at : at + ref.shape[0], window])
            at += ref.shape[0]
        if t < steps:
            for k, ref in enumerate((wg_ref, wu_ref)):
                for h in range(2):
                    lane = (2 * k + h) * ff
                    source = ref.at[h * half + t * TILE : h * half + (t + 1) * TILE, :]
                    add(t, source, w.at[t, :, lane : lane + ff])
        else:
            for h in range(2):
                source = wd_ref.at[:, h * share : (h + 1) * share]
                add(t, source, d.at[h * ff : (h + 1) * ff, :])
    for group in copies:
        for copy in group:
            copy.start()
    for t in range(steps):
        for copy in copies[t]:
            copy.wait()
        value = jnp.dot(x[:, t * TILE : (t + 1) * TILE], w[t], preferred_element_type=F32)
        if t == 0:
            acc[...] = value
        else:
            acc[...] += value
    for copy in copies[steps]:
        copy.wait()

    def fold_halves(value):
        value = value.reshape(rows // (2 * CAP), 2 * CAP, 2 * ff)
        return (value[:, :CAP, :ff] + value[:, CAP:, ff:]).reshape(rows // 2, ff)

    part_ref[...] = fold_halves(contract_cols(x[:, half:], d[...]))
    gate = fold_halves(acc[:, : 2 * ff])
    up = fold_halves(acc[:, 2 * ff :])
    sig = 1.0 / (1.0 + jnp.exp(-gate))
    swish = gate * sig
    slope_ref[...] = up * sig * (1.0 + gate * (1.0 - sig))
    swish_ref[...] = swish
    outer_ref[...] = swish * up


def pre(blocks, w_gate, w_up, w_down, share):
    cols = blocks[0].shape[1]
    rows = sum(b.shape[0] for b in blocks)
    ff = w_gate.shape[1]
    steps = (cols - share) // TILE
    copies = (len(blocks) + 4) * steps + len(blocks) + 2
    return call(
        functools.partial(pre_kernel, len(blocks)),
        "pre",
        200 * (8 * rows * cols * ff),
        200 * (2 * cols * (rows + 4 * ff)),
        in_specs=[ANY] * (len(blocks) + 3),
        out_specs=[VMEM] * 4,
        out_shape=[jax.ShapeDtypeStruct((rows // 2, ff), F32)] * 4,
        scratch_shapes=[
            pltpu.VMEM((rows, cols), BF),
            pltpu.VMEM((steps, TILE, 4 * ff), BF),
            pltpu.VMEM((2 * ff, share), BF),
            pltpu.VMEM((rows, 4 * ff), F32),
            pltpu.SemaphoreType.DMA((copies,)),
        ],
    )(*blocks, w_gate, w_up, w_down)


def load_weights(wg_ref, wu_ref, w, first, sem, index):
    count = w.shape[0]
    ff = wg_ref.shape[1]
    copies = []
    for k, ref in enumerate((wg_ref, wu_ref)):
        source = ref.at[first : first + count, :]
        target = w.at[:, k * ff : (k + 1) * ff]
        copies.append(pltpu.make_async_copy(source, target, sem.at[index + k]))
    return copies


def start_all(copies):
    for copy in copies:
        copy.start()


def wait_all(copies):
    for copy in copies:
        copy.wait()


def hidden_kernel(
    g_ref, wd_ref, wg_ref, wu_ref, *refs
):
    own, side, far = refs[0:3], refs[3:6], refs[6:9]
    gu_ref, near_ref, top_ref, bottom_ref, g, d, w, small, staged, sem = refs[9:]
    groups, span, double = gu_ref.shape
    ff = double // 2
    locs = span // CAP
    unit = 2 * CAP
    cols = g.shape[1]
    wide_cols = top_ref.shape[1]
    first_col = wd_ref.shape[1] - 2 * cols
    steps = 2
    tile = cols // steps
    loads = []
    for t in range(steps):
        window = slice(t * tile, (t + 1) * tile)
        loads.append(pltpu.make_async_copy(g_ref.at[:, window], g.at[:, window], sem.at[3 * t]))
        for h in range(2):
            start = first_col + h * cols + t * tile
            source = wd_ref.at[:, start : start + tile]
            target = d.at[h * ff : (h + 1) * ff, window]
            loads.append(pltpu.make_async_copy(source, target, sem.at[3 * t + 1 + h]))
    more = []
    index = 3 * steps
    for k in range(3):
        places = [(own[k], 0), (side[k].at[:span], 1), (far[k], 2), (side[k].at[span:], 3)]
        for source, group in places:
            more.append(pltpu.make_async_copy(source, small.at[k, group], sem.at[index]))
            index += 1
    weights = load_weights(wg_ref, wu_ref, w, wg_ref.shape[0] - wide_cols, sem, index)
    start_all(loads)
    start_all(more)
    start_all(weights)
    total = None
    for t in range(steps):
        wait_all(loads[3 * t : 3 * t + 3])
        window = slice(t * tile, (t + 1) * tile)
        value = contract_cols(g[:, window], d[:, window])
        total = value if total is None else total + value
    wait_all(more)
    halves = total.reshape(locs, groups * unit, double)
    for group in range(groups):
        first = group * unit
        hidden = (
            halves[:, first : first + CAP, :ff] + halves[:, first + CAP : first + unit, ff:]
        ).reshape(span, ff) + small[2, group]
        gate = hidden * small[0, group]
        up = hidden * small[1, group]
        both = jnp.concatenate([gate, up], axis=1)
        gu_ref[group] = both.astype(BF)
        near_ref[:, group * CAP : (group + 1) * CAP, :] = both.reshape(locs, CAP, double).astype(BF)
    wait_all(weights)
    staged[...] = contract_cols(gu_ref[2], w[...]).astype(BF)
    stores = [
        pltpu.make_async_copy(staged.at[: span // 2], top_ref, sem.at[index + 2]),
        pltpu.make_async_copy(staged.at[span // 2 :], bottom_ref, sem.at[index + 3]),
    ]
    start_all(stores)
    wait_all(stores)


def hidden(g_rows, w_down, w_gate, w_up, own, side, far, wide_cols):
    rows, cols = g_rows.shape
    span, ff = own[0].shape
    groups = rows // 2 // span
    small = lambda *shape: jax.ShapeDtypeStruct(shape, BF)
    return call(
        hidden_kernel,
        "hidden",
        4 * rows * cols * ff + 4 * span * ff * wide_cols,
        2 * (rows * cols + 2 * wide_cols * ff + span * wide_cols),
        in_specs=[ANY] * 13,
        out_specs=[VMEM, VMEM, ANY, ANY],
        out_shape=[
            small(groups, span, 2 * ff),
            small(span // CAP, groups * CAP, 2 * ff),
            small(span // 2, wide_cols),
            small(span // 2, wide_cols),
        ],
        scratch_shapes=[
            pltpu.VMEM((rows, cols), BF),
            pltpu.VMEM((2 * ff, cols), BF),
            pltpu.VMEM((wide_cols, 2 * ff), BF),
            pltpu.VMEM((3, groups, span, ff), F32),
            pltpu.VMEM((span, wide_cols), BF),
            pltpu.SemaphoreType.DMA((6 + 12 + 4,)),
        ],
    )(g_rows, w_down, w_gate, w_up, *own, *side, *far)


def ring_part_kernel(near_ref, wg_ref, wu_ref, out_ref, w, staged, sem):
    rows, ring_cols = out_ref.shape
    loads = load_weights(wg_ref, wu_ref, w, 0, sem, 0)
    start_all(loads)
    wait_all(loads)
    left = near_ref[...].reshape(rows, w.shape[1])
    stores = []
    for c in range(ring_cols // TILE):
        window = slice(c * TILE, (c + 1) * TILE)
        staged[:, window] = contract_cols(left, w[window, :]).astype(BF)
        target = out_ref.at[:, window]
        stores.append(pltpu.make_async_copy(staged.at[:, window], target, sem.at[2 + c]))
        stores[-1].start()
    wait_all(stores)


def ring_part(near, w_gate, w_up, ring_cols):
    locs, depth, double = near.shape
    rows = locs * depth
    return call(
        ring_part_kernel,
        "ring_part",
        2 * rows * double * ring_cols,
        2 * ring_cols * (rows + double),
        in_specs=[VMEM, ANY, ANY],
        out_specs=ANY,
        out_shape=jax.ShapeDtypeStruct((rows, ring_cols), BF),
        scratch_shapes=[
            pltpu.VMEM((ring_cols, double), BF),
            pltpu.VMEM((rows, ring_cols), BF),
            pltpu.SemaphoreType.DMA((2 + ring_cols // TILE,)),
        ],
    )(near, w_gate, w_up)


def side_kernel(gu_ref, wg_ref, wu_ref, top_ref, bottom_ref, next_ref, prev_ref, own_ref, w, held, staged, sem):
    _, span, double = gu_ref.shape
    wide_cols = next_ref.shape[1]
    weights = load_weights(wg_ref, wu_ref, w, wg_ref.shape[0] - wide_cols, sem, 0)
    came = [
        pltpu.make_async_copy(top_ref, held.at[0], sem.at[2]),
        pltpu.make_async_copy(bottom_ref, held.at[1], sem.at[3]),
    ]
    start_all(weights)
    start_all(came)
    wait_all(weights)
    wait_all(came)
    left = jnp.concatenate([gu_ref[1], gu_ref[3], gu_ref[0]], axis=0)
    mid = span // 2
    stores = []
    for c in range(wide_cols // TILE):
        window = slice(c * TILE, (c + 1) * TILE)
        value = contract_cols(left, w[window, :])
        top = held[0, :, window].astype(F32)
        bottom = held[1, :, window].astype(F32)
        staged[0, :mid, window] = (value[:mid] + top).astype(BF)
        staged[0, mid:, window] = value[mid:span].astype(BF)
        staged[1, :mid, window] = value[span : span + mid].astype(BF)
        staged[1, mid:, window] = (value[span + mid : 2 * span] + bottom).astype(BF)
        staged[2, :, window] = value[2 * span :].astype(BF)
        for k, ref in enumerate((next_ref, prev_ref, own_ref)):
            copy = pltpu.make_async_copy(
                staged.at[k, :, window], ref.at[:, window], sem.at[4 + 3 * c + k]
            )
            copy.start()
            stores.append(copy)
    wait_all(stores)


def side_part(gu, w_gate, w_up, top, bottom):
    _, span, double = gu.shape
    wide_cols = top.shape[1]
    return call(
        side_kernel,
        "side_part",
        40 * (6 * span * double * wide_cols),
        40 * (2 * wide_cols * (4 * span + double)),
        mib=24,
        in_specs=[VMEM, ANY, ANY, ANY, ANY],
        out_specs=[ANY] * 3,
        out_shape=[jax.ShapeDtypeStruct((span, wide_cols), BF)] * 3,
        scratch_shapes=[
            pltpu.VMEM((wide_cols, double), BF),
            pltpu.VMEM((2, span // 2, wide_cols), BF),
            pltpu.VMEM((3, span, wide_cols), BF),
            pltpu.SemaphoreType.DMA((4 + 3 * (wide_cols // TILE),)),
        ],
    )(gu, w_gate, w_up, top, bottom)


def sum_kernel(a_ref, b_ref, c_ref, out_ref, held, staged, sem):
    locs, _, cols = out_ref.shape
    steps = cols // TILE
    loads, stores = [], []
    for t in range(steps):
        window = slice(t * TILE, (t + 1) * TILE)
        for k, ref in enumerate((a_ref, b_ref, c_ref)):
            loads.append(
                pltpu.make_async_copy(ref.at[:, window], held.at[k, :, window], sem.at[4 * t + k])
            )
    start_all(loads)
    for t in range(steps):
        wait_all(loads[3 * t : 3 * t + 3])
        window = slice(t * TILE, (t + 1) * TILE)
        total = sum(held[k, :, window].astype(F32) for k in range(3))
        staged[:, :, window] = total.reshape(locs, CAP, TILE).astype(BF)
        source = staged.at[:, :, window]
        stores.append(pltpu.make_async_copy(source, out_ref.at[:, :, window], sem.at[4 * t + 3]))
        stores[-1].start()
    wait_all(stores)


def sum_blocks(a, b, c):
    rows, cols = a.shape
    return call(
        sum_kernel,
        "sum_blocks",
        2 * rows * cols,
        8 * rows * cols,
        mib=24,
        in_specs=[ANY] * 3,
        out_specs=ANY,
        out_shape=jax.ShapeDtypeStruct((rows // CAP, CAP, cols), BF),
        scratch_shapes=[
            pltpu.VMEM((3, rows, cols), BF),
            pltpu.VMEM((rows // CAP, CAP, cols), BF),
            pltpu.SemaphoreType.DMA((4 * (cols // TILE),)),
        ],
    )(a, b, c)


def row_grads_kernel(gu_ref, own_ref, next_ref, top_ref, bottom_ref, prev_ref, gate_ref, up_ref, wide):
    groups, span, double = gu_ref.shape
    ff = double // 2
    locs = span // CAP

    @pl.when(pl.program_id(0) == 0)
    def _():
        zero = jnp.zeros((locs, CAP, ff), F32)
        for group in range(groups):
            both = gu_ref[group].astype(F32).reshape(locs, CAP, double)
            gate, up = both[:, :, :ff], both[:, :, ff:]
            low = jnp.concatenate([gate, zero, up, zero], axis=2)
            high = jnp.concatenate([zero, gate, zero, up], axis=2)
            both = jnp.concatenate([low, high], axis=1).reshape(2 * span, 4 * ff)
            wide[2 * span * group : 2 * span * (group + 1), :] = both.astype(BF)

    x = jnp.concatenate(
        [own_ref[...], next_ref[...], top_ref[...], bottom_ref[...], prev_ref[...]], axis=0
    )
    total = contract_rows(x, wide[...]).astype(BF)
    gate_ref[0] = total[:, :ff]
    gate_ref[1] = total[:, ff : 2 * ff]
    up_ref[0] = total[:, 2 * ff : 3 * ff]
    up_ref[1] = total[:, 3 * ff :]


def row_grads(gu, blocks, share):
    groups, span, double = gu.shape
    ff = double // 2
    rows = 2 * groups * span
    half = blocks[0].shape[1] - share
    out = jax.ShapeDtypeStruct((2, half, ff), BF)
    gate, up = call(
        row_grads_kernel,
        "row_grads",
        8 * rows * half * ff,
        2 * half * (rows + 4 * ff),
        grid=(half // TILE,),
        in_specs=[
            whole(gu.shape),
            *[pl.BlockSpec((b.shape[0], TILE), lambda j: (0, j)) for b in blocks],
        ],
        out_specs=[pl.BlockSpec((2, TILE, ff), lambda j: (0, j, 0))] * 2,
        out_shape=[out, out],
        scratch_shapes=[pltpu.VMEM((rows, 4 * ff), BF)],
    )(gu, *blocks)
    return gate.reshape(2 * half, ff), up.reshape(2 * half, ff)


def down_kernel(g_ref, *refs):
    outers, blocks = refs[:3], refs[3:8]
    out_ref, wide, held, sem = refs[8:]
    own, side, far = outers
    span, ff = own.shape
    locs = span // CAP
    unit = 2 * CAP
    step = pl.program_id(0)
    tile = g_ref.shape[1]
    share = held.shape[1]

    def spread(outer):
        rows = outer.reshape(locs, CAP, ff)
        zero = jnp.zeros_like(rows)
        low = jnp.concatenate([rows, zero], axis=2)
        high = jnp.concatenate([zero, rows], axis=2)
        return jnp.concatenate([low, high], axis=1)

    @pl.when(step == 0)
    def _():
        copies = []
        at = 0
        for k, ref in enumerate(blocks):
            source = ref.at[:, ref.shape[1] - share :]
            copies.append(
                pltpu.make_async_copy(source, held.at[at : at + ref.shape[0], :], sem.at[k])
            )
            at += ref.shape[0]
        start_all(copies)
        rows = []
        for k, outer in enumerate((own[...], side[:span], far[...], side[span:])):
            block = spread(outer).astype(BF)
            wide[:, k * unit : (k + 1) * unit, :] = block
            rows.append(block.reshape(2 * span, 2 * ff))
        wait_all(copies)
        total = contract_rows(jnp.concatenate(rows, axis=0), held[...]).astype(BF)
        out_ref[:, :share] = total[:ff]
        out_ref[:, share : 2 * share] = total[ff:]

    rows = wide[...].reshape(g_ref.shape[0], 2 * ff)
    total = contract_rows(rows, g_ref[...]).astype(BF)
    low = 2 * share + step * tile
    high = low + pl.num_programs(0) * tile
    out_ref[:, pl.ds(pl.multiple_of(low, 128), tile)] = total[:ff]
    out_ref[:, pl.ds(pl.multiple_of(high, 128), tile)] = total[ff:]


def down(outers, blocks, g_rows, share):
    rows, cols = g_rows.shape
    span, ff = outers[0].shape
    width = 2 * (cols + share)
    tile = TILE if cols % TILE == 0 else TILE // 2
    return call(
        down_kernel,
        "down",
        4 * rows * (cols + share) * ff,
        2 * (cols + share) * (rows + 2 * ff),
        grid=(cols // tile,),
        in_specs=[
            pl.BlockSpec((rows, tile), lambda j: (0, j)),
            *[whole(o.shape) for o in outers],
            *[ANY] * 5,
        ],
        out_specs=whole((ff, width)),
        out_shape=jax.ShapeDtypeStruct((ff, width), BF),
        scratch_shapes=[
            pltpu.VMEM((span // CAP, rows * CAP // span, 2 * ff), BF),
            pltpu.VMEM((rows, share), BF),
            pltpu.SemaphoreType.DMA((5,)),
        ],
    )(g_rows, *outers, *blocks)


def fold_kernel(in_ref, top_ref, bottom_ref, rest_ref):
    _, experts, depth, tile = in_ref.shape
    total = in_ref[0].astype(F32) + in_ref[1].astype(F32)
    at = 0
    for step in range(depth // CAP):
        part = total[:, step * CAP : (step + 1) * CAP, :].reshape(experts * CAP, tile).astype(BF)
        if step == 2:
            top_ref[...] = part[: experts * CAP // 2]
            bottom_ref[...] = part[experts * CAP // 2 :]
        else:
            rest_ref[at] = part
            at += 1


def fold(home):
    _, experts, depth, width = home.shape
    buf = experts * CAP
    tile = TILE
    return call(
        fold_kernel,
        "fold",
        experts * depth * width,
        6 * experts * depth * width,
        mib=20,
        grid=(width // tile,),
        in_specs=[pl.BlockSpec((2, experts, depth, tile), lambda j: (0, 0, 0, j))],
        out_specs=[
            pl.BlockSpec((buf // 2, tile), lambda j: (0, j)),
            pl.BlockSpec((buf // 2, tile), lambda j: (0, j)),
            pl.BlockSpec((3, buf, tile), lambda j: (0, 0, j)),
        ],
        out_shape=[
            jax.ShapeDtypeStruct((buf // 2, width), BF),
            jax.ShapeDtypeStruct((buf // 2, width), BF),
            jax.ShapeDtypeStruct((3, buf, width), BF),
        ],
    )(home)


def add_kernel(rest_ref, top_ref, bottom_ref, next_ref, prev_ref):
    mid = top_ref.shape[0]
    next_ref[:mid] = (rest_ref[1, :mid].astype(F32) + top_ref[...].astype(F32)).astype(BF)
    next_ref[mid:] = rest_ref[1, mid:]
    prev_ref[:mid] = rest_ref[2, :mid]
    prev_ref[mid:] = (rest_ref[2, mid:].astype(F32) + bottom_ref[...].astype(F32)).astype(BF)


def add_far(rest, top, bottom):
    _, buf, cols = rest.shape
    return call(
        add_kernel,
        "add_far",
        buf * cols,
        10 * buf * cols,
        mib=20,
        in_specs=[VMEM] * 3,
        out_specs=[VMEM] * 2,
        out_shape=[jax.ShapeDtypeStruct((buf, cols), BF)] * 2,
    )(rest, top, bottom)


def combine_kernel(table_ref, rest_ref, left_ref, right_ref, wide_ref, out_ref, ring, wide, staged, sem):
    buf = table_ref.shape[0]
    ring_cols = ring.shape[1]
    locs, _, wide_cols = wide.shape
    loads, stores = [], []

    def add(source, target):
        loads.append(pltpu.make_async_copy(source, target, sem.at[len(loads)]))

    for k, ref in enumerate((rest_ref.at[0], left_ref, right_ref)):
        add(ref, ring.at[k * buf : (k + 1) * buf, :])
    for first in range(0, wide_cols, TILE):
        window = slice(first, first + TILE)
        add(wide_ref.at[:, :, window], wide.at[:, :, window])
    start_all(loads)
    table = table_ref[...]
    twice = jnp.concatenate([table] * 2, axis=0)
    thrice = jnp.concatenate([table] * 3, axis=0)
    wait_all(loads[:3])
    for t in range((ring_cols + wide_cols) // TILE):
        window = slice(t * TILE, (t + 1) * TILE)
        first = t * TILE - ring_cols
        if first < 0:
            total = contract_rows(thrice, ring[:, window])
        else:
            loads[3 + first // TILE].wait()
            rows = wide[:, :, first : first + TILE].astype(F32).reshape(locs * CAP, TILE).astype(BF)
            total = contract_rows(twice, rows)
        staged[:, window] = total.astype(BF)
        target = out_ref.at[:, window]
        index = len(loads) + len(stores)
        stores.append(pltpu.make_async_copy(staged.at[:, window], target, sem.at[index]))
        stores[-1].start()
    wait_all(stores)


def combine(table, rest, left, right, wide):
    buf, tok = table.shape
    ring_cols, wide_cols = left.shape[1], wide.shape[2]
    width = ring_cols + wide_cols
    return call(
        combine_kernel,
        "combine",
        2 * tok * buf * width,
        2 * width * (tok + 2 * buf),
        mib=24,
        in_specs=[VMEM, ANY, ANY, ANY, ANY],
        out_specs=ANY,
        out_shape=jax.ShapeDtypeStruct((tok, width), BF),
        scratch_shapes=[
            pltpu.VMEM((3 * buf, ring_cols), BF),
            pltpu.VMEM((wide.shape[0], CAP, wide_cols), BF),
            pltpu.VMEM((tok, width), BF),
            pltpu.SemaphoreType.DMA((3 + wide_cols // TILE + width // TILE,)),
        ],
    )(table, rest, left, right, wide)


def over_loc(a):
    return lax.all_to_all(a, "loc", split_axis=0, concat_axis=0, tiled=True)


def shift(a, step):
    groups = lax.axis_size("grp")
    return lax.ppermute(a, "grp", [(i, (i + step) % groups) for i in range(groups)])


def ring_gather(own):
    mid = own.shape[0] // 2
    before, after = shift(own, 1), shift(own, -1)
    return [own, after, shift(before[:mid], 1), shift(after[mid:], -1), before]


def body(tokens, grad_out, expert_ids, route_weight, gate_weight, up_weight, down_weight):
    groups = lax.axis_size("grp")
    locs = lax.axis_size("loc")
    experts = locs // 2
    width = tokens.shape[1]
    buf = experts * CAP
    unit = 2 * CAP
    share = 768
    ring_cols = 3072
    wide_cols = width - ring_cols

    w_gate, w_up, w_down = gate_weight[0], up_weight[0], down_weight[0]

    table, pick, g_share, g_send = dispatch_gradient(
        expert_ids.T, route_weight.T, grad_out, experts, share
    )
    g_blocks = ring_gather(g_send)
    xg_send = dispatch_token(pick, g_share, tokens, experts)
    xg = over_loc(xg_send.reshape(locs, unit, xg_send.shape[3]))
    xg, *g_blocks = lax.optimization_barrier((xg, *g_blocks))
    blocks = ring_gather(xg.reshape(locs * unit, xg.shape[2]))
    g_out = regroup(g_blocks)
    g_rows = over_loc(g_out.reshape(locs, groups * unit, g_out.shape[3]))
    g_rows = g_rows.reshape(locs * groups * unit, g_out.shape[3])

    own, after, top, bottom, before = blocks
    *pre_own, outer_own = pre([own], w_gate, w_up, w_down, share)
    *pre_side, outer_side = pre([after, before], w_gate, w_up, w_down, share)
    *pre_far, outer_far = pre([top, bottom], w_gate, w_up, w_down, share)
    gu, near, far_top, far_bottom = hidden(
        g_rows, w_down, w_gate, w_up, pre_own, pre_side, pre_far, wide_cols
    )

    came_top, came_bottom = shift(far_top, 1), shift(far_bottom, -1)
    part_ring = ring_part(near, w_gate, w_up, ring_cols)
    part_ring, gu = lax.optimization_barrier((part_ring, gu))
    home_ring = over_loc(part_ring.reshape(locs, groups * CAP, ring_cols))
    part_next, part_prev, part_own = side_part(gu, w_gate, w_up, came_top, came_bottom)
    from_before, from_after = shift(part_next, 1), shift(part_prev, -1)

    outers = (outer_own, outer_side, outer_far)
    part_own, gu, outers = lax.optimization_barrier((part_own, gu, outers))
    gate_grad, up_grad = row_grads(gu, blocks, share)
    down_grad = down(outers, blocks, g_rows, share)
    part_own, gate_grad, up_grad, down_grad = lax.optimization_barrier(
        (part_own, gate_grad, up_grad, down_grad)
    )
    home_wide = over_loc(sum_blocks(part_own, from_before, from_after))

    fold_top, fold_bottom, rest = fold(home_ring.reshape(2, experts, groups * CAP, ring_cols))
    fold_next, fold_prev = add_far(rest, shift(fold_top, 1), shift(fold_bottom, -1))
    tokens_grad = combine(table, rest, shift(fold_next, 1), shift(fold_prev, -1), home_wide)
    return (tokens_grad, gate_grad[None], up_grad[None], down_grad[None])


def solution(mesh):
    in_specs = (
        P(("grp", "loc"), None),
        P(("grp", "loc"), None),
        P(("grp", "loc"), None),
        P(("grp", "loc"), None),
        P("loc", None, "grp"),
        P("loc", None, "grp"),
        P("loc", "grp", None),
    )
    out_specs = (
        P(("grp", "loc"), None),
        P("loc", None, "grp"),
        P("loc", None, "grp"),
        P("loc", "grp", None),
    )
    return jax.shard_map(body, mesh=mesh, in_specs=in_specs, out_specs=out_specs, check_vma=False)
```

```python
import functools

import jax
import jax.numpy as jnp
from jax import lax
from jax.experimental import pallas as pl
from jax.experimental.pallas import tpu as pltpu
from jax.sharding import PartitionSpec as P

CAP = 4
BF = jnp.bfloat16
F32 = jnp.float32
TILE = 512
ANY = pl.BlockSpec(memory_space=pl.ANY)
VMEM = pl.BlockSpec(memory_space=pltpu.VMEM)
HBM = pl.BlockSpec(memory_space=pltpu.HBM)


def contract_rows(left, right):
    return lax.dot_general(left, right, (((0,), (0,)), ((), ())), preferred_element_type=F32)


def contract_cols(left, right):
    return lax.dot_general(left, right, (((1,), (1,)), ((), ())), preferred_element_type=F32)


def whole(shape):
    return pl.BlockSpec(shape, lambda *_: (0,) * len(shape))


def call(kernel, name, flops, nbytes, mib=56, **kwargs):
    return pl.pallas_call(
        kernel,
        name=name,
        compiler_params=pltpu.CompilerParams(vmem_limit_bytes=mib << 20),
        cost_estimate=pl.CostEstimate(flops=flops, bytes_accessed=nbytes, transcendentals=0),
        **kwargs,
    )


def dispatch_gradient_kernel(ids_ref, w_ref, g_ref, table_ref, pick_ref, share_ref, ring_ref, held, sem):
    load = pltpu.make_async_copy(g_ref, held, sem.at[0])
    load.start()
    topk, tok = ids_ref.shape
    buf = table_ref.shape[0]
    unit = 2 * CAP
    share = share_ref.shape[1]
    cols = ring_ref.shape[1]

    def tables(count, per_expert):
        slot_row = lax.broadcasted_iota(jnp.int32, (count, tok), 0)
        expert = lax.div(slot_row, per_expert)
        weights = w_ref[...].astype(F32)
        chosen = jnp.zeros((count, tok), F32)
        weight = jnp.zeros((count, tok), F32)
        for k in range(topk):
            hit = ids_ref[k : k + 1, :] == expert
            chosen = jnp.where(hit, 1.0, chosen)
            weight = jnp.where(hit, weights[k : k + 1, :], weight)
        before = lax.broadcasted_iota(jnp.int32, (tok, tok), 0)
        after = lax.broadcasted_iota(jnp.int32, (tok, tok), 1)
        earlier = jnp.where(before < after, 1.0, 0.0).astype(BF)
        slot = jnp.dot(chosen.astype(BF), earlier, preferred_element_type=F32)
        mine = (chosen > 0.5) & (slot == lax.rem(slot_row, CAP).astype(F32))
        return jnp.where(mine, 1.0, 0.0), jnp.where(mine, weight, 0.0), slot_row

    table_ref[...] = tables(buf, CAP)[0].astype(BF)
    table, weighted, slot_row = tables(2 * buf, unit)
    low = lax.rem(slot_row, unit) < CAP
    pick_ref[0] = jnp.where(low, table, 0.0).astype(BF)
    pick_ref[1] = jnp.where(low, 0.0, table).astype(BF)
    both = jnp.concatenate(
        [jnp.where(low, weighted, 0.0).astype(BF), jnp.where(low, 0.0, weighted).astype(BF)], axis=1
    )
    load.wait()

    def rows(first, second, count):
        parts = jnp.concatenate(
            [held[:, first : first + count], held[:, second : second + count]], axis=0
        )
        return jnp.dot(both, parts, preferred_element_type=F32).astype(BF)

    share_ref[...] = rows(0, share, share)
    part = TILE // 2
    for first in range(0, cols, part):
        start = 2 * share + first
        ring_ref[:, first : first + part] = rows(start, start + cols, part)


def dispatch_gradient(ids, weights, grad_out, experts, share):
    tok, width = grad_out.shape
    buf = experts * CAP
    small = lambda *shape: jax.ShapeDtypeStruct(shape, BF)
    return call(
        dispatch_gradient_kernel,
        "dispatch_gradient",
        4 * tok * buf * width,
        2 * width * (tok + buf),
        in_specs=[VMEM, VMEM, ANY],
        out_specs=[VMEM] * 4,
        out_shape=[
            small(buf, tok),
            small(2, 2 * buf, tok),
            small(2 * buf, share),
            small(2 * buf, width // 2 - share),
        ],
        scratch_shapes=[pltpu.VMEM((tok, width), BF), pltpu.SemaphoreType.DMA((1,))],
    )(ids, weights, grad_out)


def dispatch_token_kernel(pick_ref, share_ref, t_ref, out_ref, held, staged, sem):
    load = pltpu.make_async_copy(t_ref, held, sem.at[0])
    load.start()
    _, experts, unit, cols = out_ref.shape
    share = share_ref.shape[1]
    half = cols - share
    both = jnp.concatenate([pick_ref[0], pick_ref[1]], axis=1)
    staged[:, :, half:] = share_ref[...].reshape(experts, unit, share)
    load.wait()
    for first in range(0, half, TILE):
        parts = jnp.concatenate(
            [held[:, first : first + TILE], held[:, half + first : half + first + TILE]], axis=0
        )
        rows = jnp.dot(both, parts, preferred_element_type=F32).astype(BF)
        staged[:, :, first : first + TILE] = rows.reshape(experts, unit, TILE)
    stores = [pltpu.make_async_copy(staged, out_ref.at[h], sem.at[1 + h]) for h in range(2)]
    for store in stores:
        store.start()
    for store in stores:
        store.wait()


def dispatch_token(pick, share, tokens, experts):
    tok, width = tokens.shape
    unit = 2 * CAP
    cols = width // 2 + share.shape[1]
    return call(
        dispatch_token_kernel,
        "dispatch_token",
        4 * tok * experts * CAP * width,
        2 * width * (tok + 2 * experts * CAP),
        in_specs=[VMEM, VMEM, ANY],
        out_specs=ANY,
        out_shape=jax.ShapeDtypeStruct((2, experts, unit, cols), BF),
        scratch_shapes=[
            pltpu.VMEM((tok, width), BF),
            pltpu.VMEM((experts, unit, cols), BF),
            pltpu.SemaphoreType.DMA((3,)),
        ],
    )(pick, share, tokens)


def regroup_kernel(own_ref, next_ref, top_ref, bottom_ref, prev_ref, out_ref, held, sem):
    experts, unit, _ = own_ref.shape
    parts = 4
    size = experts // parts
    loads, stores = [], []
    for p in range(parts):
        window = slice(p * size, (p + 1) * size)
        if p < parts // 2:
            far = top_ref.at[window]
        else:
            far = bottom_ref.at[p * size - experts // 2 : (p + 1) * size - experts // 2]
        sources = [own_ref.at[window], next_ref.at[window], far, prev_ref.at[window]]
        for k, source in enumerate(sources):
            target = held.at[window, k * unit : (k + 1) * unit, :]
            loads.append(pltpu.make_async_copy(source, target, sem.at[p * 4 + k]))
            loads[-1].start()
    for p in range(parts):
        window = slice(p * size, (p + 1) * size)
        for k in range(4):
            loads[p * 4 + k].wait()
        for h in range(2):
            index = parts * 4 + 2 * p + h
            stores.append(pltpu.make_async_copy(held.at[window], out_ref.at[h, window], sem.at[index]))
            stores[-1].start()
    for store in stores:
        store.wait()


def regroup(blocks):
    count, cols = blocks[0].shape
    unit = 2 * CAP
    experts = count // unit
    return call(
        regroup_kernel,
        "regroup",
        0,
        24 * count * cols,
        in_specs=[ANY] * 5,
        out_specs=ANY,
        out_shape=jax.ShapeDtypeStruct((2, experts, 4 * unit, cols), BF),
        scratch_shapes=[
            pltpu.VMEM((experts, 4 * unit, cols), BF),
            pltpu.SemaphoreType.DMA((24,)),
        ],
    )(*[b.reshape(b.shape[0] // unit, unit, cols) for b in blocks])


def pre_kernel(count, *refs):
    x_refs = refs[:count]
    wg_ref, wu_ref, wd_ref, slope_ref, swish_ref, part_ref, outer_ref, x, w, d, acc, sem = refs[count:]
    rows, cols = x.shape
    ff = w.shape[2] // 4
    share = d.shape[1]
    half = cols - share
    steps = half // TILE
    copies = [[] for _ in range(steps + 1)]
    index = 0

    def add(step, source, target):
        nonlocal index
        copies[step].append(pltpu.make_async_copy(source, target, sem.at[index]))
        index += 1

    for t in range(steps + 1):
        window = slice(t * TILE, (t + 1) * TILE) if t < steps else slice(half, cols)
        at = 0
        for ref in x_refs:
            add(t, ref.at[:, window], x.at[at : at + ref.shape[0], window])
            at += ref.shape[0]
        if t < steps:
            for k, ref in enumerate((wg_ref, wu_ref)):
                for h in range(2):
                    lane = (2 * k + h) * ff
                    source = ref.at[h * half + t * TILE : h * half + (t + 1) * TILE, :]
                    add(t, source, w.at[t, :, lane : lane + ff])
        else:
            for h in range(2):
                source = wd_ref.at[:, h * share : (h + 1) * share]
                add(t, source, d.at[h * ff : (h + 1) * ff, :])
    for group in copies:
        for copy in group:
            copy.start()
    for t in range(steps):
        for copy in copies[t]:
            copy.wait()
        value = jnp.dot(x[:, t * TILE : (t + 1) * TILE], w[t], preferred_element_type=F32)
        if t == 0:
            acc[...] = value
        else:
            acc[...] += value
    for copy in copies[steps]:
        copy.wait()

    def fold_halves(value):
        value = value.reshape(rows // (2 * CAP), 2 * CAP, 2 * ff)
        return (value[:, :CAP, :ff] + value[:, CAP:, ff:]).reshape(rows // 2, ff)

    part_ref[...] = fold_halves(contract_cols(x[:, half:], d[...]))
    gate = fold_halves(acc[:, : 2 * ff])
    up = fold_halves(acc[:, 2 * ff :])
    sig = 1.0 / (1.0 + jnp.exp(-gate))
    swish = gate * sig
    slope_ref[...] = up * sig * (1.0 + gate * (1.0 - sig))
    swish_ref[...] = swish
    outer_ref[...] = swish * up


def pre(blocks, w_gate, w_up, w_down, share):
    cols = blocks[0].shape[1]
    rows = sum(b.shape[0] for b in blocks)
    ff = w_gate.shape[1]
    steps = (cols - share) // TILE
    copies = (len(blocks) + 4) * steps + len(blocks) + 2
    return call(
        functools.partial(pre_kernel, len(blocks)),
        "pre",
        200 * (8 * rows * cols * ff),
        200 * (2 * cols * (rows + 4 * ff)),
        in_specs=[ANY] * len(blocks) + [HBM] * 3,
        out_specs=[VMEM] * 4,
        out_shape=[jax.ShapeDtypeStruct((rows // 2, ff), F32)] * 4,
        scratch_shapes=[
            pltpu.VMEM((rows, cols), BF),
            pltpu.VMEM((steps, TILE, 4 * ff), BF),
            pltpu.VMEM((2 * ff, share), BF),
            pltpu.VMEM((rows, 4 * ff), F32),
            pltpu.SemaphoreType.DMA((copies,)),
        ],
    )(*blocks, w_gate, w_up, w_down)


def load_weights(wg_ref, wu_ref, w, first, sem, index):
    count = w.shape[0]
    ff = wg_ref.shape[1]
    copies = []
    for k, ref in enumerate((wg_ref, wu_ref)):
        source = ref.at[first : first + count, :]
        target = w.at[:, k * ff : (k + 1) * ff]
        copies.append(pltpu.make_async_copy(source, target, sem.at[index + k]))
    return copies


def start_all(copies):
    for copy in copies:
        copy.start()


def wait_all(copies):
    for copy in copies:
        copy.wait()


def hidden_kernel(
    g_ref, wd_ref, wg_ref, wu_ref, *refs
):
    own, side, far = refs[0:3], refs[3:6], refs[6:9]
    gu_ref, near_ref, top_ref, bottom_ref, g, d, w, small, staged, sem = refs[9:]
    groups, span, double = gu_ref.shape
    ff = double // 2
    locs = span // CAP
    unit = 2 * CAP
    cols = g.shape[1]
    wide_cols = top_ref.shape[1]
    first_col = wd_ref.shape[1] - 2 * cols
    tile = 3 * TILE // 2
    windows = [slice(at, min(at + tile, cols)) for at in range(0, cols, tile)]
    steps = len(windows)
    loads = []
    for t, window in enumerate(windows):
        loads.append(pltpu.make_async_copy(g_ref.at[:, window], g.at[:, window], sem.at[3 * t]))
        for h in range(2):
            start = first_col + h * cols + window.start
            source = wd_ref.at[:, start : start + window.stop - window.start]
            target = d.at[h * ff : (h + 1) * ff, window]
            loads.append(pltpu.make_async_copy(source, target, sem.at[3 * t + 1 + h]))
    more = []
    index = 3 * steps
    for k in range(3):
        places = [(own[k], 0), (side[k].at[:span], 1), (far[k], 2), (side[k].at[span:], 3)]
        for source, group in places:
            more.append(pltpu.make_async_copy(source, small.at[k, group], sem.at[index]))
            index += 1
    weights = load_weights(wg_ref, wu_ref, w, wg_ref.shape[0] - wide_cols, sem, index)
    start_all(loads)
    start_all(more)
    start_all(weights)
    total = None
    for t, window in enumerate(windows):
        wait_all(loads[3 * t : 3 * t + 3])
        value = contract_cols(g[:, window], d[:, window])
        total = value if total is None else total + value
    wait_all(more)
    halves = total.reshape(locs, groups * unit, double)
    for group in range(groups):
        first = group * unit
        hidden = (
            halves[:, first : first + CAP, :ff] + halves[:, first + CAP : first + unit, ff:]
        ).reshape(span, ff) + small[2, group]
        gate = hidden * small[0, group]
        up = hidden * small[1, group]
        both = jnp.concatenate([gate, up], axis=1)
        gu_ref[group] = both.astype(BF)
        near_ref[:, group * CAP : (group + 1) * CAP, :] = both.reshape(locs, CAP, double).astype(BF)
    wait_all(weights)
    staged[...] = contract_cols(gu_ref[2], w[...]).astype(BF)
    stores = [
        pltpu.make_async_copy(staged.at[: span // 2], top_ref, sem.at[index + 2]),
        pltpu.make_async_copy(staged.at[span // 2 :], bottom_ref, sem.at[index + 3]),
    ]
    start_all(stores)
    wait_all(stores)


def hidden(g_rows, w_down, w_gate, w_up, own, side, far, wide_cols):
    rows, cols = g_rows.shape
    span, ff = own[0].shape
    groups = rows // 2 // span
    small = lambda *shape: jax.ShapeDtypeStruct(shape, BF)
    return call(
        hidden_kernel,
        "hidden",
        4 * rows * cols * ff + 4 * span * ff * wide_cols,
        2 * (rows * cols + 2 * wide_cols * ff + span * wide_cols),
        in_specs=[ANY] + [HBM] * 3 + [ANY] * 9,
        out_specs=[VMEM, VMEM, ANY, ANY],
        out_shape=[
            small(groups, span, 2 * ff),
            small(span // CAP, groups * CAP, 2 * ff),
            small(span // 2, wide_cols),
            small(span // 2, wide_cols),
        ],
        scratch_shapes=[
            pltpu.VMEM((rows, cols), BF),
            pltpu.VMEM((2 * ff, cols), BF),
            pltpu.VMEM((wide_cols, 2 * ff), BF),
            pltpu.VMEM((3, groups, span, ff), F32),
            pltpu.VMEM((span, wide_cols), BF),
            pltpu.SemaphoreType.DMA((3 * pl.cdiv(cols, 3 * TILE // 2) + 12 + 4,)),
        ],
    )(g_rows, w_down, w_gate, w_up, *own, *side, *far)


def ring_part_kernel(near_ref, wg_ref, wu_ref, out_ref, w, staged, sem):
    rows, ring_cols = out_ref.shape
    loads = load_weights(wg_ref, wu_ref, w, 0, sem, 0)
    start_all(loads)
    wait_all(loads)
    left = near_ref[...].reshape(rows, w.shape[1])
    stores = []
    for c in range(ring_cols // TILE):
        window = slice(c * TILE, (c + 1) * TILE)
        staged[:, window] = contract_cols(left, w[window, :]).astype(BF)
        target = out_ref.at[:, window]
        stores.append(pltpu.make_async_copy(staged.at[:, window], target, sem.at[2 + c]))
        stores[-1].start()
    wait_all(stores)


def ring_part(near, w_gate, w_up, ring_cols):
    locs, depth, double = near.shape
    rows = locs * depth
    return call(
        ring_part_kernel,
        "ring_part",
        2 * rows * double * ring_cols,
        2 * ring_cols * (rows + double),
        in_specs=[VMEM, HBM, HBM],
        out_specs=ANY,
        out_shape=jax.ShapeDtypeStruct((rows, ring_cols), BF),
        scratch_shapes=[
            pltpu.VMEM((ring_cols, double), BF),
            pltpu.VMEM((rows, ring_cols), BF),
            pltpu.SemaphoreType.DMA((2 + ring_cols // TILE,)),
        ],
    )(near, w_gate, w_up)


def side_kernel(gu_ref, wg_ref, wu_ref, top_ref, bottom_ref, next_ref, prev_ref, own_ref, w, held, staged, sem):
    _, span, double = gu_ref.shape
    wide_cols = next_ref.shape[1]
    weights = load_weights(wg_ref, wu_ref, w, wg_ref.shape[0] - wide_cols, sem, 0)
    came = [
        pltpu.make_async_copy(top_ref, held.at[0], sem.at[2]),
        pltpu.make_async_copy(bottom_ref, held.at[1], sem.at[3]),
    ]
    start_all(weights)
    start_all(came)
    wait_all(weights)
    wait_all(came)
    left = jnp.concatenate([gu_ref[1], gu_ref[3], gu_ref[0]], axis=0)
    mid = span // 2
    stores = []
    for c in range(wide_cols // TILE):
        window = slice(c * TILE, (c + 1) * TILE)
        value = contract_cols(left, w[window, :])
        top = held[0, :, window].astype(F32)
        bottom = held[1, :, window].astype(F32)
        staged[0, :mid, window] = (value[:mid] + top).astype(BF)
        staged[0, mid:, window] = value[mid:span].astype(BF)
        staged[1, :mid, window] = value[span : span + mid].astype(BF)
        staged[1, mid:, window] = (value[span + mid : 2 * span] + bottom).astype(BF)
        staged[2, :, window] = value[2 * span :].astype(BF)
        for k, ref in enumerate((next_ref, prev_ref, own_ref)):
            copy = pltpu.make_async_copy(
                staged.at[k, :, window], ref.at[:, window], sem.at[4 + 3 * c + k]
            )
            copy.start()
            stores.append(copy)
    wait_all(stores)


def side_part(gu, w_gate, w_up, top, bottom):
    _, span, double = gu.shape
    wide_cols = top.shape[1]
    return call(
        side_kernel,
        "side_part",
        40 * (6 * span * double * wide_cols),
        40 * (2 * wide_cols * (4 * span + double)),
        in_specs=[VMEM, HBM, HBM, ANY, ANY],
        out_specs=[ANY] * 3,
        out_shape=[jax.ShapeDtypeStruct((span, wide_cols), BF)] * 3,
        scratch_shapes=[
            pltpu.VMEM((wide_cols, double), BF),
            pltpu.VMEM((2, span // 2, wide_cols), BF),
            pltpu.VMEM((3, span, wide_cols), BF),
            pltpu.SemaphoreType.DMA((4 + 3 * (wide_cols // TILE),)),
        ],
    )(gu, w_gate, w_up, top, bottom)


def sum_kernel(a_ref, b_ref, c_ref, out_ref, held, staged, sem):
    locs, _, cols = out_ref.shape
    steps = cols // TILE
    loads, stores = [], []
    for t in range(steps):
        window = slice(t * TILE, (t + 1) * TILE)
        for k, ref in enumerate((a_ref, b_ref, c_ref)):
            loads.append(
                pltpu.make_async_copy(ref.at[:, window], held.at[k, :, window], sem.at[4 * t + k])
            )
    start_all(loads)
    for t in range(steps):
        wait_all(loads[3 * t : 3 * t + 3])
        window = slice(t * TILE, (t + 1) * TILE)
        total = sum(held[k, :, window].astype(F32) for k in range(3))
        staged[:, :, window] = total.reshape(locs, CAP, TILE).astype(BF)
        source = staged.at[:, :, window]
        stores.append(pltpu.make_async_copy(source, out_ref.at[:, :, window], sem.at[4 * t + 3]))
        stores[-1].start()
    wait_all(stores)


def sum_blocks(a, b, c):
    rows, cols = a.shape
    return call(
        sum_kernel,
        "sum_blocks",
        2 * rows * cols,
        8 * rows * cols,
        in_specs=[HBM, ANY, ANY],
        out_specs=ANY,
        out_shape=jax.ShapeDtypeStruct((rows // CAP, CAP, cols), BF),
        scratch_shapes=[
            pltpu.VMEM((3, rows, cols), BF),
            pltpu.VMEM((rows // CAP, CAP, cols), BF),
            pltpu.SemaphoreType.DMA((4 * (cols // TILE),)),
        ],
    )(a, b, c)


def row_grads_kernel(gu_ref, own_ref, next_ref, top_ref, bottom_ref, prev_ref, gate_ref, up_ref, wide):
    groups, span, double = gu_ref.shape
    ff = double // 2
    locs = span // CAP

    @pl.when(pl.program_id(0) == 0)
    def _():
        zero = jnp.zeros((locs, CAP, ff), F32)
        for group in range(groups):
            both = gu_ref[group].astype(F32).reshape(locs, CAP, double)
            gate, up = both[:, :, :ff], both[:, :, ff:]
            low = jnp.concatenate([gate, zero, up, zero], axis=2)
            high = jnp.concatenate([zero, gate, zero, up], axis=2)
            both = jnp.concatenate([low, high], axis=1).reshape(2 * span, 4 * ff)
            wide[2 * span * group : 2 * span * (group + 1), :] = both.astype(BF)

    x = jnp.concatenate(
        [own_ref[...], next_ref[...], top_ref[...], bottom_ref[...], prev_ref[...]], axis=0
    )
    total = contract_rows(x, wide[...]).astype(BF)
    gate_ref[0] = total[:, :ff]
    gate_ref[1] = total[:, ff : 2 * ff]
    up_ref[0] = total[:, 2 * ff : 3 * ff]
    up_ref[1] = total[:, 3 * ff :]


def row_grads(gu, blocks, share):
    groups, span, double = gu.shape
    ff = double // 2
    rows = 2 * groups * span
    half = blocks[0].shape[1] - share
    out = jax.ShapeDtypeStruct((2, half, ff), BF)
    gate, up = call(
        row_grads_kernel,
        "row_grads",
        8 * rows * half * ff,
        2 * half * (rows + 4 * ff),
        grid=(half // TILE,),
        in_specs=[
            whole(gu.shape),
            *[pl.BlockSpec((b.shape[0], TILE), lambda j: (0, j)) for b in blocks],
        ],
        out_specs=[pl.BlockSpec((2, TILE, ff), lambda j: (0, j, 0))] * 2,
        out_shape=[out, out],
        scratch_shapes=[pltpu.VMEM((rows, 4 * ff), BF)],
    )(gu, *blocks)
    return gate.reshape(2 * half, ff), up.reshape(2 * half, ff)


def down_kernel(g_ref, *refs):
    outers, blocks = refs[:3], refs[3:8]
    out_ref, wide, held, sem = refs[8:]
    own, side, far = outers
    span, ff = own.shape
    locs = span // CAP
    unit = 2 * CAP
    step = pl.program_id(0)
    tile = g_ref.shape[1]
    share = held.shape[1]

    def spread(outer):
        rows = outer.reshape(locs, CAP, ff)
        zero = jnp.zeros_like(rows)
        low = jnp.concatenate([rows, zero], axis=2)
        high = jnp.concatenate([zero, rows], axis=2)
        return jnp.concatenate([low, high], axis=1)

    @pl.when(step == 0)
    def _():
        copies = []
        at = 0
        for k, ref in enumerate(blocks):
            source = ref.at[:, ref.shape[1] - share :]
            copies.append(
                pltpu.make_async_copy(source, held.at[at : at + ref.shape[0], :], sem.at[k])
            )
            at += ref.shape[0]
        start_all(copies)
        rows = []
        for k, outer in enumerate((own[...], side[:span], far[...], side[span:])):
            block = spread(outer).astype(BF)
            wide[:, k * unit : (k + 1) * unit, :] = block
            rows.append(block.reshape(2 * span, 2 * ff))
        wait_all(copies)
        total = contract_rows(jnp.concatenate(rows, axis=0), held[...]).astype(BF)
        out_ref[:, :share] = total[:ff]
        out_ref[:, share : 2 * share] = total[ff:]

    rows = wide[...].reshape(g_ref.shape[0], 2 * ff)
    total = contract_rows(rows, g_ref[...]).astype(BF)
    low = 2 * share + step * tile
    high = low + pl.num_programs(0) * tile
    out_ref[:, pl.ds(pl.multiple_of(low, 128), tile)] = total[:ff]
    out_ref[:, pl.ds(pl.multiple_of(high, 128), tile)] = total[ff:]


def down(outers, blocks, g_rows, share):
    rows, cols = g_rows.shape
    span, ff = outers[0].shape
    width = 2 * (cols + share)
    tile = TILE if cols % TILE == 0 else TILE // 2
    return call(
        down_kernel,
        "down",
        4 * rows * (cols + share) * ff,
        2 * (cols + share) * (rows + 2 * ff),
        grid=(cols // tile,),
        in_specs=[
            pl.BlockSpec((rows, tile), lambda j: (0, j)),
            *[whole(o.shape) for o in outers],
            *[ANY] * 5,
        ],
        out_specs=whole((ff, width)),
        out_shape=jax.ShapeDtypeStruct((ff, width), BF),
        scratch_shapes=[
            pltpu.VMEM((span // CAP, rows * CAP // span, 2 * ff), BF),
            pltpu.VMEM((rows, share), BF),
            pltpu.SemaphoreType.DMA((5,)),
        ],
    )(g_rows, *outers, *blocks)


def fold_kernel(in_ref, own_ref, top_ref, bottom_ref, side_ref):
    _, experts, depth, tile = in_ref.shape
    total = in_ref[0].astype(F32) + in_ref[1].astype(F32)
    for step in range(depth // CAP):
        part = total[:, step * CAP : (step + 1) * CAP, :].reshape(experts * CAP, tile).astype(BF)
        if step == 2:
            top_ref[...] = part[: experts * CAP // 2]
            bottom_ref[...] = part[experts * CAP // 2 :]
        elif step == 0:
            own_ref[...] = part
        else:
            side_ref[step // 2] = part


def fold(home):
    _, experts, depth, width = home.shape
    buf = experts * CAP
    tile = TILE
    return call(
        fold_kernel,
        "fold",
        experts * depth * width,
        6 * experts * depth * width,
        mib=20,
        grid=(width // tile,),
        in_specs=[pl.BlockSpec((2, experts, depth, tile), lambda j: (0, 0, 0, j))],
        out_specs=[
            pl.BlockSpec((buf, tile), lambda j: (0, j)),
            pl.BlockSpec((buf // 2, tile), lambda j: (0, j)),
            pl.BlockSpec((buf // 2, tile), lambda j: (0, j)),
            pl.BlockSpec((2, buf, tile), lambda j: (0, 0, j)),
        ],
        out_shape=[
            jax.ShapeDtypeStruct((buf, width), BF),
            jax.ShapeDtypeStruct((buf // 2, width), BF),
            jax.ShapeDtypeStruct((buf // 2, width), BF),
            jax.ShapeDtypeStruct((2, buf, width), BF),
        ],
    )(home)


def add_kernel(side_ref, top_ref, bottom_ref, next_ref, prev_ref):
    mid = top_ref.shape[0]
    next_ref[:mid] = (side_ref[0, :mid].astype(F32) + top_ref[...].astype(F32)).astype(BF)
    next_ref[mid:] = side_ref[0, mid:]
    prev_ref[:mid] = side_ref[1, :mid]
    prev_ref[mid:] = (side_ref[1, mid:].astype(F32) + bottom_ref[...].astype(F32)).astype(BF)


def add_far(side, top, bottom):
    _, buf, cols = side.shape
    return call(
        add_kernel,
        "add_far",
        buf * cols,
        10 * buf * cols,
        mib=20,
        in_specs=[VMEM] * 3,
        out_specs=[VMEM] * 2,
        out_shape=[jax.ShapeDtypeStruct((buf, cols), BF)] * 2,
    )(side, top, bottom)


def combine_kernel(table_ref, own_ref, left_ref, right_ref, wide_ref, out_ref, ring, wide, staged, sem):
    buf = table_ref.shape[0]
    ring_cols = ring.shape[1]
    locs, _, wide_cols = wide.shape
    loads, stores = [], []

    def add(source, target):
        loads.append(pltpu.make_async_copy(source, target, sem.at[len(loads)]))

    for k, ref in enumerate((own_ref, left_ref, right_ref)):
        add(ref, ring.at[k * buf : (k + 1) * buf, :])
    for first in range(0, wide_cols, TILE):
        window = slice(first, first + TILE)
        add(wide_ref.at[:, :, window], wide.at[:, :, window])
    start_all(loads)
    table = table_ref[...]
    twice = jnp.concatenate([table] * 2, axis=0)
    thrice = jnp.concatenate([table] * 3, axis=0)
    wait_all(loads[:3])
    for t in range((ring_cols + wide_cols) // TILE):
        window = slice(t * TILE, (t + 1) * TILE)
        first = t * TILE - ring_cols
        if first < 0:
            total = contract_rows(thrice, ring[:, window])
        else:
            loads[3 + first // TILE].wait()
            rows = wide[:, :, first : first + TILE].astype(F32).reshape(locs * CAP, TILE).astype(BF)
            total = contract_rows(twice, rows)
        staged[:, window] = total.astype(BF)
        target = out_ref.at[:, window]
        index = len(loads) + len(stores)
        stores.append(pltpu.make_async_copy(staged.at[:, window], target, sem.at[index]))
        stores[-1].start()
    wait_all(stores)


def combine(table, own, left, right, wide):
    buf, tok = table.shape
    ring_cols, wide_cols = left.shape[1], wide.shape[2]
    width = ring_cols + wide_cols
    return call(
        combine_kernel,
        "combine",
        2 * tok * buf * width,
        2 * width * (tok + 2 * buf),
        mib=24,
        in_specs=[VMEM, HBM, ANY, ANY, ANY],
        out_specs=ANY,
        out_shape=jax.ShapeDtypeStruct((tok, width), BF),
        scratch_shapes=[
            pltpu.VMEM((3 * buf, ring_cols), BF),
            pltpu.VMEM((wide.shape[0], CAP, wide_cols), BF),
            pltpu.VMEM((tok, width), BF),
            pltpu.SemaphoreType.DMA((3 + wide_cols // TILE + width // TILE,)),
        ],
    )(table, own, left, right, wide)


def over_loc(a):
    return lax.all_to_all(a, "loc", split_axis=0, concat_axis=0, tiled=True)


def shift(a, step):
    groups = lax.axis_size("grp")
    return lax.ppermute(a, "grp", [(i, (i + step) % groups) for i in range(groups)])


def ring_gather(own):
    mid = own.shape[0] // 2
    before, after = shift(own, 1), shift(own, -1)
    return [own, after, shift(before[:mid], 1), shift(after[mid:], -1), before]


def body(tokens, grad_out, expert_ids, route_weight, gate_weight, up_weight, down_weight):
    groups = lax.axis_size("grp")
    locs = lax.axis_size("loc")
    experts = locs // 2
    width = tokens.shape[1]
    buf = experts * CAP
    unit = 2 * CAP
    share = 768
    ring_cols = 2560
    wide_cols = width - ring_cols

    w_gate, w_up, w_down = gate_weight[0], up_weight[0], down_weight[0]

    table, pick, g_share, g_send = dispatch_gradient(
        expert_ids.T, route_weight.T, grad_out, experts, share
    )
    g_blocks = ring_gather(g_send)
    xg_send = dispatch_token(pick, g_share, tokens, experts)
    xg = over_loc(xg_send.reshape(locs, unit, xg_send.shape[3]))
    xg, *g_blocks = lax.optimization_barrier((xg, *g_blocks))
    blocks = ring_gather(xg.reshape(locs * unit, xg.shape[2]))
    g_out = regroup(g_blocks)
    g_rows = over_loc(g_out.reshape(locs, groups * unit, g_out.shape[3]))
    g_rows = g_rows.reshape(locs * groups * unit, g_out.shape[3])

    own, after, top, bottom, before = blocks
    *pre_own, outer_own = pre([own], w_gate, w_up, w_down, share)
    *pre_side, outer_side = pre([after, before], w_gate, w_up, w_down, share)
    *pre_far, outer_far = pre([top, bottom], w_gate, w_up, w_down, share)
    gu, near, far_top, far_bottom = hidden(
        g_rows, w_down, w_gate, w_up, pre_own, pre_side, pre_far, wide_cols
    )

    came_top, came_bottom = shift(far_top, 1), shift(far_bottom, -1)
    part_ring = ring_part(near, w_gate, w_up, ring_cols)
    part_ring, gu = lax.optimization_barrier((part_ring, gu))
    home_ring = over_loc(part_ring.reshape(locs, groups * CAP, ring_cols))
    part_next, part_prev, part_own = side_part(gu, w_gate, w_up, came_top, came_bottom)
    from_before, from_after = shift(part_next, 1), shift(part_prev, -1)

    outers = (outer_own, outer_side, outer_far)
    part_own, gu, outers = lax.optimization_barrier((part_own, gu, outers))
    gate_grad, up_grad = row_grads(gu, blocks, share)
    down_grad = down(outers, blocks, g_rows, share)
    part_own, gate_grad, up_grad, down_grad = lax.optimization_barrier(
        (part_own, gate_grad, up_grad, down_grad)
    )
    fold_own, fold_top, fold_bottom, fold_side = fold(
        home_ring.reshape(2, experts, groups * CAP, ring_cols)
    )
    part_own, fold_top, fold_bottom = lax.optimization_barrier((part_own, fold_top, fold_bottom))
    home_wide = over_loc(sum_blocks(part_own, from_before, from_after))
    fold_next, fold_prev = add_far(fold_side, shift(fold_top, 1), shift(fold_bottom, -1))
    tokens_grad = combine(table, fold_own, shift(fold_next, 1), shift(fold_prev, -1), home_wide)
    return (tokens_grad, gate_grad[None], up_grad[None], down_grad[None])


def solution(mesh):
    in_specs = (
        P(("grp", "loc"), None),
        P(("grp", "loc"), None),
        P(("grp", "loc"), None),
        P(("grp", "loc"), None),
        P("loc", None, "grp"),
        P("loc", None, "grp"),
        P("loc", "grp", None),
    )
    out_specs = (
        P(("grp", "loc"), None),
        P("loc", None, "grp"),
        P("loc", None, "grp"),
        P("loc", "grp", None),
    )
    return jax.shard_map(body, mesh=mesh, in_specs=in_specs, out_specs=out_specs, check_vma=False)
```

```python
import functools

import jax
import jax.numpy as jnp
from jax import lax
from jax.experimental import pallas as pl
from jax.experimental.pallas import tpu as pltpu
from jax.sharding import PartitionSpec as P

CAP = 4
BF = jnp.bfloat16
F32 = jnp.float32
TILE = 512
ANY = pl.BlockSpec(memory_space=pl.ANY)
VMEM = pl.BlockSpec(memory_space=pltpu.VMEM)
HBM = pl.BlockSpec(memory_space=pltpu.HBM)


def contract_rows(left, right):
    return lax.dot_general(left, right, (((0,), (0,)), ((), ())), preferred_element_type=F32)


def contract_cols(left, right):
    return lax.dot_general(left, right, (((1,), (1,)), ((), ())), preferred_element_type=F32)


def whole(shape):
    return pl.BlockSpec(shape, lambda *_: (0,) * len(shape))


def call(kernel, name, flops, nbytes, mib=56, **kwargs):
    return pl.pallas_call(
        kernel,
        name=name,
        compiler_params=pltpu.CompilerParams(vmem_limit_bytes=mib << 20),
        cost_estimate=pl.CostEstimate(flops=flops, bytes_accessed=nbytes, transcendentals=0),
        **kwargs,
    )


def dispatch_kernel(ids_ref, w_ref, g_ref, t_ref, table_ref, ring_ref, out_ref, held, tokens, staged, sem):
    load = pltpu.make_async_copy(g_ref, held, sem.at[0])
    load.start()
    load_tokens = pltpu.make_async_copy(t_ref, tokens, sem.at[1])
    load_tokens.start()
    topk, tok = ids_ref.shape
    buf = table_ref.shape[0]
    unit = 2 * CAP
    experts = out_ref.shape[1]
    cols = ring_ref.shape[1]
    half = tokens.shape[1] // 2
    share = half - cols

    def tables(count, per_expert):
        slot_row = lax.broadcasted_iota(jnp.int32, (count, tok), 0)
        expert = lax.div(slot_row, per_expert)
        weights = w_ref[...].astype(F32)
        chosen = jnp.zeros((count, tok), F32)
        weight = jnp.zeros((count, tok), F32)
        for k in range(topk):
            hit = ids_ref[k : k + 1, :] == expert
            chosen = jnp.where(hit, 1.0, chosen)
            weight = jnp.where(hit, weights[k : k + 1, :], weight)
        before = lax.broadcasted_iota(jnp.int32, (tok, tok), 0)
        after = lax.broadcasted_iota(jnp.int32, (tok, tok), 1)
        earlier = jnp.where(before < after, 1.0, 0.0).astype(BF)
        slot = jnp.dot(chosen.astype(BF), earlier, preferred_element_type=F32)
        mine = (chosen > 0.5) & (slot == lax.rem(slot_row, CAP).astype(F32))
        return jnp.where(mine, 1.0, 0.0), jnp.where(mine, weight, 0.0), slot_row

    table_ref[...] = tables(buf, CAP)[0].astype(BF)
    table, weighted, slot_row = tables(2 * buf, unit)
    low = lax.rem(slot_row, unit) < CAP
    pick = jnp.concatenate(
        [jnp.where(low, table, 0.0).astype(BF), jnp.where(low, 0.0, table).astype(BF)], axis=1
    )
    both = jnp.concatenate(
        [jnp.where(low, weighted, 0.0).astype(BF), jnp.where(low, 0.0, weighted).astype(BF)], axis=1
    )
    load.wait()

    def rows(left, source, first, second, count):
        parts = jnp.concatenate(
            [source[:, first : first + count], source[:, second : second + count]], axis=0
        )
        return jnp.dot(left, parts, preferred_element_type=F32).astype(BF)

    staged[:, :, half:] = rows(both, held, 0, share, share).reshape(experts, unit, share)
    part = TILE // 2
    for first in range(0, cols, part):
        start = 2 * share + first
        ring_ref[:, first : first + part] = rows(both, held, start, start + cols, part)
    load_tokens.wait()
    for first in range(0, half, TILE):
        value = rows(pick, tokens, first, half + first, TILE)
        staged[:, :, first : first + TILE] = value.reshape(experts, unit, TILE)
    stores = [pltpu.make_async_copy(staged, out_ref.at[h], sem.at[2 + h]) for h in range(2)]
    for store in stores:
        store.start()
    for store in stores:
        store.wait()


def dispatch(ids, weights, grad_out, tokens, experts, share):
    tok, width = grad_out.shape
    buf = experts * CAP
    unit = 2 * CAP
    half = width // 2
    small = lambda *shape: jax.ShapeDtypeStruct(shape, BF)
    return call(
        dispatch_kernel,
        "dispatch",
        8 * tok * buf * width,
        2 * width * (2 * tok + 3 * buf),
        in_specs=[VMEM, VMEM, ANY, ANY],
        out_specs=[VMEM, VMEM, ANY],
        out_shape=[
            small(buf, tok),
            small(2 * buf, half - share),
            small(2, experts, unit, half + share),
        ],
        scratch_shapes=[
            pltpu.VMEM((tok, width), BF),
            pltpu.VMEM((tok, width), BF),
            pltpu.VMEM((experts, unit, half + share), BF),
            pltpu.SemaphoreType.DMA((4,)),
        ],
    )(ids, weights, grad_out, tokens)


def regroup_kernel(own_ref, next_ref, top_ref, bottom_ref, prev_ref, out_ref, held, sem):
    experts, unit, _ = own_ref.shape
    parts = 4
    size = experts // parts
    loads, stores = [], []
    for p in range(parts):
        window = slice(p * size, (p + 1) * size)
        if p < parts // 2:
            far = top_ref.at[window]
        else:
            far = bottom_ref.at[p * size - experts // 2 : (p + 1) * size - experts // 2]
        sources = [own_ref.at[window], next_ref.at[window], far, prev_ref.at[window]]
        for k, source in enumerate(sources):
            target = held.at[window, k * unit : (k + 1) * unit, :]
            loads.append(pltpu.make_async_copy(source, target, sem.at[p * 4 + k]))
            loads[-1].start()
    for p in range(parts):
        window = slice(p * size, (p + 1) * size)
        for k in range(4):
            loads[p * 4 + k].wait()
        for h in range(2):
            index = parts * 4 + 2 * p + h
            stores.append(pltpu.make_async_copy(held.at[window], out_ref.at[h, window], sem.at[index]))
            stores[-1].start()
    for store in stores:
        store.wait()


def regroup(blocks):
    count, cols = blocks[0].shape
    unit = 2 * CAP
    experts = count // unit
    return call(
        regroup_kernel,
        "regroup",
        0,
        24 * count * cols,
        in_specs=[ANY] * 5,
        out_specs=ANY,
        out_shape=jax.ShapeDtypeStruct((2, experts, 4 * unit, cols), BF),
        scratch_shapes=[
            pltpu.VMEM((experts, 4 * unit, cols), BF),
            pltpu.SemaphoreType.DMA((24,)),
        ],
    )(*[b.reshape(b.shape[0] // unit, unit, cols) for b in blocks])


def pre_copies(x_refs, wg_ref, wu_ref, wd_ref, x, w, d, sem):
    cols = x.shape[1]
    ff = w.shape[2] // 4
    share = d.shape[1]
    half = cols - share
    steps = half // TILE
    copies = [[] for _ in range(steps + 1)]
    index = 0

    def add(step, source, target):
        nonlocal index
        copies[step].append(pltpu.make_async_copy(source, target, sem.at[index]))
        index += 1

    for t in range(steps + 1):
        window = slice(t * TILE, (t + 1) * TILE) if t < steps else slice(half, cols)
        at = 0
        for ref in x_refs:
            add(t, ref.at[:, window], x.at[at : at + ref.shape[0], window])
            at += ref.shape[0]
        if t < steps:
            for k, ref in enumerate((wg_ref, wu_ref)):
                for h in range(2):
                    lane = (2 * k + h) * ff
                    source = ref.at[h * half + t * TILE : h * half + (t + 1) * TILE, :]
                    add(t, source, w.at[t, :, lane : lane + ff])
        else:
            for h in range(2):
                source = wd_ref.at[:, h * share : (h + 1) * share]
                add(t, source, d.at[h * ff : (h + 1) * ff, :])
    return copies


def pre_values(copies, x, w, d, acc):
    rows, cols = x.shape
    ff = w.shape[2] // 4
    half = cols - d.shape[1]
    steps = half // TILE
    for t in range(steps):
        wait_all(copies[t])
        value = jnp.dot(x[:, t * TILE : (t + 1) * TILE], w[t], preferred_element_type=F32)
        if t == 0:
            acc[...] = value
        else:
            acc[...] += value
    wait_all(copies[steps])

    def fold_halves(value):
        value = value.reshape(rows // (2 * CAP), 2 * CAP, 2 * ff)
        return (value[:, :CAP, :ff] + value[:, CAP:, ff:]).reshape(rows // 2, ff)

    part = fold_halves(contract_cols(x[:, half:], d[...]))
    gate = fold_halves(acc[:, : 2 * ff])
    up = fold_halves(acc[:, 2 * ff :])
    sig = 1.0 / (1.0 + jnp.exp(-gate))
    swish = gate * sig
    return up * sig * (1.0 + gate * (1.0 - sig)), swish, part, swish * up


def pre_kernel(count, *refs):
    wg_ref, wu_ref, wd_ref = refs[count : count + 3]
    out_refs = refs[count + 3 : count + 7]
    x, w, d, acc, sem = refs[count + 7 :]
    copies = pre_copies(refs[:count], wg_ref, wu_ref, wd_ref, x, w, d, sem)
    for group in copies:
        start_all(group)
    for ref, value in zip(out_refs, pre_values(copies, x, w, d, acc)):
        ref[...] = value


def pre_scratch(rows, cols, share, ff, blocks):
    steps = (cols - share) // TILE
    return [
        pltpu.VMEM((rows, cols), BF),
        pltpu.VMEM((steps, TILE, 4 * ff), BF),
        pltpu.VMEM((2 * ff, share), BF),
        pltpu.VMEM((rows, 4 * ff), F32),
        pltpu.SemaphoreType.DMA(((blocks + 4) * steps + blocks + 2,)),
    ]


def pre(blocks, w_gate, w_up, w_down, share):
    cols = blocks[0].shape[1]
    rows = sum(b.shape[0] for b in blocks)
    ff = w_gate.shape[1]
    return call(
        functools.partial(pre_kernel, len(blocks)),
        "pre",
        200 * (8 * rows * cols * ff),
        200 * (2 * cols * (rows + 4 * ff)),
        in_specs=[ANY] * len(blocks) + [HBM] * 3,
        out_specs=[VMEM] * 4,
        out_shape=[jax.ShapeDtypeStruct((rows // 2, ff), F32)] * 4,
        scratch_shapes=pre_scratch(rows, cols, share, ff, len(blocks)),
    )(*blocks, w_gate, w_up, w_down)


def load_weights(wg_ref, wu_ref, w, first, sem, index):
    count = w.shape[0]
    ff = wg_ref.shape[1]
    copies = []
    for k, ref in enumerate((wg_ref, wu_ref)):
        source = ref.at[first : first + count, :]
        target = w.at[:, k * ff : (k + 1) * ff]
        copies.append(pltpu.make_async_copy(source, target, sem.at[index + k]))
    return copies


def start_all(copies):
    for copy in copies:
        copy.start()


def wait_all(copies):
    for copy in copies:
        copy.wait()


def hidden_kernel(
    g_ref, wd_ref, wg_ref, wu_ref, *refs
):
    own, side, far_rows = refs[0:3], refs[3:6], refs[6:8]
    gu_ref, near_ref, top_ref, bottom_ref, outer_ref, g, d, w, small, staged, sem = refs[8:19]
    far_x, far_w, far_d, far_acc, far_sem = refs[19:]
    groups, span, double = gu_ref.shape
    ff = double // 2
    locs = span // CAP
    unit = 2 * CAP
    cols = g.shape[1]
    wide_cols = top_ref.shape[1]
    first_col = wd_ref.shape[1] - 2 * cols
    tile = 3 * TILE // 2
    windows = [slice(at, min(at + tile, cols)) for at in range(0, cols, tile)]
    steps = len(windows)
    loads = []
    for t, window in enumerate(windows):
        loads.append(pltpu.make_async_copy(g_ref.at[:, window], g.at[:, window], sem.at[3 * t]))
        for h in range(2):
            start = first_col + h * cols + window.start
            source = wd_ref.at[:, start : start + window.stop - window.start]
            target = d.at[h * ff : (h + 1) * ff, window]
            loads.append(pltpu.make_async_copy(source, target, sem.at[3 * t + 1 + h]))
    more = []
    index = 3 * steps
    for k in range(3):
        places = [(own[k], 0), (side[k].at[:span], 1), (side[k].at[span:], 3)]
        for source, group in places:
            more.append(pltpu.make_async_copy(source, small.at[k, group], sem.at[index]))
            index += 1
    weights = load_weights(wg_ref, wu_ref, w, wg_ref.shape[0] - wide_cols, sem, index)
    far_copies = pre_copies(far_rows, wg_ref, wu_ref, wd_ref, far_x, far_w, far_d, far_sem)
    for group in far_copies:
        start_all(group)
    start_all(loads)
    start_all(more)
    start_all(weights)
    slope, swish, part, outer_ref[...] = pre_values(far_copies, far_x, far_w, far_d, far_acc)
    total = None
    for t, window in enumerate(windows):
        wait_all(loads[3 * t : 3 * t + 3])
        value = contract_cols(g[:, window], d[:, window])
        total = value if total is None else total + value
    wait_all(more)
    halves = total.reshape(locs, groups * unit, double)
    for group in range(groups):
        first = group * unit
        hidden = (
            halves[:, first : first + CAP, :ff] + halves[:, first + CAP : first + unit, ff:]
        ).reshape(span, ff) + (part if group == 2 else small[2, group])
        gate = hidden * (slope if group == 2 else small[0, group])
        up = hidden * (swish if group == 2 else small[1, group])
        both = jnp.concatenate([gate, up], axis=1)
        gu_ref[group] = both.astype(BF)
        near_ref[:, group * CAP : (group + 1) * CAP, :] = both.reshape(locs, CAP, double).astype(BF)
    wait_all(weights)
    staged[...] = contract_cols(gu_ref[2], w[...]).astype(BF)
    stores = [
        pltpu.make_async_copy(staged.at[: span // 2], top_ref, sem.at[index + 2]),
        pltpu.make_async_copy(staged.at[span // 2 :], bottom_ref, sem.at[index + 3]),
    ]
    start_all(stores)
    wait_all(stores)


def hidden(g_rows, w_down, w_gate, w_up, own, side, far, share, wide_cols):
    rows, cols = g_rows.shape
    span, ff = own[0].shape
    groups = rows // 2 // span
    small = lambda *shape: jax.ShapeDtypeStruct(shape, BF)
    return call(
        hidden_kernel,
        "hidden",
        4 * rows * cols * ff + 4 * span * ff * wide_cols,
        2 * (rows * cols + 2 * wide_cols * ff + span * wide_cols),
        in_specs=[ANY] + [HBM] * 3 + [ANY] * 8,
        out_specs=[VMEM, VMEM, ANY, ANY, VMEM],
        out_shape=[
            small(groups, span, 2 * ff),
            small(span // CAP, groups * CAP, 2 * ff),
            small(span // 2, wide_cols),
            small(span // 2, wide_cols),
            jax.ShapeDtypeStruct((span, ff), F32),
        ],
        scratch_shapes=[
            pltpu.VMEM((rows, cols), BF),
            pltpu.VMEM((2 * ff, cols), BF),
            pltpu.VMEM((wide_cols, 2 * ff), BF),
            pltpu.VMEM((3, groups, span, ff), F32),
            pltpu.VMEM((span, wide_cols), BF),
            pltpu.SemaphoreType.DMA((3 * pl.cdiv(cols, 3 * TILE // 2) + 9 + 4,)),
            *pre_scratch(2 * span, far[0].shape[1], share, ff, 2),
        ],
    )(g_rows, w_down, w_gate, w_up, *own, *side, *far)


def ring_part_kernel(near_ref, wg_ref, wu_ref, out_ref, w, staged, sem):
    rows, ring_cols = out_ref.shape
    loads = load_weights(wg_ref, wu_ref, w, 0, sem, 0)
    start_all(loads)
    wait_all(loads)
    left = near_ref[...].reshape(rows, w.shape[1])
    stores = []
    for c in range(ring_cols // TILE):
        window = slice(c * TILE, (c + 1) * TILE)
        staged[:, window] = contract_cols(left, w[window, :]).astype(BF)
        target = out_ref.at[:, window]
        stores.append(pltpu.make_async_copy(staged.at[:, window], target, sem.at[2 + c]))
        stores[-1].start()
    wait_all(stores)


def ring_part(near, w_gate, w_up, ring_cols):
    locs, depth, double = near.shape
    rows = locs * depth
    return call(
        ring_part_kernel,
        "ring_part",
        2 * rows * double * ring_cols,
        2 * ring_cols * (rows + double),
        in_specs=[VMEM, HBM, HBM],
        out_specs=ANY,
        out_shape=jax.ShapeDtypeStruct((rows, ring_cols), BF),
        scratch_shapes=[
            pltpu.VMEM((ring_cols, double), BF),
            pltpu.VMEM((rows, ring_cols), BF),
            pltpu.SemaphoreType.DMA((2 + ring_cols // TILE,)),
        ],
    )(near, w_gate, w_up)


def side_kernel(gu_ref, wg_ref, wu_ref, top_ref, bottom_ref, next_ref, prev_ref, own_ref, w, held, staged, sem):
    _, span, double = gu_ref.shape
    wide_cols = next_ref.shape[1]
    weights = load_weights(wg_ref, wu_ref, w, wg_ref.shape[0] - wide_cols, sem, 0)
    came = [
        pltpu.make_async_copy(top_ref, held.at[0], sem.at[2]),
        pltpu.make_async_copy(bottom_ref, held.at[1], sem.at[3]),
    ]
    start_all(weights)
    start_all(came)
    wait_all(weights)
    wait_all(came)
    left = jnp.concatenate([gu_ref[1], gu_ref[3], gu_ref[0]], axis=0)
    mid = span // 2
    stores = []
    for c in range(wide_cols // TILE):
        window = slice(c * TILE, (c + 1) * TILE)
        value = contract_cols(left, w[window, :])
        top = held[0, :, window].astype(F32)
        bottom = held[1, :, window].astype(F32)
        staged[0, :mid, window] = (value[:mid] + top).astype(BF)
        staged[0, mid:, window] = value[mid:span].astype(BF)
        staged[1, :mid, window] = value[span : span + mid].astype(BF)
        staged[1, mid:, window] = (value[span + mid : 2 * span] + bottom).astype(BF)
        staged[2, :, window] = value[2 * span :].astype(BF)
        for k, ref in enumerate((next_ref, prev_ref, own_ref)):
            copy = pltpu.make_async_copy(
                staged.at[k, :, window], ref.at[:, window], sem.at[4 + 3 * c + k]
            )
            copy.start()
            stores.append(copy)
    wait_all(stores)


def side_part(gu, w_gate, w_up, top, bottom):
    _, span, double = gu.shape
    wide_cols = top.shape[1]
    return call(
        side_kernel,
        "side_part",
        40 * (6 * span * double * wide_cols),
        40 * (2 * wide_cols * (4 * span + double)),
        in_specs=[VMEM, HBM, HBM, ANY, ANY],
        out_specs=[ANY] * 3,
        out_shape=[jax.ShapeDtypeStruct((span, wide_cols), BF)] * 3,
        scratch_shapes=[
            pltpu.VMEM((wide_cols, double), BF),
            pltpu.VMEM((2, span // 2, wide_cols), BF),
            pltpu.VMEM((3, span, wide_cols), BF),
            pltpu.SemaphoreType.DMA((4 + 3 * (wide_cols // TILE),)),
        ],
    )(gu, w_gate, w_up, top, bottom)


def sum_kernel(a_ref, b_ref, c_ref, out_ref, held, staged, sem):
    locs, _, cols = out_ref.shape
    steps = cols // TILE
    loads, stores = [], []
    for t in range(steps):
        window = slice(t * TILE, (t + 1) * TILE)
        for k, ref in enumerate((a_ref, b_ref, c_ref)):
            loads.append(
                pltpu.make_async_copy(ref.at[:, window], held.at[k, :, window], sem.at[4 * t + k])
            )
    start_all(loads)
    for t in range(steps):
        wait_all(loads[3 * t : 3 * t + 3])
        window = slice(t * TILE, (t + 1) * TILE)
        total = sum(held[k, :, window].astype(F32) for k in range(3))
        staged[:, :, window] = total.reshape(locs, CAP, TILE).astype(BF)
        source = staged.at[:, :, window]
        stores.append(pltpu.make_async_copy(source, out_ref.at[:, :, window], sem.at[4 * t + 3]))
        stores[-1].start()
    wait_all(stores)


def sum_blocks(a, b, c):
    rows, cols = a.shape
    return call(
        sum_kernel,
        "sum_blocks",
        2 * rows * cols,
        8 * rows * cols,
        in_specs=[HBM, ANY, ANY],
        out_specs=ANY,
        out_shape=jax.ShapeDtypeStruct((rows // CAP, CAP, cols), BF),
        scratch_shapes=[
            pltpu.VMEM((3, rows, cols), BF),
            pltpu.VMEM((rows // CAP, CAP, cols), BF),
            pltpu.SemaphoreType.DMA((4 * (cols // TILE),)),
        ],
    )(a, b, c)


def row_grads_kernel(gu_ref, own_ref, next_ref, top_ref, bottom_ref, prev_ref, gate_ref, up_ref, wide):
    groups, span, double = gu_ref.shape
    ff = double // 2
    locs = span // CAP

    @pl.when(pl.program_id(0) == 0)
    def _():
        zero = jnp.zeros((locs, CAP, ff), F32)
        for group in range(groups):
            both = gu_ref[group].astype(F32).reshape(locs, CAP, double)
            gate, up = both[:, :, :ff], both[:, :, ff:]
            low = jnp.concatenate([gate, zero, up, zero], axis=2)
            high = jnp.concatenate([zero, gate, zero, up], axis=2)
            both = jnp.concatenate([low, high], axis=1).reshape(2 * span, 4 * ff)
            wide[2 * span * group : 2 * span * (group + 1), :] = both.astype(BF)

    x = jnp.concatenate(
        [own_ref[...], next_ref[...], top_ref[...], bottom_ref[...], prev_ref[...]], axis=0
    )
    total = contract_rows(x, wide[...]).astype(BF)
    gate_ref[0] = total[:, :ff]
    gate_ref[1] = total[:, ff : 2 * ff]
    up_ref[0] = total[:, 2 * ff : 3 * ff]
    up_ref[1] = total[:, 3 * ff :]


def row_grads(gu, blocks, share):
    groups, span, double = gu.shape
    ff = double // 2
    rows = 2 * groups * span
    half = blocks[0].shape[1] - share
    out = jax.ShapeDtypeStruct((2, half, ff), BF)
    gate, up = call(
        row_grads_kernel,
        "row_grads",
        8 * rows * half * ff,
        2 * half * (rows + 4 * ff),
        grid=(half // TILE,),
        in_specs=[
            whole(gu.shape),
            *[pl.BlockSpec((b.shape[0], TILE), lambda j: (0, j)) for b in blocks],
        ],
        out_specs=[pl.BlockSpec((2, TILE, ff), lambda j: (0, j, 0))] * 2,
        out_shape=[out, out],
        scratch_shapes=[pltpu.VMEM((rows, 4 * ff), BF)],
    )(gu, *blocks)
    return gate.reshape(2 * half, ff), up.reshape(2 * half, ff)


def down_kernel(g_ref, *refs):
    outers, blocks = refs[:3], refs[3:8]
    out_ref, wide, held, sem = refs[8:]
    own, side, far = outers
    span, ff = own.shape
    locs = span // CAP
    unit = 2 * CAP
    step = pl.program_id(0)
    tile = g_ref.shape[1]
    share = held.shape[1]

    def spread(outer):
        rows = outer.reshape(locs, CAP, ff)
        zero = jnp.zeros_like(rows)
        low = jnp.concatenate([rows, zero], axis=2)
        high = jnp.concatenate([zero, rows], axis=2)
        return jnp.concatenate([low, high], axis=1)

    @pl.when(step == 0)
    def _():
        copies = []
        at = 0
        for k, ref in enumerate(blocks):
            source = ref.at[:, ref.shape[1] - share :]
            copies.append(
                pltpu.make_async_copy(source, held.at[at : at + ref.shape[0], :], sem.at[k])
            )
            at += ref.shape[0]
        start_all(copies)
        rows = []
        for k, outer in enumerate((own[...], side[:span], far[...], side[span:])):
            block = spread(outer).astype(BF)
            wide[:, k * unit : (k + 1) * unit, :] = block
            rows.append(block.reshape(2 * span, 2 * ff))
        wait_all(copies)
        total = contract_rows(jnp.concatenate(rows, axis=0), held[...]).astype(BF)
        out_ref[:, :share] = total[:ff]
        out_ref[:, share : 2 * share] = total[ff:]

    rows = wide[...].reshape(g_ref.shape[0], 2 * ff)
    total = contract_rows(rows, g_ref[...]).astype(BF)
    low = 2 * share + step * tile
    high = low + pl.num_programs(0) * tile
    out_ref[:, pl.ds(pl.multiple_of(low, 128), tile)] = total[:ff]
    out_ref[:, pl.ds(pl.multiple_of(high, 128), tile)] = total[ff:]


def down(outers, blocks, g_rows, share):
    rows, cols = g_rows.shape
    span, ff = outers[0].shape
    width = 2 * (cols + share)
    tile = TILE if cols % TILE == 0 else TILE // 2
    return call(
        down_kernel,
        "down",
        4 * rows * (cols + share) * ff,
        2 * (cols + share) * (rows + 2 * ff),
        grid=(cols // tile,),
        in_specs=[
            pl.BlockSpec((rows, tile), lambda j: (0, j)),
            *[whole(o.shape) for o in outers],
            *[ANY] * 5,
        ],
        out_specs=whole((ff, width)),
        out_shape=jax.ShapeDtypeStruct((ff, width), BF),
        scratch_shapes=[
            pltpu.VMEM((span // CAP, rows * CAP // span, 2 * ff), BF),
            pltpu.VMEM((rows, share), BF),
            pltpu.SemaphoreType.DMA((5,)),
        ],
    )(g_rows, *outers, *blocks)


def fold_kernel(in_ref, own_ref, top_ref, bottom_ref, side_ref):
    _, experts, depth, tile = in_ref.shape
    total = in_ref[0].astype(F32) + in_ref[1].astype(F32)
    for step in range(depth // CAP):
        part = total[:, step * CAP : (step + 1) * CAP, :].reshape(experts * CAP, tile).astype(BF)
        if step == 2:
            top_ref[...] = part[: experts * CAP // 2]
            bottom_ref[...] = part[experts * CAP // 2 :]
        elif step == 0:
            own_ref[...] = part
        else:
            side_ref[step // 2] = part


def fold(home):
    _, experts, depth, width = home.shape
    buf = experts * CAP
    tile = TILE
    return call(
        fold_kernel,
        "fold",
        experts * depth * width,
        6 * experts * depth * width,
        mib=20,
        grid=(width // tile,),
        in_specs=[pl.BlockSpec((2, experts, depth, tile), lambda j: (0, 0, 0, j))],
        out_specs=[
            pl.BlockSpec((buf, tile), lambda j: (0, j)),
            pl.BlockSpec((buf // 2, tile), lambda j: (0, j)),
            pl.BlockSpec((buf // 2, tile), lambda j: (0, j)),
            pl.BlockSpec((2, buf, tile), lambda j: (0, 0, j)),
        ],
        out_shape=[
            jax.ShapeDtypeStruct((buf, width), BF),
            jax.ShapeDtypeStruct((buf // 2, width), BF),
            jax.ShapeDtypeStruct((buf // 2, width), BF),
            jax.ShapeDtypeStruct((2, buf, width), BF),
        ],
    )(home)


def add_kernel(side_ref, top_ref, bottom_ref, next_ref, prev_ref):
    mid = top_ref.shape[0]
    next_ref[:mid] = (side_ref[0, :mid].astype(F32) + top_ref[...].astype(F32)).astype(BF)
    next_ref[mid:] = side_ref[0, mid:]
    prev_ref[:mid] = side_ref[1, :mid]
    prev_ref[mid:] = (side_ref[1, mid:].astype(F32) + bottom_ref[...].astype(F32)).astype(BF)


def add_far(side, top, bottom):
    _, buf, cols = side.shape
    return call(
        add_kernel,
        "add_far",
        buf * cols,
        10 * buf * cols,
        mib=20,
        in_specs=[VMEM] * 3,
        out_specs=[VMEM] * 2,
        out_shape=[jax.ShapeDtypeStruct((buf, cols), BF)] * 2,
    )(side, top, bottom)


def combine_kernel(table_ref, own_ref, left_ref, right_ref, wide_ref, out_ref, ring, wide, staged, sem):
    buf = table_ref.shape[0]
    ring_cols = ring.shape[1]
    locs, _, wide_cols = wide.shape
    loads, stores = [], []

    def add(source, target):
        loads.append(pltpu.make_async_copy(source, target, sem.at[len(loads)]))

    for k, ref in enumerate((own_ref, left_ref, right_ref)):
        add(ref, ring.at[k * buf : (k + 1) * buf, :])
    for first in range(0, wide_cols, TILE):
        window = slice(first, first + TILE)
        add(wide_ref.at[:, :, window], wide.at[:, :, window])
    start_all(loads)
    table = table_ref[...]
    twice = jnp.concatenate([table] * 2, axis=0)
    thrice = jnp.concatenate([table] * 3, axis=0)
    wait_all(loads[:3])
    for t in range((ring_cols + wide_cols) // TILE):
        window = slice(t * TILE, (t + 1) * TILE)
        first = t * TILE - ring_cols
        if first < 0:
            total = contract_rows(thrice, ring[:, window])
        else:
            loads[3 + first // TILE].wait()
            rows = wide[:, :, first : first + TILE].astype(F32).reshape(locs * CAP, TILE).astype(BF)
            total = contract_rows(twice, rows)
        staged[:, window] = total.astype(BF)
        target = out_ref.at[:, window]
        index = len(loads) + len(stores)
        stores.append(pltpu.make_async_copy(staged.at[:, window], target, sem.at[index]))
        stores[-1].start()
    wait_all(stores)


def combine(table, own, left, right, wide):
    buf, tok = table.shape
    ring_cols, wide_cols = left.shape[1], wide.shape[2]
    width = ring_cols + wide_cols
    return call(
        combine_kernel,
        "combine",
        2 * tok * buf * width,
        2 * width * (tok + 2 * buf),
        mib=24,
        in_specs=[VMEM, HBM, ANY, ANY, ANY],
        out_specs=ANY,
        out_shape=jax.ShapeDtypeStruct((tok, width), BF),
        scratch_shapes=[
            pltpu.VMEM((3 * buf, ring_cols), BF),
            pltpu.VMEM((wide.shape[0], CAP, wide_cols), BF),
            pltpu.VMEM((tok, width), BF),
            pltpu.SemaphoreType.DMA((3 + wide_cols // TILE + width // TILE,)),
        ],
    )(table, own, left, right, wide)


def over_loc(a):
    return lax.all_to_all(a, "loc", split_axis=0, concat_axis=0, tiled=True)


def shift(a, step):
    groups = lax.axis_size("grp")
    return lax.ppermute(a, "grp", [(i, (i + step) % groups) for i in range(groups)])


def ring_gather(own):
    mid = own.shape[0] // 2
    before, after = shift(own, 1), shift(own, -1)
    return [own, after, shift(before[:mid], 1), shift(after[mid:], -1), before]


def body(tokens, grad_out, expert_ids, route_weight, gate_weight, up_weight, down_weight):
    groups = lax.axis_size("grp")
    locs = lax.axis_size("loc")
    experts = locs // 2
    width = tokens.shape[1]
    buf = experts * CAP
    unit = 2 * CAP
    share = 768
    ring_cols = 2560
    wide_cols = width - ring_cols

    w_gate, w_up, w_down = gate_weight[0], up_weight[0], down_weight[0]

    table, g_send, xg_send = dispatch(
        expert_ids.T, route_weight.T, grad_out, tokens, experts, share
    )
    g_blocks = ring_gather(g_send)
    xg = over_loc(xg_send.reshape(locs, unit, xg_send.shape[3]))
    xg, *g_blocks = lax.optimization_barrier((xg, *g_blocks))
    blocks = ring_gather(xg.reshape(locs * unit, xg.shape[2]))
    g_out = regroup(g_blocks)
    g_rows = over_loc(g_out.reshape(locs, groups * unit, g_out.shape[3]))
    g_rows = g_rows.reshape(locs * groups * unit, g_out.shape[3])

    own, after, top, bottom, before = blocks
    *pre_own, outer_own = pre([own], w_gate, w_up, w_down, share)
    *pre_side, outer_side = pre([after, before], w_gate, w_up, w_down, share)
    gu, near, far_top, far_bottom, outer_far = hidden(
        g_rows, w_down, w_gate, w_up, pre_own, pre_side, [top, bottom], share, wide_cols
    )

    came_top, came_bottom = shift(far_top, 1), shift(far_bottom, -1)
    part_ring = ring_part(near, w_gate, w_up, ring_cols)
    part_ring, gu = lax.optimization_barrier((part_ring, gu))
    home_ring = over_loc(part_ring.reshape(locs, groups * CAP, ring_cols))
    part_next, part_prev, part_own = side_part(gu, w_gate, w_up, came_top, came_bottom)
    from_before, from_after = shift(part_next, 1), shift(part_prev, -1)

    outers = (outer_own, outer_side, outer_far)
    part_own, gu, outers = lax.optimization_barrier((part_own, gu, outers))
    gate_grad, up_grad = row_grads(gu, blocks, share)
    down_grad = down(outers, blocks, g_rows, share)
    part_own, gate_grad, up_grad, down_grad = lax.optimization_barrier(
        (part_own, gate_grad, up_grad, down_grad)
    )
    fold_own, fold_top, fold_bottom, fold_side = fold(
        home_ring.reshape(2, experts, groups * CAP, ring_cols)
    )
    part_own, fold_top, fold_bottom = lax.optimization_barrier((part_own, fold_top, fold_bottom))
    home_wide = over_loc(sum_blocks(part_own, from_before, from_after))
    fold_next, fold_prev = add_far(fold_side, shift(fold_top, 1), shift(fold_bottom, -1))
    tokens_grad = combine(table, fold_own, shift(fold_next, 1), shift(fold_prev, -1), home_wide)
    return (tokens_grad, gate_grad[None], up_grad[None], down_grad[None])


def solution(mesh):
    in_specs = (
        P(("grp", "loc"), None),
        P(("grp", "loc"), None),
        P(("grp", "loc"), None),
        P(("grp", "loc"), None),
        P("loc", None, "grp"),
        P("loc", None, "grp"),
        P("loc", "grp", None),
    )
    out_specs = (
        P(("grp", "loc"), None),
        P("loc", None, "grp"),
        P("loc", None, "grp"),
        P("loc", "grp", None),
    )
    return jax.shard_map(body, mesh=mesh, in_specs=in_specs, out_specs=out_specs, check_vma=False)
```

```python
import functools

import jax
import jax.numpy as jnp
from jax import lax
from jax.experimental import pallas as pl
from jax.experimental.pallas import tpu as pltpu
from jax.sharding import PartitionSpec as P

CAP = 4
BF = jnp.bfloat16
F32 = jnp.float32
TILE = 512
ANY = pl.BlockSpec(memory_space=pl.ANY)
VMEM = pl.BlockSpec(memory_space=pltpu.VMEM)
HBM = pl.BlockSpec(memory_space=pltpu.HBM)


def contract_rows(left, right):
    return lax.dot_general(left, right, (((0,), (0,)), ((), ())), preferred_element_type=F32)


def contract_cols(left, right):
    return lax.dot_general(left, right, (((1,), (1,)), ((), ())), preferred_element_type=F32)


def whole(shape):
    return pl.BlockSpec(shape, lambda *_: (0,) * len(shape))


def call(kernel, name, flops, nbytes, mib=56, **kwargs):
    return pl.pallas_call(
        kernel,
        name=name,
        compiler_params=pltpu.CompilerParams(vmem_limit_bytes=mib << 20),
        cost_estimate=pl.CostEstimate(flops=flops, bytes_accessed=nbytes, transcendentals=0),
        **kwargs,
    )


def dispatch_kernel(ids_ref, w_ref, g_ref, t_ref, table_ref, ring_ref, out_ref, held, tokens, staged, sem):
    load = pltpu.make_async_copy(g_ref, held, sem.at[0])
    load.start()
    load_tokens = pltpu.make_async_copy(t_ref, tokens, sem.at[1])
    load_tokens.start()
    topk, tok = ids_ref.shape
    buf = table_ref.shape[0]
    unit = 2 * CAP
    experts = out_ref.shape[1]
    cols = ring_ref.shape[1]
    half = tokens.shape[1] // 2
    share = half - cols

    def tables(count, per_expert):
        slot_row = lax.broadcasted_iota(jnp.int32, (count, tok), 0)
        expert = lax.div(slot_row, per_expert)
        weights = w_ref[...].astype(F32)
        chosen = jnp.zeros((count, tok), F32)
        weight = jnp.zeros((count, tok), F32)
        for k in range(topk):
            hit = ids_ref[k : k + 1, :] == expert
            chosen = jnp.where(hit, 1.0, chosen)
            weight = jnp.where(hit, weights[k : k + 1, :], weight)
        before = lax.broadcasted_iota(jnp.int32, (tok, tok), 0)
        after = lax.broadcasted_iota(jnp.int32, (tok, tok), 1)
        earlier = jnp.where(before < after, 1.0, 0.0).astype(BF)
        slot = jnp.dot(chosen.astype(BF), earlier, preferred_element_type=F32)
        mine = (chosen > 0.5) & (slot == lax.rem(slot_row, CAP).astype(F32))
        return jnp.where(mine, 1.0, 0.0), jnp.where(mine, weight, 0.0), slot_row

    table_ref[...] = tables(buf, CAP)[0].astype(BF)
    table, weighted, slot_row = tables(2 * buf, unit)
    low = lax.rem(slot_row, unit) < CAP
    pick = jnp.concatenate(
        [jnp.where(low, table, 0.0).astype(BF), jnp.where(low, 0.0, table).astype(BF)], axis=1
    )
    both = jnp.concatenate(
        [jnp.where(low, weighted, 0.0).astype(BF), jnp.where(low, 0.0, weighted).astype(BF)], axis=1
    )
    load.wait()

    def rows(left, source, first, second, count):
        parts = jnp.concatenate(
            [source[:, first : first + count], source[:, second : second + count]], axis=0
        )
        return jnp.dot(left, parts, preferred_element_type=F32).astype(BF)

    staged[:, :, half:] = rows(both, held, 0, share, share).reshape(experts, unit, share)
    part = TILE // 2
    for first in range(0, cols, part):
        start = 2 * share + first
        ring_ref[:, first : first + part] = rows(both, held, start, start + cols, part)
    load_tokens.wait()
    for first in range(0, half, TILE):
        value = rows(pick, tokens, first, half + first, TILE)
        staged[:, :, first : first + TILE] = value.reshape(experts, unit, TILE)
    stores = [pltpu.make_async_copy(staged, out_ref.at[h], sem.at[2 + h]) for h in range(2)]
    for store in stores:
        store.start()
    for store in stores:
        store.wait()


def dispatch(ids, weights, grad_out, tokens, experts, share):
    tok, width = grad_out.shape
    buf = experts * CAP
    unit = 2 * CAP
    half = width // 2
    small = lambda *shape: jax.ShapeDtypeStruct(shape, BF)
    return call(
        dispatch_kernel,
        "dispatch",
        8 * tok * buf * width,
        2 * width * (2 * tok + 3 * buf),
        in_specs=[VMEM, VMEM, ANY, ANY],
        out_specs=[VMEM, VMEM, ANY],
        out_shape=[
            small(buf, tok),
            small(2 * buf, half - share),
            small(2, experts, unit, half + share),
        ],
        scratch_shapes=[
            pltpu.VMEM((tok, width), BF),
            pltpu.VMEM((tok, width), BF),
            pltpu.VMEM((experts, unit, half + share), BF),
            pltpu.SemaphoreType.DMA((4,)),
        ],
    )(ids, weights, grad_out, tokens)


def regroup_kernel(own_ref, next_ref, top_ref, bottom_ref, prev_ref, out_ref, held, sem):
    experts, unit, _ = own_ref.shape
    parts = 4
    size = experts // parts
    loads, stores = [], []
    for p in range(parts):
        window = slice(p * size, (p + 1) * size)
        if p < parts // 2:
            far = top_ref.at[window]
        else:
            far = bottom_ref.at[p * size - experts // 2 : (p + 1) * size - experts // 2]
        sources = [own_ref.at[window], next_ref.at[window], far, prev_ref.at[window]]
        for k, source in enumerate(sources):
            target = held.at[window, k * unit : (k + 1) * unit, :]
            loads.append(pltpu.make_async_copy(source, target, sem.at[p * 4 + k]))
            loads[-1].start()
    for p in range(parts):
        window = slice(p * size, (p + 1) * size)
        for k in range(4):
            loads[p * 4 + k].wait()
        for h in range(2):
            index = parts * 4 + 2 * p + h
            stores.append(pltpu.make_async_copy(held.at[window], out_ref.at[h, window], sem.at[index]))
            stores[-1].start()
    for store in stores:
        store.wait()


def regroup(blocks):
    count, cols = blocks[0].shape
    unit = 2 * CAP
    experts = count // unit
    return call(
        regroup_kernel,
        "regroup",
        0,
        24 * count * cols,
        in_specs=[ANY] * 5,
        out_specs=ANY,
        out_shape=jax.ShapeDtypeStruct((2, experts, 4 * unit, cols), BF),
        scratch_shapes=[
            pltpu.VMEM((experts, 4 * unit, cols), BF),
            pltpu.SemaphoreType.DMA((24,)),
        ],
    )(*[b.reshape(b.shape[0] // unit, unit, cols) for b in blocks])


def pre_kernel(count, *refs):
    x_refs = refs[:count]
    wg_ref, wu_ref, wd_ref, slope_ref, swish_ref, part_ref, outer_ref, x, w, d, acc, sem = refs[count:]
    rows, cols = x.shape
    ff = w.shape[2] // 4
    share = d.shape[1]
    half = cols - share
    steps = half // TILE
    copies = [[] for _ in range(steps + 1)]
    index = 0

    def add(step, source, target):
        nonlocal index
        copies[step].append(pltpu.make_async_copy(source, target, sem.at[index]))
        index += 1

    for t in range(steps + 1):
        window = slice(t * TILE, (t + 1) * TILE) if t < steps else slice(half, cols)
        at = 0
        for ref in x_refs:
            add(t, ref.at[:, window], x.at[at : at + ref.shape[0], window])
            at += ref.shape[0]
        if t < steps:
            for k, ref in enumerate((wg_ref, wu_ref)):
                for h in range(2):
                    lane = (2 * k + h) * ff
                    source = ref.at[h * half + t * TILE : h * half + (t + 1) * TILE, :]
                    add(t, source, w.at[t, :, lane : lane + ff])
        else:
            for h in range(2):
                source = wd_ref.at[:, h * share : (h + 1) * share]
                add(t, source, d.at[h * ff : (h + 1) * ff, :])
    for group in copies:
        for copy in group:
            copy.start()
    for t in range(steps):
        for copy in copies[t]:
            copy.wait()
        value = jnp.dot(x[:, t * TILE : (t + 1) * TILE], w[t], preferred_element_type=F32)
        if t == 0:
            acc[...] = value
        else:
            acc[...] += value
    for copy in copies[steps]:
        copy.wait()

    def fold_halves(value):
        value = value.reshape(rows // (2 * CAP), 2 * CAP, 2 * ff)
        return (value[:, :CAP, :ff] + value[:, CAP:, ff:]).reshape(rows // 2, ff)

    part_ref[...] = fold_halves(contract_cols(x[:, half:], d[...]))
    gate = fold_halves(acc[:, : 2 * ff])
    up = fold_halves(acc[:, 2 * ff :])
    sig = 1.0 / (1.0 + jnp.exp(-gate))
    swish = gate * sig
    slope_ref[...] = up * sig * (1.0 + gate * (1.0 - sig))
    swish_ref[...] = swish
    outer_ref[...] = swish * up


def pre(blocks, w_gate, w_up, w_down, share):
    cols = blocks[0].shape[1]
    rows = sum(b.shape[0] for b in blocks)
    ff = w_gate.shape[1]
    steps = (cols - share) // TILE
    copies = (len(blocks) + 4) * steps + len(blocks) + 2
    return call(
        functools.partial(pre_kernel, len(blocks)),
        "pre",
        200 * (8 * rows * cols * ff),
        200 * (2 * cols * (rows + 4 * ff)),
        in_specs=[ANY] * len(blocks) + [HBM] * 3,
        out_specs=[VMEM] * 4,
        out_shape=[jax.ShapeDtypeStruct((rows // 2, ff), F32)] * 4,
        scratch_shapes=[
            pltpu.VMEM((rows, cols), BF),
            pltpu.VMEM((steps, TILE, 4 * ff), BF),
            pltpu.VMEM((2 * ff, share), BF),
            pltpu.VMEM((rows, 4 * ff), F32),
            pltpu.SemaphoreType.DMA((copies,)),
        ],
    )(*blocks, w_gate, w_up, w_down)


def load_weights(wg_ref, wu_ref, w, first, sem, index):
    count = w.shape[0]
    ff = wg_ref.shape[1]
    copies = []
    for k, ref in enumerate((wg_ref, wu_ref)):
        source = ref.at[first : first + count, :]
        target = w.at[:, k * ff : (k + 1) * ff]
        copies.append(pltpu.make_async_copy(source, target, sem.at[index + k]))
    return copies


def start_all(copies):
    for copy in copies:
        copy.start()


def wait_all(copies):
    for copy in copies:
        copy.wait()


def hidden_kernel(
    g_ref, wd_ref, wg_ref, wu_ref, *refs
):
    own, side, far = refs[0:3], refs[3:6], refs[6:9]
    gu_ref, near_ref, top_ref, bottom_ref, g, d, w, small, staged, sem = refs[9:]
    groups, span, double = gu_ref.shape
    ff = double // 2
    locs = span // CAP
    unit = 2 * CAP
    cols = g.shape[1]
    wide_cols = top_ref.shape[1]
    first_col = wd_ref.shape[1] - 2 * cols
    tile = 3 * TILE // 2
    windows = [slice(at, min(at + tile, cols)) for at in range(0, cols, tile)]
    steps = len(windows)
    loads = []
    for t, window in enumerate(windows):
        loads.append(pltpu.make_async_copy(g_ref.at[:, window], g.at[:, window], sem.at[3 * t]))
        for h in range(2):
            start = first_col + h * cols + window.start
            source = wd_ref.at[:, start : start + window.stop - window.start]
            target = d.at[h * ff : (h + 1) * ff, window]
            loads.append(pltpu.make_async_copy(source, target, sem.at[3 * t + 1 + h]))
    more = []
    index = 3 * steps
    for k in range(3):
        places = [(own[k], 0), (side[k].at[:span], 1), (far[k], 2), (side[k].at[span:], 3)]
        for source, group in places:
            more.append(pltpu.make_async_copy(source, small.at[k, group], sem.at[index]))
            index += 1
    weights = load_weights(wg_ref, wu_ref, w, wg_ref.shape[0] - wide_cols, sem, index)
    start_all(loads)
    start_all(more)
    start_all(weights)
    total = None
    for t, window in enumerate(windows):
        wait_all(loads[3 * t : 3 * t + 3])
        value = contract_cols(g[:, window], d[:, window])
        total = value if total is None else total + value
    wait_all(more)
    halves = total.reshape(locs, groups * unit, double)
    for group in range(groups):
        first = group * unit
        hidden = (
            halves[:, first : first + CAP, :ff] + halves[:, first + CAP : first + unit, ff:]
        ).reshape(span, ff) + small[2, group]
        gate = hidden * small[0, group]
        up = hidden * small[1, group]
        both = jnp.concatenate([gate, up], axis=1)
        gu_ref[group] = both.astype(BF)
        near_ref[:, group * CAP : (group + 1) * CAP, :] = both.reshape(locs, CAP, double).astype(BF)
    wait_all(weights)
    staged[...] = contract_cols(gu_ref[2], w[...]).astype(BF)
    stores = [
        pltpu.make_async_copy(staged.at[: span // 2], top_ref, sem.at[index + 2]),
        pltpu.make_async_copy(staged.at[span // 2 :], bottom_ref, sem.at[index + 3]),
    ]
    start_all(stores)
    wait_all(stores)


def hidden(g_rows, w_down, w_gate, w_up, own, side, far, wide_cols):
    rows, cols = g_rows.shape
    span, ff = own[0].shape
    groups = rows // 2 // span
    small = lambda *shape: jax.ShapeDtypeStruct(shape, BF)
    return call(
        hidden_kernel,
        "hidden",
        4 * rows * cols * ff + 4 * span * ff * wide_cols,
        2 * (rows * cols + 2 * wide_cols * ff + span * wide_cols),
        in_specs=[ANY] + [HBM] * 3 + [ANY] * 9,
        out_specs=[VMEM, VMEM, ANY, ANY],
        out_shape=[
            small(groups, span, 2 * ff),
            small(span // CAP, groups * CAP, 2 * ff),
            small(span // 2, wide_cols),
            small(span // 2, wide_cols),
        ],
        scratch_shapes=[
            pltpu.VMEM((rows, cols), BF),
            pltpu.VMEM((2 * ff, cols), BF),
            pltpu.VMEM((wide_cols, 2 * ff), BF),
            pltpu.VMEM((3, groups, span, ff), F32),
            pltpu.VMEM((span, wide_cols), BF),
            pltpu.SemaphoreType.DMA((3 * pl.cdiv(cols, 3 * TILE // 2) + 12 + 4,)),
        ],
    )(g_rows, w_down, w_gate, w_up, *own, *side, *far)


def ring_part_kernel(near_ref, wg_ref, wu_ref, out_ref, w, staged, sem):
    rows, ring_cols = out_ref.shape
    loads = load_weights(wg_ref, wu_ref, w, 0, sem, 0)
    start_all(loads)
    wait_all(loads)
    left = near_ref[...].reshape(rows, w.shape[1])
    stores = []
    for c in range(ring_cols // TILE):
        window = slice(c * TILE, (c + 1) * TILE)
        staged[:, window] = contract_cols(left, w[window, :]).astype(BF)
        target = out_ref.at[:, window]
        stores.append(pltpu.make_async_copy(staged.at[:, window], target, sem.at[2 + c]))
        stores[-1].start()
    wait_all(stores)


def ring_part(near, w_gate, w_up, ring_cols):
    locs, depth, double = near.shape
    rows = locs * depth
    return call(
        ring_part_kernel,
        "ring_part",
        2 * rows * double * ring_cols,
        2 * ring_cols * (rows + double),
        in_specs=[VMEM, HBM, HBM],
        out_specs=ANY,
        out_shape=jax.ShapeDtypeStruct((rows, ring_cols), BF),
        scratch_shapes=[
            pltpu.VMEM((ring_cols, double), BF),
            pltpu.VMEM((rows, ring_cols), BF),
            pltpu.SemaphoreType.DMA((2 + ring_cols // TILE,)),
        ],
    )(near, w_gate, w_up)


def side_kernel(gu_ref, wg_ref, wu_ref, top_ref, bottom_ref, next_ref, prev_ref, own_ref, w, held, staged, sem):
    _, span, double = gu_ref.shape
    wide_cols = next_ref.shape[1]
    weights = load_weights(wg_ref, wu_ref, w, wg_ref.shape[0] - wide_cols, sem, 0)
    came = [
        pltpu.make_async_copy(top_ref, held.at[0], sem.at[2]),
        pltpu.make_async_copy(bottom_ref, held.at[1], sem.at[3]),
    ]
    start_all(weights)
    start_all(came)
    wait_all(weights)
    wait_all(came)
    left = jnp.concatenate([gu_ref[1], gu_ref[3], gu_ref[0]], axis=0)
    mid = span // 2
    stores = []
    for c in range(wide_cols // TILE):
        window = slice(c * TILE, (c + 1) * TILE)
        value = contract_cols(left, w[window, :])
        top = held[0, :, window].astype(F32)
        bottom = held[1, :, window].astype(F32)
        staged[0, :mid, window] = (value[:mid] + top).astype(BF)
        staged[0, mid:, window] = value[mid:span].astype(BF)
        staged[1, :mid, window] = value[span : span + mid].astype(BF)
        staged[1, mid:, window] = (value[span + mid : 2 * span] + bottom).astype(BF)
        staged[2, :, window] = value[2 * span :].astype(BF)
        for k, ref in enumerate((next_ref, prev_ref, own_ref)):
            copy = pltpu.make_async_copy(
                staged.at[k, :, window], ref.at[:, window], sem.at[4 + 3 * c + k]
            )
            copy.start()
            stores.append(copy)
    wait_all(stores)


def side_part(gu, w_gate, w_up, top, bottom):
    _, span, double = gu.shape
    wide_cols = top.shape[1]
    return call(
        side_kernel,
        "side_part",
        40 * (6 * span * double * wide_cols),
        40 * (2 * wide_cols * (4 * span + double)),
        in_specs=[VMEM, HBM, HBM, ANY, ANY],
        out_specs=[ANY] * 3,
        out_shape=[jax.ShapeDtypeStruct((span, wide_cols), BF)] * 3,
        scratch_shapes=[
            pltpu.VMEM((wide_cols, double), BF),
            pltpu.VMEM((2, span // 2, wide_cols), BF),
            pltpu.VMEM((3, span, wide_cols), BF),
            pltpu.SemaphoreType.DMA((4 + 3 * (wide_cols // TILE),)),
        ],
    )(gu, w_gate, w_up, top, bottom)


def sum_kernel(a_ref, b_ref, c_ref, out_ref, held, staged, sem):
    locs, _, cols = out_ref.shape
    steps = cols // TILE
    loads, stores = [], []
    for t in range(steps):
        window = slice(t * TILE, (t + 1) * TILE)
        for k, ref in enumerate((a_ref, b_ref, c_ref)):
            loads.append(
                pltpu.make_async_copy(ref.at[:, window], held.at[k, :, window], sem.at[4 * t + k])
            )
    start_all(loads)
    for t in range(steps):
        wait_all(loads[3 * t : 3 * t + 3])
        window = slice(t * TILE, (t + 1) * TILE)
        total = sum(held[k, :, window].astype(F32) for k in range(3))
        staged[:, :, window] = total.reshape(locs, CAP, TILE).astype(BF)
        source = staged.at[:, :, window]
        stores.append(pltpu.make_async_copy(source, out_ref.at[:, :, window], sem.at[4 * t + 3]))
        stores[-1].start()
    wait_all(stores)


def sum_blocks(a, b, c):
    rows, cols = a.shape
    return call(
        sum_kernel,
        "sum_blocks",
        2 * rows * cols,
        8 * rows * cols,
        in_specs=[HBM, ANY, ANY],
        out_specs=ANY,
        out_shape=jax.ShapeDtypeStruct((rows // CAP, CAP, cols), BF),
        scratch_shapes=[
            pltpu.VMEM((3, rows, cols), BF),
            pltpu.VMEM((rows // CAP, CAP, cols), BF),
            pltpu.SemaphoreType.DMA((4 * (cols // TILE),)),
        ],
    )(a, b, c)


def row_grads_kernel(gu_ref, own_ref, next_ref, top_ref, bottom_ref, prev_ref, gate_ref, up_ref, wide):
    groups, span, double = gu_ref.shape
    ff = double // 2
    locs = span // CAP

    @pl.when(pl.program_id(0) == 0)
    def _():
        zero = jnp.zeros((locs, CAP, ff), F32)
        for group in range(groups):
            both = gu_ref[group].astype(F32).reshape(locs, CAP, double)
            gate, up = both[:, :, :ff], both[:, :, ff:]
            low = jnp.concatenate([gate, zero, up, zero], axis=2)
            high = jnp.concatenate([zero, gate, zero, up], axis=2)
            both = jnp.concatenate([low, high], axis=1).reshape(2 * span, 4 * ff)
            wide[2 * span * group : 2 * span * (group + 1), :] = both.astype(BF)

    x = jnp.concatenate(
        [own_ref[...], next_ref[...], top_ref[...], bottom_ref[...], prev_ref[...]], axis=0
    )
    total = contract_rows(x, wide[...]).astype(BF)
    gate_ref[0] = total[:, :ff]
    gate_ref[1] = total[:, ff : 2 * ff]
    up_ref[0] = total[:, 2 * ff : 3 * ff]
    up_ref[1] = total[:, 3 * ff :]


def row_grads(gu, blocks, share):
    groups, span, double = gu.shape
    ff = double // 2
    rows = 2 * groups * span
    half = blocks[0].shape[1] - share
    out = jax.ShapeDtypeStruct((2, half, ff), BF)
    gate, up = call(
        row_grads_kernel,
        "row_grads",
        8 * rows * half * ff,
        2 * half * (rows + 4 * ff),
        grid=(half // TILE,),
        in_specs=[
            whole(gu.shape),
            *[pl.BlockSpec((b.shape[0], TILE), lambda j: (0, j)) for b in blocks],
        ],
        out_specs=[pl.BlockSpec((2, TILE, ff), lambda j: (0, j, 0))] * 2,
        out_shape=[out, out],
        scratch_shapes=[pltpu.VMEM((rows, 4 * ff), BF)],
    )(gu, *blocks)
    return gate.reshape(2 * half, ff), up.reshape(2 * half, ff)


def down_kernel(g_ref, *refs):
    outers, blocks = refs[:3], refs[3:8]
    out_ref, wide, held, sem = refs[8:]
    own, side, far = outers
    span, ff = own.shape
    locs = span // CAP
    unit = 2 * CAP
    step = pl.program_id(0)
    tile = g_ref.shape[1]
    share = held.shape[1]

    def spread(outer):
        rows = outer.reshape(locs, CAP, ff)
        zero = jnp.zeros_like(rows)
        low = jnp.concatenate([rows, zero], axis=2)
        high = jnp.concatenate([zero, rows], axis=2)
        return jnp.concatenate([low, high], axis=1)

    @pl.when(step == 0)
    def _():
        copies = []
        at = 0
        for k, ref in enumerate(blocks):
            source = ref.at[:, ref.shape[1] - share :]
            copies.append(
                pltpu.make_async_copy(source, held.at[at : at + ref.shape[0], :], sem.at[k])
            )
            at += ref.shape[0]
        start_all(copies)
        rows = []
        for k, outer in enumerate((own[...], side[:span], far[...], side[span:])):
            block = spread(outer).astype(BF)
            wide[:, k * unit : (k + 1) * unit, :] = block
            rows.append(block.reshape(2 * span, 2 * ff))
        wait_all(copies)
        total = contract_rows(jnp.concatenate(rows, axis=0), held[...]).astype(BF)
        out_ref[:, :share] = total[:ff]
        out_ref[:, share : 2 * share] = total[ff:]

    rows = wide[...].reshape(g_ref.shape[0], 2 * ff)
    total = contract_rows(rows, g_ref[...]).astype(BF)
    low = 2 * share + step * tile
    high = low + pl.num_programs(0) * tile
    out_ref[:, pl.ds(pl.multiple_of(low, 128), tile)] = total[:ff]
    out_ref[:, pl.ds(pl.multiple_of(high, 128), tile)] = total[ff:]


def down(outers, blocks, g_rows, share):
    rows, cols = g_rows.shape
    span, ff = outers[0].shape
    width = 2 * (cols + share)
    tile = TILE if cols % TILE == 0 else TILE // 2
    return call(
        down_kernel,
        "down",
        4 * rows * (cols + share) * ff,
        2 * (cols + share) * (rows + 2 * ff),
        grid=(cols // tile,),
        in_specs=[
            pl.BlockSpec((rows, tile), lambda j: (0, j)),
            *[whole(o.shape) for o in outers],
            *[ANY] * 5,
        ],
        out_specs=whole((ff, width)),
        out_shape=jax.ShapeDtypeStruct((ff, width), BF),
        scratch_shapes=[
            pltpu.VMEM((span // CAP, rows * CAP // span, 2 * ff), BF),
            pltpu.VMEM((rows, share), BF),
            pltpu.SemaphoreType.DMA((5,)),
        ],
    )(g_rows, *outers, *blocks)


def fold_kernel(in_ref, own_ref, top_ref, bottom_ref, side_ref):
    _, experts, depth, tile = in_ref.shape
    total = in_ref[0].astype(F32) + in_ref[1].astype(F32)
    for step in range(depth // CAP):
        part = total[:, step * CAP : (step + 1) * CAP, :].reshape(experts * CAP, tile).astype(BF)
        if step == 2:
            top_ref[...] = part[: experts * CAP // 2]
            bottom_ref[...] = part[experts * CAP // 2 :]
        elif step == 0:
            own_ref[...] = part
        else:
            side_ref[step // 2] = part


def fold(home):
    _, experts, depth, width = home.shape
    buf = experts * CAP
    tile = TILE
    return call(
        fold_kernel,
        "fold",
        experts * depth * width,
        6 * experts * depth * width,
        mib=20,
        grid=(width // tile,),
        in_specs=[pl.BlockSpec((2, experts, depth, tile), lambda j: (0, 0, 0, j))],
        out_specs=[
            pl.BlockSpec((buf, tile), lambda j: (0, j)),
            pl.BlockSpec((buf // 2, tile), lambda j: (0, j)),
            pl.BlockSpec((buf // 2, tile), lambda j: (0, j)),
            pl.BlockSpec((2, buf, tile), lambda j: (0, 0, j)),
        ],
        out_shape=[
            jax.ShapeDtypeStruct((buf, width), BF),
            jax.ShapeDtypeStruct((buf // 2, width), BF),
            jax.ShapeDtypeStruct((buf // 2, width), BF),
            jax.ShapeDtypeStruct((2, buf, width), BF),
        ],
    )(home)


def add_kernel(side_ref, top_ref, bottom_ref, next_ref, prev_ref):
    mid = top_ref.shape[0]
    next_ref[:mid] = (side_ref[0, :mid].astype(F32) + top_ref[...].astype(F32)).astype(BF)
    next_ref[mid:] = side_ref[0, mid:]
    prev_ref[:mid] = side_ref[1, :mid]
    prev_ref[mid:] = (side_ref[1, mid:].astype(F32) + bottom_ref[...].astype(F32)).astype(BF)


def add_far(side, top, bottom):
    _, buf, cols = side.shape
    return call(
        add_kernel,
        "add_far",
        buf * cols,
        10 * buf * cols,
        mib=20,
        in_specs=[VMEM] * 3,
        out_specs=[VMEM] * 2,
        out_shape=[jax.ShapeDtypeStruct((buf, cols), BF)] * 2,
    )(side, top, bottom)


def combine_kernel(table_ref, own_ref, left_ref, right_ref, wide_ref, out_ref, ring, wide, staged, sem):
    buf = table_ref.shape[0]
    ring_cols = ring.shape[1]
    locs, _, wide_cols = wide.shape
    loads, stores = [], []

    def add(source, target):
        loads.append(pltpu.make_async_copy(source, target, sem.at[len(loads)]))

    for k, ref in enumerate((own_ref, left_ref, right_ref)):
        add(ref, ring.at[k * buf : (k + 1) * buf, :])
    for first in range(0, wide_cols, TILE):
        window = slice(first, first + TILE)
        add(wide_ref.at[:, :, window], wide.at[:, :, window])
    start_all(loads)
    table = table_ref[...]
    twice = jnp.concatenate([table] * 2, axis=0)
    thrice = jnp.concatenate([table] * 3, axis=0)
    wait_all(loads[:3])
    for t in range((ring_cols + wide_cols) // TILE):
        window = slice(t * TILE, (t + 1) * TILE)
        first = t * TILE - ring_cols
        if first < 0:
            total = contract_rows(thrice, ring[:, window])
        else:
            loads[3 + first // TILE].wait()
            rows = wide[:, :, first : first + TILE].astype(F32).reshape(locs * CAP, TILE).astype(BF)
            total = contract_rows(twice, rows)
        staged[:, window] = total.astype(BF)
        target = out_ref.at[:, window]
        index = len(loads) + len(stores)
        stores.append(pltpu.make_async_copy(staged.at[:, window], target, sem.at[index]))
        stores[-1].start()
    wait_all(stores)


def combine(table, own, left, right, wide):
    buf, tok = table.shape
    ring_cols, wide_cols = left.shape[1], wide.shape[2]
    width = ring_cols + wide_cols
    return call(
        combine_kernel,
        "combine",
        2 * tok * buf * width,
        2 * width * (tok + 2 * buf),
        mib=24,
        in_specs=[VMEM, HBM, ANY, ANY, ANY],
        out_specs=ANY,
        out_shape=jax.ShapeDtypeStruct((tok, width), BF),
        scratch_shapes=[
            pltpu.VMEM((3 * buf, ring_cols), BF),
            pltpu.VMEM((wide.shape[0], CAP, wide_cols), BF),
            pltpu.VMEM((tok, width), BF),
            pltpu.SemaphoreType.DMA((3 + wide_cols // TILE + width // TILE,)),
        ],
    )(table, own, left, right, wide)


def over_loc(a):
    return lax.all_to_all(a, "loc", split_axis=0, concat_axis=0, tiled=True)


def shift(a, step):
    groups = lax.axis_size("grp")
    return lax.ppermute(a, "grp", [(i, (i + step) % groups) for i in range(groups)])


def ring_gather(own):
    mid = own.shape[0] // 2
    before, after = shift(own, 1), shift(own, -1)
    return [own, after, shift(before[:mid], 1), shift(after[mid:], -1), before]


def body(tokens, grad_out, expert_ids, route_weight, gate_weight, up_weight, down_weight):
    groups = lax.axis_size("grp")
    locs = lax.axis_size("loc")
    experts = locs // 2
    width = tokens.shape[1]
    buf = experts * CAP
    unit = 2 * CAP
    share = 768
    ring_cols = 2560
    wide_cols = width - ring_cols

    w_gate, w_up, w_down = gate_weight[0], up_weight[0], down_weight[0]

    table, g_send, xg_send = dispatch(
        expert_ids.T, route_weight.T, grad_out, tokens, experts, share
    )
    g_blocks = ring_gather(g_send)
    xg = over_loc(xg_send.reshape(locs, unit, xg_send.shape[3]))
    xg, *g_blocks = lax.optimization_barrier((xg, *g_blocks))
    blocks = ring_gather(xg.reshape(locs * unit, xg.shape[2]))
    g_out = regroup(g_blocks)
    g_rows = over_loc(g_out.reshape(locs, groups * unit, g_out.shape[3]))
    g_rows = g_rows.reshape(locs * groups * unit, g_out.shape[3])

    own, after, top, bottom, before = blocks
    *pre_own, outer_own = pre([own], w_gate, w_up, w_down, share)
    *pre_side, outer_side = pre([after, before], w_gate, w_up, w_down, share)
    *pre_far, outer_far = pre([top, bottom], w_gate, w_up, w_down, share)
    gu, near, far_top, far_bottom = hidden(
        g_rows, w_down, w_gate, w_up, pre_own, pre_side, pre_far, wide_cols
    )

    came_top, came_bottom = shift(far_top, 1), shift(far_bottom, -1)
    part_ring = ring_part(near, w_gate, w_up, ring_cols)
    part_ring, gu = lax.optimization_barrier((part_ring, gu))
    home_ring = over_loc(part_ring.reshape(locs, groups * CAP, ring_cols))
    part_next, part_prev, part_own = side_part(gu, w_gate, w_up, came_top, came_bottom)
    from_before, from_after = shift(part_next, 1), shift(part_prev, -1)

    outers = (outer_own, outer_side, outer_far)
    part_own, gu, outers = lax.optimization_barrier((part_own, gu, outers))
    gate_grad, up_grad = row_grads(gu, blocks, share)
    down_grad = down(outers, blocks, g_rows, share)
    part_own, gate_grad, up_grad, down_grad = lax.optimization_barrier(
        (part_own, gate_grad, up_grad, down_grad)
    )
    fold_own, fold_top, fold_bottom, fold_side = fold(
        home_ring.reshape(2, experts, groups * CAP, ring_cols)
    )
    part_own, fold_top, fold_bottom = lax.optimization_barrier((part_own, fold_top, fold_bottom))
    home_wide = over_loc(sum_blocks(part_own, from_before, from_after))
    fold_next, fold_prev = add_far(fold_side, shift(fold_top, 1), shift(fold_bottom, -1))
    tokens_grad = combine(table, fold_own, shift(fold_next, 1), shift(fold_prev, -1), home_wide)
    return (tokens_grad, gate_grad[None], up_grad[None], down_grad[None])


def solution(mesh):
    in_specs = (
        P(("grp", "loc"), None),
        P(("grp", "loc"), None),
        P(("grp", "loc"), None),
        P(("grp", "loc"), None),
        P("loc", None, "grp"),
        P("loc", None, "grp"),
        P("loc", "grp", None),
    )
    out_specs = (
        P(("grp", "loc"), None),
        P("loc", None, "grp"),
        P("loc", None, "grp"),
        P("loc", "grp", None),
    )
    return jax.shard_map(body, mesh=mesh, in_specs=in_specs, out_specs=out_specs, check_vma=False)
```

```python
import functools

import jax
import jax.numpy as jnp
from jax import lax
from jax.experimental import pallas as pl
from jax.experimental.pallas import tpu as pltpu
from jax.sharding import PartitionSpec as P

CAP = 4
BF = jnp.bfloat16
F32 = jnp.float32
TILE = 512
ANY = pl.BlockSpec(memory_space=pl.ANY)
VMEM = pl.BlockSpec(memory_space=pltpu.VMEM)
HBM = pl.BlockSpec(memory_space=pltpu.HBM)


def contract_rows(left, right):
    return lax.dot_general(left, right, (((0,), (0,)), ((), ())), preferred_element_type=F32)


def contract_cols(left, right):
    return lax.dot_general(left, right, (((1,), (1,)), ((), ())), preferred_element_type=F32)


def whole(shape):
    return pl.BlockSpec(shape, lambda *_: (0,) * len(shape))


def call(kernel, name, flops, nbytes, mib=56, **kwargs):
    return pl.pallas_call(
        kernel,
        name=name,
        compiler_params=pltpu.CompilerParams(vmem_limit_bytes=mib << 20),
        cost_estimate=pl.CostEstimate(flops=flops, bytes_accessed=nbytes, transcendentals=0),
        **kwargs,
    )


def dispatch_kernel(ids_ref, w_ref, g_ref, t_ref, table_ref, ring_ref, out_ref, held, tokens, staged, sem):
    load = pltpu.make_async_copy(g_ref, held, sem.at[0])
    load.start()
    load_tokens = pltpu.make_async_copy(t_ref, tokens, sem.at[1])
    load_tokens.start()
    topk, tok = ids_ref.shape
    buf = table_ref.shape[0]
    unit = 2 * CAP
    experts = out_ref.shape[1]
    cols = ring_ref.shape[1]
    half = tokens.shape[1] // 2
    share = half - cols

    def tables(count, per_expert):
        slot_row = lax.broadcasted_iota(jnp.int32, (count, tok), 0)
        expert = lax.div(slot_row, per_expert)
        weights = w_ref[...].astype(F32)
        chosen = jnp.zeros((count, tok), F32)
        weight = jnp.zeros((count, tok), F32)
        for k in range(topk):
            hit = ids_ref[k : k + 1, :] == expert
            chosen = jnp.where(hit, 1.0, chosen)
            weight = jnp.where(hit, weights[k : k + 1, :], weight)
        before = lax.broadcasted_iota(jnp.int32, (tok, tok), 0)
        after = lax.broadcasted_iota(jnp.int32, (tok, tok), 1)
        earlier = jnp.where(before < after, 1.0, 0.0).astype(BF)
        slot = jnp.dot(chosen.astype(BF), earlier, preferred_element_type=F32)
        mine = (chosen > 0.5) & (slot == lax.rem(slot_row, CAP).astype(F32))
        return jnp.where(mine, 1.0, 0.0), jnp.where(mine, weight, 0.0), slot_row

    table_ref[...] = tables(buf, CAP)[0].astype(BF)
    table, weighted, slot_row = tables(2 * buf, unit)
    low = lax.rem(slot_row, unit) < CAP
    pick = jnp.concatenate(
        [jnp.where(low, table, 0.0).astype(BF), jnp.where(low, 0.0, table).astype(BF)], axis=1
    )
    both = jnp.concatenate(
        [jnp.where(low, weighted, 0.0).astype(BF), jnp.where(low, 0.0, weighted).astype(BF)], axis=1
    )
    load.wait()

    def rows(left, source, first, second, count):
        parts = jnp.concatenate(
            [source[:, first : first + count], source[:, second : second + count]], axis=0
        )
        return jnp.dot(left, parts, preferred_element_type=F32).astype(BF)

    staged[:, :, half:] = rows(both, held, 0, share, share).reshape(experts, unit, share)
    part = TILE // 2
    for first in range(0, cols, part):
        start = 2 * share + first
        ring_ref[:, first : first + part] = rows(both, held, start, start + cols, part)
    load_tokens.wait()
    for first in range(0, half, TILE):
        value = rows(pick, tokens, first, half + first, TILE)
        staged[:, :, first : first + TILE] = value.reshape(experts, unit, TILE)
    stores = [pltpu.make_async_copy(staged, out_ref.at[h], sem.at[2 + h]) for h in range(2)]
    for store in stores:
        store.start()
    for store in stores:
        store.wait()


def dispatch(ids, weights, grad_out, tokens, experts, share):
    tok, width = grad_out.shape
    buf = experts * CAP
    unit = 2 * CAP
    half = width // 2
    small = lambda *shape: jax.ShapeDtypeStruct(shape, BF)
    return call(
        dispatch_kernel,
        "dispatch",
        8 * tok * buf * width,
        2 * width * (2 * tok + 3 * buf),
        in_specs=[VMEM, VMEM, ANY, ANY],
        out_specs=[VMEM, VMEM, ANY],
        out_shape=[
            small(buf, tok),
            small(2 * buf, half - share),
            small(2, experts, unit, half + share),
        ],
        scratch_shapes=[
            pltpu.VMEM((tok, width), BF),
            pltpu.VMEM((tok, width), BF),
            pltpu.VMEM((experts, unit, half + share), BF),
            pltpu.SemaphoreType.DMA((4,)),
        ],
    )(ids, weights, grad_out, tokens)


def regroup_kernel(own_ref, next_ref, top_ref, bottom_ref, prev_ref, out_ref, held, sem):
    experts, unit, _ = own_ref.shape
    parts = 4
    size = experts // parts
    loads, stores = [], []
    for p in range(parts):
        window = slice(p * size, (p + 1) * size)
        if p < parts // 2:
            far = top_ref.at[window]
        else:
            far = bottom_ref.at[p * size - experts // 2 : (p + 1) * size - experts // 2]
        sources = [own_ref.at[window], next_ref.at[window], far, prev_ref.at[window]]
        for k, source in enumerate(sources):
            target = held.at[window, k * unit : (k + 1) * unit, :]
            loads.append(pltpu.make_async_copy(source, target, sem.at[p * 4 + k]))
            loads[-1].start()
    for p in range(parts):
        window = slice(p * size, (p + 1) * size)
        for k in range(4):
            loads[p * 4 + k].wait()
        for h in range(2):
            index = parts * 4 + 2 * p + h
            stores.append(pltpu.make_async_copy(held.at[window], out_ref.at[h, window], sem.at[index]))
            stores[-1].start()
    for store in stores:
        store.wait()


def regroup(blocks):
    count, cols = blocks[0].shape
    unit = 2 * CAP
    experts = count // unit
    return call(
        regroup_kernel,
        "regroup",
        0,
        24 * count * cols,
        in_specs=[ANY] * 5,
        out_specs=ANY,
        out_shape=jax.ShapeDtypeStruct((2, experts, 4 * unit, cols), BF),
        scratch_shapes=[
            pltpu.VMEM((experts, 4 * unit, cols), BF),
            pltpu.SemaphoreType.DMA((24,)),
        ],
    )(*[b.reshape(b.shape[0] // unit, unit, cols) for b in blocks])


def pre_kernel(count, *refs):
    x_refs = refs[:count]
    wg_ref, wu_ref, wd_ref, slope_ref, swish_ref, part_ref, outer_ref, x, w, d, acc, sem = refs[count:]
    rows, cols = x.shape
    ff = w.shape[2] // 4
    share = d.shape[1]
    half = cols - share
    steps = half // TILE
    copies = [[] for _ in range(steps + 1)]
    index = 0

    def add(step, source, target):
        nonlocal index
        copies[step].append(pltpu.make_async_copy(source, target, sem.at[index]))
        index += 1

    for t in range(steps + 1):
        window = slice(t * TILE, (t + 1) * TILE) if t < steps else slice(half, cols)
        at = 0
        for ref in x_refs:
            add(t, ref.at[:, window], x.at[at : at + ref.shape[0], window])
            at += ref.shape[0]
        if t < steps:
            for k, ref in enumerate((wg_ref, wu_ref)):
                for h in range(2):
                    lane = (2 * k + h) * ff
                    source = ref.at[h * half + t * TILE : h * half + (t + 1) * TILE, :]
                    add(t, source, w.at[t, :, lane : lane + ff])
        else:
            for h in range(2):
                source = wd_ref.at[:, h * share : (h + 1) * share]
                add(t, source, d.at[h * ff : (h + 1) * ff, :])
    for group in copies:
        for copy in group:
            copy.start()
    for t in range(steps):
        for copy in copies[t]:
            copy.wait()
        value = jnp.dot(x[:, t * TILE : (t + 1) * TILE], w[t], preferred_element_type=F32)
        if t == 0:
            acc[...] = value
        else:
            acc[...] += value
    for copy in copies[steps]:
        copy.wait()

    def fold_halves(value):
        value = value.reshape(rows // (2 * CAP), 2 * CAP, 2 * ff)
        return (value[:, :CAP, :ff] + value[:, CAP:, ff:]).reshape(rows // 2, ff)

    part_ref[...] = fold_halves(contract_cols(x[:, half:], d[...]))
    gate = fold_halves(acc[:, : 2 * ff])
    up = fold_halves(acc[:, 2 * ff :])
    sig = 1.0 / (1.0 + jnp.exp(-gate))
    swish = gate * sig
    slope_ref[...] = up * sig * (1.0 + gate * (1.0 - sig))
    swish_ref[...] = swish
    outer_ref[...] = swish * up


def pre(blocks, w_gate, w_up, w_down, share):
    cols = blocks[0].shape[1]
    rows = sum(b.shape[0] for b in blocks)
    ff = w_gate.shape[1]
    steps = (cols - share) // TILE
    copies = (len(blocks) + 4) * steps + len(blocks) + 2
    return call(
        functools.partial(pre_kernel, len(blocks)),
        "pre",
        200 * (8 * rows * cols * ff),
        200 * (2 * cols * (rows + 4 * ff)),
        in_specs=[ANY] * len(blocks) + [HBM] * 3,
        out_specs=[VMEM] * 4,
        out_shape=[jax.ShapeDtypeStruct((rows // 2, ff), F32)] * 4,
        scratch_shapes=[
            pltpu.VMEM((rows, cols), BF),
            pltpu.VMEM((steps, TILE, 4 * ff), BF),
            pltpu.VMEM((2 * ff, share), BF),
            pltpu.VMEM((rows, 4 * ff), F32),
            pltpu.SemaphoreType.DMA((copies,)),
        ],
    )(*blocks, w_gate, w_up, w_down)


def load_weights(wg_ref, wu_ref, w, first, sem, index):
    count = w.shape[0]
    ff = wg_ref.shape[1]
    copies = []
    for k, ref in enumerate((wg_ref, wu_ref)):
        source = ref.at[first : first + count, :]
        target = w.at[:, k * ff : (k + 1) * ff]
        copies.append(pltpu.make_async_copy(source, target, sem.at[index + k]))
    return copies


def start_all(copies):
    for copy in copies:
        copy.start()


def wait_all(copies):
    for copy in copies:
        copy.wait()


def hidden_kernel(
    g_ref, wd_ref, wg_ref, wu_ref, *refs
):
    own, side, far = refs[0:3], refs[3:6], refs[6:9]
    gu_ref, near_ref, top_ref, bottom_ref, g, d, w, small, staged, sem = refs[9:]
    groups, span, double = gu_ref.shape
    ff = double // 2
    locs = span // CAP
    unit = 2 * CAP
    cols = g.shape[1]
    wide_cols = top_ref.shape[1]
    first_col = wd_ref.shape[1] - 2 * cols
    tile = 3 * TILE // 2
    windows = [slice(at, min(at + tile, cols)) for at in range(0, cols, tile)]
    steps = len(windows)
    loads = []
    for t, window in enumerate(windows):
        loads.append(pltpu.make_async_copy(g_ref.at[:, window], g.at[:, window], sem.at[3 * t]))
        for h in range(2):
            start = first_col + h * cols + window.start
            source = wd_ref.at[:, start : start + window.stop - window.start]
            target = d.at[h * ff : (h + 1) * ff, window]
            loads.append(pltpu.make_async_copy(source, target, sem.at[3 * t + 1 + h]))
    more = []
    index = 3 * steps
    for k in range(3):
        places = [(own[k], 0), (side[k].at[:span], 1), (far[k], 2), (side[k].at[span:], 3)]
        for source, group in places:
            more.append(pltpu.make_async_copy(source, small.at[k, group], sem.at[index]))
            index += 1
    weights = load_weights(wg_ref, wu_ref, w, wg_ref.shape[0] - wide_cols, sem, index)
    start_all(loads)
    start_all(more)
    start_all(weights)
    total = None
    for t, window in enumerate(windows):
        wait_all(loads[3 * t : 3 * t + 3])
        value = contract_cols(g[:, window], d[:, window])
        total = value if total is None else total + value
    wait_all(more)
    halves = total.reshape(locs, groups * unit, double)
    for group in range(groups):
        first = group * unit
        hidden = (
            halves[:, first : first + CAP, :ff] + halves[:, first + CAP : first + unit, ff:]
        ).reshape(span, ff) + small[2, group]
        gate = hidden * small[0, group]
        up = hidden * small[1, group]
        both = jnp.concatenate([gate, up], axis=1)
        gu_ref[group] = both.astype(BF)
        near_ref[:, group * CAP : (group + 1) * CAP, :] = both.reshape(locs, CAP, double).astype(BF)
    wait_all(weights)
    staged[...] = contract_cols(gu_ref[2], w[...]).astype(BF)
    stores = [
        pltpu.make_async_copy(staged.at[: span // 2], top_ref, sem.at[index + 2]),
        pltpu.make_async_copy(staged.at[span // 2 :], bottom_ref, sem.at[index + 3]),
    ]
    start_all(stores)
    wait_all(stores)


def hidden(g_rows, w_down, w_gate, w_up, own, side, far, wide_cols):
    rows, cols = g_rows.shape
    span, ff = own[0].shape
    groups = rows // 2 // span
    small = lambda *shape: jax.ShapeDtypeStruct(shape, BF)
    return call(
        hidden_kernel,
        "hidden",
        4 * rows * cols * ff + 4 * span * ff * wide_cols,
        2 * (rows * cols + 2 * wide_cols * ff + span * wide_cols),
        in_specs=[ANY] + [HBM] * 3 + [ANY] * 9,
        out_specs=[VMEM, VMEM, ANY, ANY],
        out_shape=[
            small(groups, span, 2 * ff),
            small(span // CAP, groups * CAP, 2 * ff),
            small(span // 2, wide_cols),
            small(span // 2, wide_cols),
        ],
        scratch_shapes=[
            pltpu.VMEM((rows, cols), BF),
            pltpu.VMEM((2 * ff, cols), BF),
            pltpu.VMEM((wide_cols, 2 * ff), BF),
            pltpu.VMEM((3, groups, span, ff), F32),
            pltpu.VMEM((span, wide_cols), BF),
            pltpu.SemaphoreType.DMA((3 * pl.cdiv(cols, 3 * TILE // 2) + 12 + 4,)),
        ],
    )(g_rows, w_down, w_gate, w_up, *own, *side, *far)


def ring_part_kernel(near_ref, wg_ref, wu_ref, out_ref, w, staged, sem):
    rows, ring_cols = out_ref.shape
    loads = load_weights(wg_ref, wu_ref, w, 0, sem, 0)
    start_all(loads)
    wait_all(loads)
    left = near_ref[...].reshape(rows, w.shape[1])
    stores = []
    for c in range(ring_cols // TILE):
        window = slice(c * TILE, (c + 1) * TILE)
        staged[:, window] = contract_cols(left, w[window, :]).astype(BF)
        target = out_ref.at[:, window]
        stores.append(pltpu.make_async_copy(staged.at[:, window], target, sem.at[2 + c]))
        stores[-1].start()
    wait_all(stores)


def ring_part(near, w_gate, w_up, ring_cols):
    locs, depth, double = near.shape
    rows = locs * depth
    return call(
        ring_part_kernel,
        "ring_part",
        2 * rows * double * ring_cols,
        2 * ring_cols * (rows + double),
        in_specs=[VMEM, HBM, HBM],
        out_specs=ANY,
        out_shape=jax.ShapeDtypeStruct((rows, ring_cols), BF),
        scratch_shapes=[
            pltpu.VMEM((ring_cols, double), BF),
            pltpu.VMEM((rows, ring_cols), BF),
            pltpu.SemaphoreType.DMA((2 + ring_cols // TILE,)),
        ],
    )(near, w_gate, w_up)


def side_kernel(gu_ref, wg_ref, wu_ref, top_ref, bottom_ref, next_ref, prev_ref, own_ref, w, held, staged, sem):
    _, span, double = gu_ref.shape
    wide_cols = next_ref.shape[1]
    weights = load_weights(wg_ref, wu_ref, w, wg_ref.shape[0] - wide_cols, sem, 0)
    came = [
        pltpu.make_async_copy(top_ref, held.at[0], sem.at[2]),
        pltpu.make_async_copy(bottom_ref, held.at[1], sem.at[3]),
    ]
    start_all(weights)
    start_all(came)
    wait_all(weights)
    wait_all(came)
    left = jnp.concatenate([gu_ref[1], gu_ref[3], gu_ref[0]], axis=0)
    mid = span // 2
    stores = []
    for c in range(wide_cols // TILE):
        window = slice(c * TILE, (c + 1) * TILE)
        value = contract_cols(left, w[window, :])
        top = held[0, :, window].astype(F32)
        bottom = held[1, :, window].astype(F32)
        staged[0, :mid, window] = (value[:mid] + top).astype(BF)
        staged[0, mid:, window] = value[mid:span].astype(BF)
        staged[1, :mid, window] = value[span : span + mid].astype(BF)
        staged[1, mid:, window] = (value[span + mid : 2 * span] + bottom).astype(BF)
        staged[2, :, window] = value[2 * span :].astype(BF)
        for k, ref in enumerate((next_ref, prev_ref, own_ref)):
            copy = pltpu.make_async_copy(
                staged.at[k, :, window], ref.at[:, window], sem.at[4 + 3 * c + k]
            )
            copy.start()
            stores.append(copy)
    wait_all(stores)


def side_part(gu, w_gate, w_up, top, bottom):
    _, span, double = gu.shape
    wide_cols = top.shape[1]
    return call(
        side_kernel,
        "side_part",
        40 * (6 * span * double * wide_cols),
        40 * (2 * wide_cols * (4 * span + double)),
        in_specs=[VMEM, HBM, HBM, ANY, ANY],
        out_specs=[ANY] * 3,
        out_shape=[jax.ShapeDtypeStruct((span, wide_cols), BF)] * 3,
        scratch_shapes=[
            pltpu.VMEM((wide_cols, double), BF),
            pltpu.VMEM((2, span // 2, wide_cols), BF),
            pltpu.VMEM((3, span, wide_cols), BF),
            pltpu.SemaphoreType.DMA((4 + 3 * (wide_cols // TILE),)),
        ],
    )(gu, w_gate, w_up, top, bottom)


def sum_kernel(a_ref, b_ref, c_ref, out_ref, held, staged, sem):
    locs, _, cols = out_ref.shape
    steps = cols // TILE
    loads, stores = [], []
    for t in range(steps):
        window = slice(t * TILE, (t + 1) * TILE)
        for k, ref in enumerate((a_ref, b_ref, c_ref)):
            loads.append(
                pltpu.make_async_copy(ref.at[:, window], held.at[k, :, window], sem.at[4 * t + k])
            )
    start_all(loads)
    for t in range(steps):
        wait_all(loads[3 * t : 3 * t + 3])
        window = slice(t * TILE, (t + 1) * TILE)
        total = sum(held[k, :, window].astype(F32) for k in range(3))
        staged[:, :, window] = total.reshape(locs, CAP, TILE).astype(BF)
        source = staged.at[:, :, window]
        stores.append(pltpu.make_async_copy(source, out_ref.at[:, :, window], sem.at[4 * t + 3]))
        stores[-1].start()
    wait_all(stores)


def sum_blocks(a, b, c):
    rows, cols = a.shape
    return call(
        sum_kernel,
        "sum_blocks",
        2 * rows * cols,
        8 * rows * cols,
        mib=24,
        in_specs=[HBM, ANY, ANY],
        out_specs=ANY,
        out_shape=jax.ShapeDtypeStruct((rows // CAP, CAP, cols), BF),
        scratch_shapes=[
            pltpu.VMEM((3, rows, cols), BF),
            pltpu.VMEM((rows // CAP, CAP, cols), BF),
            pltpu.SemaphoreType.DMA((4 * (cols // TILE),)),
        ],
    )(a, b, c)


def row_grads_kernel(gu_ref, own_ref, next_ref, top_ref, bottom_ref, prev_ref, gate_ref, up_ref, wide):
    groups, span, double = gu_ref.shape
    ff = double // 2
    locs = span // CAP

    @pl.when(pl.program_id(0) == 0)
    def _():
        zero = jnp.zeros((locs, CAP, ff), F32)
        for group in range(groups):
            both = gu_ref[group].astype(F32).reshape(locs, CAP, double)
            gate, up = both[:, :, :ff], both[:, :, ff:]
            low = jnp.concatenate([gate, zero, up, zero], axis=2)
            high = jnp.concatenate([zero, gate, zero, up], axis=2)
            both = jnp.concatenate([low, high], axis=1).reshape(2 * span, 4 * ff)
            wide[2 * span * group : 2 * span * (group + 1), :] = both.astype(BF)

    x = jnp.concatenate(
        [own_ref[...], next_ref[...], top_ref[...], bottom_ref[...], prev_ref[...]], axis=0
    )
    total = contract_rows(x, wide[...]).astype(BF)
    gate_ref[0] = total[:, :ff]
    gate_ref[1] = total[:, ff : 2 * ff]
    up_ref[0] = total[:, 2 * ff : 3 * ff]
    up_ref[1] = total[:, 3 * ff :]


def row_grads(gu, blocks, share):
    groups, span, double = gu.shape
    ff = double // 2
    rows = 2 * groups * span
    half = blocks[0].shape[1] - share
    out = jax.ShapeDtypeStruct((2, half, ff), BF)
    gate, up = call(
        row_grads_kernel,
        "row_grads",
        8 * rows * half * ff,
        2 * half * (rows + 4 * ff),
        grid=(half // TILE,),
        in_specs=[
            whole(gu.shape),
            *[pl.BlockSpec((b.shape[0], TILE), lambda j: (0, j)) for b in blocks],
        ],
        out_specs=[pl.BlockSpec((2, TILE, ff), lambda j: (0, j, 0))] * 2,
        out_shape=[out, out],
        scratch_shapes=[pltpu.VMEM((rows, 4 * ff), BF)],
    )(gu, *blocks)
    return gate.reshape(2 * half, ff), up.reshape(2 * half, ff)


def down_kernel(g_ref, *refs):
    outers, blocks = refs[:3], refs[3:8]
    out_ref, wide, held, sem = refs[8:]
    own, side, far = outers
    span, ff = own.shape
    locs = span // CAP
    unit = 2 * CAP
    step = pl.program_id(0)
    tile = g_ref.shape[1]
    share = held.shape[1]

    def spread(outer):
        rows = outer.reshape(locs, CAP, ff)
        zero = jnp.zeros_like(rows)
        low = jnp.concatenate([rows, zero], axis=2)
        high = jnp.concatenate([zero, rows], axis=2)
        return jnp.concatenate([low, high], axis=1)

    @pl.when(step == 0)
    def _():
        copies = []
        at = 0
        for k, ref in enumerate(blocks):
            source = ref.at[:, ref.shape[1] - share :]
            copies.append(
                pltpu.make_async_copy(source, held.at[at : at + ref.shape[0], :], sem.at[k])
            )
            at += ref.shape[0]
        start_all(copies)
        rows = []
        for k, outer in enumerate((own[...], side[:span], far[...], side[span:])):
            block = spread(outer).astype(BF)
            wide[:, k * unit : (k + 1) * unit, :] = block
            rows.append(block.reshape(2 * span, 2 * ff))
        wait_all(copies)
        total = contract_rows(jnp.concatenate(rows, axis=0), held[...]).astype(BF)
        out_ref[:, :share] = total[:ff]
        out_ref[:, share : 2 * share] = total[ff:]

    rows = wide[...].reshape(g_ref.shape[0], 2 * ff)
    total = contract_rows(rows, g_ref[...]).astype(BF)
    low = 2 * share + step * tile
    high = low + pl.num_programs(0) * tile
    out_ref[:, pl.ds(pl.multiple_of(low, 128), tile)] = total[:ff]
    out_ref[:, pl.ds(pl.multiple_of(high, 128), tile)] = total[ff:]


def down(outers, blocks, g_rows, share):
    rows, cols = g_rows.shape
    span, ff = outers[0].shape
    width = 2 * (cols + share)
    tile = TILE if cols % TILE == 0 else TILE // 2
    return call(
        down_kernel,
        "down",
        4 * rows * (cols + share) * ff,
        2 * (cols + share) * (rows + 2 * ff),
        grid=(cols // tile,),
        in_specs=[
            pl.BlockSpec((rows, tile), lambda j: (0, j)),
            *[whole(o.shape) for o in outers],
            *[ANY] * 5,
        ],
        out_specs=whole((ff, width)),
        out_shape=jax.ShapeDtypeStruct((ff, width), BF),
        scratch_shapes=[
            pltpu.VMEM((span // CAP, rows * CAP // span, 2 * ff), BF),
            pltpu.VMEM((rows, share), BF),
            pltpu.SemaphoreType.DMA((5,)),
        ],
    )(g_rows, *outers, *blocks)


def fold_kernel(in_ref, own_ref, top_ref, bottom_ref, side_ref):
    _, experts, depth, tile = in_ref.shape
    total = in_ref[0].astype(F32) + in_ref[1].astype(F32)
    for step in range(depth // CAP):
        part = total[:, step * CAP : (step + 1) * CAP, :].reshape(experts * CAP, tile).astype(BF)
        if step == 2:
            top_ref[...] = part[: experts * CAP // 2]
            bottom_ref[...] = part[experts * CAP // 2 :]
        elif step == 0:
            own_ref[...] = part
        else:
            side_ref[step // 2] = part


def fold(home):
    _, experts, depth, width = home.shape
    buf = experts * CAP
    tile = TILE
    return call(
        fold_kernel,
        "fold",
        experts * depth * width,
        6 * experts * depth * width,
        mib=20,
        grid=(width // tile,),
        in_specs=[pl.BlockSpec((2, experts, depth, tile), lambda j: (0, 0, 0, j))],
        out_specs=[
            pl.BlockSpec((buf, tile), lambda j: (0, j)),
            pl.BlockSpec((buf // 2, tile), lambda j: (0, j)),
            pl.BlockSpec((buf // 2, tile), lambda j: (0, j)),
            pl.BlockSpec((2, buf, tile), lambda j: (0, 0, j)),
        ],
        out_shape=[
            jax.ShapeDtypeStruct((buf, width), BF),
            jax.ShapeDtypeStruct((buf // 2, width), BF),
            jax.ShapeDtypeStruct((buf // 2, width), BF),
            jax.ShapeDtypeStruct((2, buf, width), BF),
        ],
    )(home)


def add_kernel(side_ref, top_ref, bottom_ref, next_ref, prev_ref):
    mid = top_ref.shape[0]
    next_ref[:mid] = (side_ref[0, :mid].astype(F32) + top_ref[...].astype(F32)).astype(BF)
    next_ref[mid:] = side_ref[0, mid:]
    prev_ref[:mid] = side_ref[1, :mid]
    prev_ref[mid:] = (side_ref[1, mid:].astype(F32) + bottom_ref[...].astype(F32)).astype(BF)


def add_far(side, top, bottom):
    _, buf, cols = side.shape
    return call(
        add_kernel,
        "add_far",
        buf * cols,
        10 * buf * cols,
        mib=20,
        in_specs=[VMEM] * 3,
        out_specs=[VMEM] * 2,
        out_shape=[jax.ShapeDtypeStruct((buf, cols), BF)] * 2,
    )(side, top, bottom)


def combine_kernel(table_ref, own_ref, left_ref, right_ref, wide_ref, out_ref, ring, wide, staged, sem):
    buf = table_ref.shape[0]
    ring_cols = ring.shape[1]
    locs, _, wide_cols = wide.shape
    loads, stores = [], []

    def add(source, target):
        loads.append(pltpu.make_async_copy(source, target, sem.at[len(loads)]))

    for k, ref in enumerate((own_ref, left_ref, right_ref)):
        add(ref, ring.at[k * buf : (k + 1) * buf, :])
    for first in range(0, wide_cols, TILE):
        window = slice(first, first + TILE)
        add(wide_ref.at[:, :, window], wide.at[:, :, window])
    start_all(loads)
    table = table_ref[...]
    twice = jnp.concatenate([table] * 2, axis=0)
    thrice = jnp.concatenate([table] * 3, axis=0)
    wait_all(loads[:3])
    for t in range((ring_cols + wide_cols) // TILE):
        window = slice(t * TILE, (t + 1) * TILE)
        first = t * TILE - ring_cols
        if first < 0:
            total = contract_rows(thrice, ring[:, window])
        else:
            loads[3 + first // TILE].wait()
            rows = wide[:, :, first : first + TILE].astype(F32).reshape(locs * CAP, TILE).astype(BF)
            total = contract_rows(twice, rows)
        staged[:, window] = total.astype(BF)
        target = out_ref.at[:, window]
        index = len(loads) + len(stores)
        stores.append(pltpu.make_async_copy(staged.at[:, window], target, sem.at[index]))
        stores[-1].start()
    wait_all(stores)


def combine(table, own, left, right, wide):
    buf, tok = table.shape
    ring_cols, wide_cols = left.shape[1], wide.shape[2]
    width = ring_cols + wide_cols
    return call(
        combine_kernel,
        "combine",
        2 * tok * buf * width,
        2 * width * (tok + 2 * buf),
        mib=24,
        in_specs=[VMEM, HBM, ANY, ANY, ANY],
        out_specs=ANY,
        out_shape=jax.ShapeDtypeStruct((tok, width), BF),
        scratch_shapes=[
            pltpu.VMEM((3 * buf, ring_cols), BF),
            pltpu.VMEM((wide.shape[0], CAP, wide_cols), BF),
            pltpu.VMEM((tok, width), BF),
            pltpu.SemaphoreType.DMA((3 + wide_cols // TILE + width // TILE,)),
        ],
    )(table, own, left, right, wide)


def over_loc(a):
    return lax.all_to_all(a, "loc", split_axis=0, concat_axis=0, tiled=True)


def shift(a, step):
    groups = lax.axis_size("grp")
    return lax.ppermute(a, "grp", [(i, (i + step) % groups) for i in range(groups)])


def ring_gather(own):
    mid = own.shape[0] // 2
    before, after = shift(own, 1), shift(own, -1)
    return [own, after, shift(before[:mid], 1), shift(after[mid:], -1), before]


def body(tokens, grad_out, expert_ids, route_weight, gate_weight, up_weight, down_weight):
    groups = lax.axis_size("grp")
    locs = lax.axis_size("loc")
    experts = locs // 2
    width = tokens.shape[1]
    buf = experts * CAP
    unit = 2 * CAP
    share = 768
    ring_cols = 2560
    wide_cols = width - ring_cols

    w_gate, w_up, w_down = gate_weight[0], up_weight[0], down_weight[0]

    table, g_send, xg_send = dispatch(
        expert_ids.T, route_weight.T, grad_out, tokens, experts, share
    )
    g_blocks = ring_gather(g_send)
    xg = over_loc(xg_send.reshape(locs, unit, xg_send.shape[3]))
    xg, *g_blocks = lax.optimization_barrier((xg, *g_blocks))
    blocks = ring_gather(xg.reshape(locs * unit, xg.shape[2]))
    g_out = regroup(g_blocks)
    g_rows = over_loc(g_out.reshape(locs, groups * unit, g_out.shape[3]))
    g_rows = g_rows.reshape(locs * groups * unit, g_out.shape[3])

    own, after, top, bottom, before = blocks
    *pre_own, outer_own = pre([own], w_gate, w_up, w_down, share)
    *pre_side, outer_side = pre([after, before], w_gate, w_up, w_down, share)
    *pre_far, outer_far = pre([top, bottom], w_gate, w_up, w_down, share)
    gu, near, far_top, far_bottom = hidden(
        g_rows, w_down, w_gate, w_up, pre_own, pre_side, pre_far, wide_cols
    )

    came_top, came_bottom = shift(far_top, 1), shift(far_bottom, -1)
    part_ring = ring_part(near, w_gate, w_up, ring_cols)
    part_ring, gu = lax.optimization_barrier((part_ring, gu))
    home_ring = over_loc(part_ring.reshape(locs, groups * CAP, ring_cols))
    part_next, part_prev, part_own = side_part(gu, w_gate, w_up, came_top, came_bottom)
    from_before, from_after = shift(part_next, 1), shift(part_prev, -1)

    outers = (outer_own, outer_side, outer_far)
    part_own, gu, outers = lax.optimization_barrier((part_own, gu, outers))
    gate_grad, up_grad = row_grads(gu, blocks, share)
    down_grad = down(outers, blocks, g_rows, share)
    part_own, gate_grad, up_grad, down_grad = lax.optimization_barrier(
        (part_own, gate_grad, up_grad, down_grad)
    )
    fold_own, fold_top, fold_bottom, fold_side = fold(
        home_ring.reshape(2, experts, groups * CAP, ring_cols)
    )
    home_wide = over_loc(sum_blocks(part_own, from_before, from_after))
    fold_next, fold_prev = add_far(fold_side, shift(fold_top, 1), shift(fold_bottom, -1))
    tokens_grad = combine(table, fold_own, shift(fold_next, 1), shift(fold_prev, -1), home_wide)
    return (tokens_grad, gate_grad[None], up_grad[None], down_grad[None])


def solution(mesh):
    in_specs = (
        P(("grp", "loc"), None),
        P(("grp", "loc"), None),
        P(("grp", "loc"), None),
        P(("grp", "loc"), None),
        P("loc", None, "grp"),
        P("loc", None, "grp"),
        P("loc", "grp", None),
    )
    out_specs = (
        P(("grp", "loc"), None),
        P("loc", None, "grp"),
        P("loc", None, "grp"),
        P("loc", "grp", None),
    )
    return jax.shard_map(body, mesh=mesh, in_specs=in_specs, out_specs=out_specs, check_vma=False)
```

```python
import functools

import jax
import jax.numpy as jnp
from jax import lax
from jax.experimental import pallas as pl
from jax.experimental.pallas import tpu as pltpu
from jax.sharding import PartitionSpec as P

CAP = 4
BF = jnp.bfloat16
F32 = jnp.float32
TILE = 512
ANY = pl.BlockSpec(memory_space=pl.ANY)
VMEM = pl.BlockSpec(memory_space=pltpu.VMEM)
HBM = pl.BlockSpec(memory_space=pltpu.HBM)


def contract_rows(left, right):
    return lax.dot_general(left, right, (((0,), (0,)), ((), ())), preferred_element_type=F32)


def contract_cols(left, right):
    return lax.dot_general(left, right, (((1,), (1,)), ((), ())), preferred_element_type=F32)


def whole(shape):
    return pl.BlockSpec(shape, lambda *_: (0,) * len(shape))


def call(kernel, name, flops, nbytes, mib=56, **kwargs):
    return pl.pallas_call(
        kernel,
        name=name,
        compiler_params=pltpu.CompilerParams(vmem_limit_bytes=mib << 20),
        cost_estimate=pl.CostEstimate(flops=flops, bytes_accessed=nbytes, transcendentals=0),
        **kwargs,
    )


def dispatch_kernel(ids_ref, w_ref, g_ref, t_ref, table_ref, ring_ref, out_ref, held, tokens, staged, sem):
    load = pltpu.make_async_copy(g_ref, held, sem.at[0])
    load.start()
    load_tokens = pltpu.make_async_copy(t_ref, tokens, sem.at[1])
    load_tokens.start()
    topk, tok = ids_ref.shape
    buf = table_ref.shape[0]
    unit = 2 * CAP
    experts = out_ref.shape[1]
    cols = ring_ref.shape[1]
    half = tokens.shape[1] // 2
    share = half - cols

    def tables(count, per_expert):
        slot_row = lax.broadcasted_iota(jnp.int32, (count, tok), 0)
        expert = lax.div(slot_row, per_expert)
        weights = w_ref[...].astype(F32)
        chosen = jnp.zeros((count, tok), F32)
        weight = jnp.zeros((count, tok), F32)
        for k in range(topk):
            hit = ids_ref[k : k + 1, :] == expert
            chosen = jnp.where(hit, 1.0, chosen)
            weight = jnp.where(hit, weights[k : k + 1, :], weight)
        before = lax.broadcasted_iota(jnp.int32, (tok, tok), 0)
        after = lax.broadcasted_iota(jnp.int32, (tok, tok), 1)
        earlier = jnp.where(before < after, 1.0, 0.0).astype(BF)
        slot = jnp.dot(chosen.astype(BF), earlier, preferred_element_type=F32)
        mine = (chosen > 0.5) & (slot == lax.rem(slot_row, CAP).astype(F32))
        return jnp.where(mine, 1.0, 0.0), jnp.where(mine, weight, 0.0), slot_row

    table_ref[...] = tables(buf, CAP)[0].astype(BF)
    table, weighted, slot_row = tables(2 * buf, unit)
    low = lax.rem(slot_row, unit) < CAP
    pick = jnp.concatenate(
        [jnp.where(low, table, 0.0).astype(BF), jnp.where(low, 0.0, table).astype(BF)], axis=1
    )
    both = jnp.concatenate(
        [jnp.where(low, weighted, 0.0).astype(BF), jnp.where(low, 0.0, weighted).astype(BF)], axis=1
    )
    load.wait()

    def rows(left, source, first, second, count):
        parts = jnp.concatenate(
            [source[:, first : first + count], source[:, second : second + count]], axis=0
        )
        return jnp.dot(left, parts, preferred_element_type=F32).astype(BF)

    staged[:, :, half:] = rows(both, held, 0, share, share).reshape(experts, unit, share)
    part = TILE // 2
    for first in range(0, cols, part):
        start = 2 * share + first
        ring_ref[:, first : first + part] = rows(both, held, start, start + cols, part)
    load_tokens.wait()
    for first in range(0, half, TILE):
        value = rows(pick, tokens, first, half + first, TILE)
        staged[:, :, first : first + TILE] = value.reshape(experts, unit, TILE)
    stores = [pltpu.make_async_copy(staged, out_ref.at[h], sem.at[2 + h]) for h in range(2)]
    for store in stores:
        store.start()
    for store in stores:
        store.wait()


def dispatch(ids, weights, grad_out, tokens, experts, share):
    tok, width = grad_out.shape
    buf = experts * CAP
    unit = 2 * CAP
    half = width // 2
    small = lambda *shape: jax.ShapeDtypeStruct(shape, BF)
    return call(
        dispatch_kernel,
        "dispatch",
        8 * tok * buf * width,
        2 * width * (2 * tok + 3 * buf),
        in_specs=[VMEM, VMEM, ANY, ANY],
        out_specs=[VMEM, VMEM, ANY],
        out_shape=[
            small(buf, tok),
            small(2 * buf, half - share),
            small(2, experts, unit, half + share),
        ],
        scratch_shapes=[
            pltpu.VMEM((tok, width), BF),
            pltpu.VMEM((tok, width), BF),
            pltpu.VMEM((experts, unit, half + share), BF),
            pltpu.SemaphoreType.DMA((4,)),
        ],
    )(ids, weights, grad_out, tokens)


def regroup_kernel(own_ref, next_ref, top_ref, bottom_ref, prev_ref, out_ref, held, sem):
    experts, unit, _ = own_ref.shape
    parts = 4
    size = experts // parts
    loads, stores = [], []
    for p in range(parts):
        window = slice(p * size, (p + 1) * size)
        if p < parts // 2:
            far = top_ref.at[window]
        else:
            far = bottom_ref.at[p * size - experts // 2 : (p + 1) * size - experts // 2]
        sources = [own_ref.at[window], next_ref.at[window], far, prev_ref.at[window]]
        for k, source in enumerate(sources):
            target = held.at[window, k * unit : (k + 1) * unit, :]
            loads.append(pltpu.make_async_copy(source, target, sem.at[p * 4 + k]))
            loads[-1].start()
    for p in range(parts):
        window = slice(p * size, (p + 1) * size)
        for k in range(4):
            loads[p * 4 + k].wait()
        for h in range(2):
            index = parts * 4 + 2 * p + h
            stores.append(pltpu.make_async_copy(held.at[window], out_ref.at[h, window], sem.at[index]))
            stores[-1].start()
    for store in stores:
        store.wait()


def regroup(blocks):
    count, cols = blocks[0].shape
    unit = 2 * CAP
    experts = count // unit
    return call(
        regroup_kernel,
        "regroup",
        0,
        24 * count * cols,
        in_specs=[ANY] * 5,
        out_specs=ANY,
        out_shape=jax.ShapeDtypeStruct((2, experts, 4 * unit, cols), BF),
        scratch_shapes=[
            pltpu.VMEM((experts, 4 * unit, cols), BF),
            pltpu.SemaphoreType.DMA((24,)),
        ],
    )(*[b.reshape(b.shape[0] // unit, unit, cols) for b in blocks])


def pre_kernel(count, *refs):
    x_refs = refs[:count]
    wg_ref, wu_ref, wd_ref, slope_ref, swish_ref, part_ref, outer_ref, x, w, d, acc, sem = refs[count:]
    rows, cols = x.shape
    ff = w.shape[2] // 4
    share = d.shape[1]
    half = cols - share
    steps = half // TILE
    copies = [[] for _ in range(steps + 1)]
    index = 0

    def add(step, source, target):
        nonlocal index
        copies[step].append(pltpu.make_async_copy(source, target, sem.at[index]))
        index += 1

    for t in range(steps + 1):
        window = slice(t * TILE, (t + 1) * TILE) if t < steps else slice(half, cols)
        at = 0
        for ref in x_refs:
            add(t, ref.at[:, window], x.at[at : at + ref.shape[0], window])
            at += ref.shape[0]
        if t < steps:
            for k, ref in enumerate((wg_ref, wu_ref)):
                for h in range(2):
                    lane = (2 * k + h) * ff
                    source = ref.at[h * half + t * TILE : h * half + (t + 1) * TILE, :]
                    add(t, source, w.at[t, :, lane : lane + ff])
        else:
            for h in range(2):
                source = wd_ref.at[:, h * share : (h + 1) * share]
                add(t, source, d.at[h * ff : (h + 1) * ff, :])
    for group in copies:
        for copy in group:
            copy.start()
    for t in range(steps):
        for copy in copies[t]:
            copy.wait()
        value = jnp.dot(x[:, t * TILE : (t + 1) * TILE], w[t], preferred_element_type=F32)
        if t == 0:
            acc[...] = value
        else:
            acc[...] += value
    for copy in copies[steps]:
        copy.wait()

    def fold_halves(value):
        value = value.reshape(rows // (2 * CAP), 2 * CAP, 2 * ff)
        return (value[:, :CAP, :ff] + value[:, CAP:, ff:]).reshape(rows // 2, ff)

    part_ref[...] = fold_halves(contract_cols(x[:, half:], d[...]))
    gate = fold_halves(acc[:, : 2 * ff])
    up = fold_halves(acc[:, 2 * ff :])
    sig = 1.0 / (1.0 + jnp.exp(-gate))
    swish = gate * sig
    slope_ref[...] = up * sig * (1.0 + gate * (1.0 - sig))
    swish_ref[...] = swish
    outer_ref[...] = swish * up


def pre(blocks, w_gate, w_up, w_down, share):
    cols = blocks[0].shape[1]
    rows = sum(b.shape[0] for b in blocks)
    ff = w_gate.shape[1]
    steps = (cols - share) // TILE
    copies = (len(blocks) + 4) * steps + len(blocks) + 2
    return call(
        functools.partial(pre_kernel, len(blocks)),
        "pre",
        200 * (8 * rows * cols * ff),
        200 * (2 * cols * (rows + 4 * ff)),
        in_specs=[ANY] * len(blocks) + [HBM] * 3,
        out_specs=[VMEM] * 4,
        out_shape=[jax.ShapeDtypeStruct((rows // 2, ff), F32)] * 4,
        scratch_shapes=[
            pltpu.VMEM((rows, cols), BF),
            pltpu.VMEM((steps, TILE, 4 * ff), BF),
            pltpu.VMEM((2 * ff, share), BF),
            pltpu.VMEM((rows, 4 * ff), F32),
            pltpu.SemaphoreType.DMA((copies,)),
        ],
    )(*blocks, w_gate, w_up, w_down)


def load_weights(wg_ref, wu_ref, w, first, sem, index):
    count = w.shape[0]
    ff = wg_ref.shape[1]
    copies = []
    for k, ref in enumerate((wg_ref, wu_ref)):
        source = ref.at[first : first + count, :]
        target = w.at[:, k * ff : (k + 1) * ff]
        copies.append(pltpu.make_async_copy(source, target, sem.at[index + k]))
    return copies


def start_all(copies):
    for copy in copies:
        copy.start()


def wait_all(copies):
    for copy in copies:
        copy.wait()


def hidden_kernel(
    g_ref, wd_ref, wg_ref, wu_ref, *refs
):
    own, side, far = refs[0:3], refs[3:6], refs[6:9]
    gu_ref, near_ref, top_ref, bottom_ref, g, d, w, small, staged, sem = refs[9:]
    groups, span, double = gu_ref.shape
    ff = double // 2
    locs = span // CAP
    unit = 2 * CAP
    cols = g.shape[1]
    wide_cols = top_ref.shape[1]
    first_col = wd_ref.shape[1] - 2 * cols
    tile = 3 * TILE // 2
    windows = [slice(at, min(at + tile, cols)) for at in range(0, cols, tile)]
    steps = len(windows)
    loads = []
    for t, window in enumerate(windows):
        loads.append(pltpu.make_async_copy(g_ref.at[:, window], g.at[:, window], sem.at[3 * t]))
        for h in range(2):
            start = first_col + h * cols + window.start
            source = wd_ref.at[:, start : start + window.stop - window.start]
            target = d.at[h * ff : (h + 1) * ff, window]
            loads.append(pltpu.make_async_copy(source, target, sem.at[3 * t + 1 + h]))
    more = []
    index = 3 * steps
    for k in range(3):
        places = [(own[k], 0), (side[k].at[:span], 1), (far[k], 2), (side[k].at[span:], 3)]
        for source, group in places:
            more.append(pltpu.make_async_copy(source, small.at[k, group], sem.at[index]))
            index += 1
    weights = load_weights(wg_ref, wu_ref, w, wg_ref.shape[0] - wide_cols, sem, index)
    start_all(loads)
    start_all(more)
    start_all(weights)
    total = None
    for t, window in enumerate(windows):
        wait_all(loads[3 * t : 3 * t + 3])
        value = contract_cols(g[:, window], d[:, window])
        total = value if total is None else total + value
    wait_all(more)
    halves = total.reshape(locs, groups * unit, double)
    for group in range(groups):
        first = group * unit
        hidden = (
            halves[:, first : first + CAP, :ff] + halves[:, first + CAP : first + unit, ff:]
        ).reshape(span, ff) + small[2, group]
        gate = hidden * small[0, group]
        up = hidden * small[1, group]
        both = jnp.concatenate([gate, up], axis=1)
        gu_ref[group] = both.astype(BF)
        near_ref[:, group * CAP : (group + 1) * CAP, :] = both.reshape(locs, CAP, double).astype(BF)
    wait_all(weights)
    staged[...] = contract_cols(gu_ref[2], w[...]).astype(BF)
    stores = [
        pltpu.make_async_copy(staged.at[: span // 2], top_ref, sem.at[index + 2]),
        pltpu.make_async_copy(staged.at[span // 2 :], bottom_ref, sem.at[index + 3]),
    ]
    start_all(stores)
    wait_all(stores)


def hidden(g_rows, w_down, w_gate, w_up, own, side, far, wide_cols):
    rows, cols = g_rows.shape
    span, ff = own[0].shape
    groups = rows // 2 // span
    small = lambda *shape: jax.ShapeDtypeStruct(shape, BF)
    return call(
        hidden_kernel,
        "hidden",
        4 * rows * cols * ff + 4 * span * ff * wide_cols,
        2 * (rows * cols + 2 * wide_cols * ff + span * wide_cols),
        in_specs=[ANY] + [HBM] * 3 + [ANY] * 9,
        out_specs=[VMEM, VMEM, ANY, ANY],
        out_shape=[
            small(groups, span, 2 * ff),
            small(span // CAP, groups * CAP, 2 * ff),
            small(span // 2, wide_cols),
            small(span // 2, wide_cols),
        ],
        scratch_shapes=[
            pltpu.VMEM((rows, cols), BF),
            pltpu.VMEM((2 * ff, cols), BF),
            pltpu.VMEM((wide_cols, 2 * ff), BF),
            pltpu.VMEM((3, groups, span, ff), F32),
            pltpu.VMEM((span, wide_cols), BF),
            pltpu.SemaphoreType.DMA((3 * pl.cdiv(cols, 3 * TILE // 2) + 12 + 4,)),
        ],
    )(g_rows, w_down, w_gate, w_up, *own, *side, *far)


def ring_part_kernel(near_ref, wg_ref, wu_ref, out_ref, w, staged, sem):
    rows, ring_cols = out_ref.shape
    loads = load_weights(wg_ref, wu_ref, w, 0, sem, 0)
    start_all(loads)
    wait_all(loads)
    left = near_ref[...].reshape(rows, w.shape[1])
    stores = []
    for c in range(ring_cols // TILE):
        window = slice(c * TILE, (c + 1) * TILE)
        staged[:, window] = contract_cols(left, w[window, :]).astype(BF)
        target = out_ref.at[:, window]
        stores.append(pltpu.make_async_copy(staged.at[:, window], target, sem.at[2 + c]))
        stores[-1].start()
    wait_all(stores)


def ring_part(near, w_gate, w_up, ring_cols):
    locs, depth, double = near.shape
    rows = locs * depth
    return call(
        ring_part_kernel,
        "ring_part",
        2 * rows * double * ring_cols,
        2 * ring_cols * (rows + double),
        in_specs=[VMEM, HBM, HBM],
        out_specs=ANY,
        out_shape=jax.ShapeDtypeStruct((rows, ring_cols), BF),
        scratch_shapes=[
            pltpu.VMEM((ring_cols, double), BF),
            pltpu.VMEM((rows, ring_cols), BF),
            pltpu.SemaphoreType.DMA((2 + ring_cols // TILE,)),
        ],
    )(near, w_gate, w_up)


def side_kernel(gu_ref, wg_ref, wu_ref, top_ref, bottom_ref, next_ref, prev_ref, own_ref, w, held, staged, sem):
    _, span, double = gu_ref.shape
    wide_cols = next_ref.shape[1]
    weights = load_weights(wg_ref, wu_ref, w, wg_ref.shape[0] - wide_cols, sem, 0)
    came = [
        pltpu.make_async_copy(top_ref, held.at[0], sem.at[2]),
        pltpu.make_async_copy(bottom_ref, held.at[1], sem.at[3]),
    ]
    start_all(weights)
    start_all(came)
    wait_all(weights)
    wait_all(came)
    left = jnp.concatenate([gu_ref[1], gu_ref[3], gu_ref[0]], axis=0)
    mid = span // 2
    stores = []
    for c in range(wide_cols // TILE):
        window = slice(c * TILE, (c + 1) * TILE)
        value = contract_cols(left, w[window, :])
        top = held[0, :, window].astype(F32)
        bottom = held[1, :, window].astype(F32)
        staged[0, :mid, window] = (value[:mid] + top).astype(BF)
        staged[0, mid:, window] = value[mid:span].astype(BF)
        staged[1, :mid, window] = value[span : span + mid].astype(BF)
        staged[1, mid:, window] = (value[span + mid : 2 * span] + bottom).astype(BF)
        staged[2, :, window] = value[2 * span :].astype(BF)
        for k, ref in enumerate((next_ref, prev_ref, own_ref)):
            copy = pltpu.make_async_copy(
                staged.at[k, :, window], ref.at[:, window], sem.at[4 + 3 * c + k]
            )
            copy.start()
            stores.append(copy)
    wait_all(stores)


def side_part(gu, w_gate, w_up, top, bottom):
    _, span, double = gu.shape
    wide_cols = top.shape[1]
    return call(
        side_kernel,
        "side_part",
        40 * (6 * span * double * wide_cols),
        40 * (2 * wide_cols * (4 * span + double)),
        in_specs=[VMEM, HBM, HBM, ANY, ANY],
        out_specs=[ANY] * 3,
        out_shape=[jax.ShapeDtypeStruct((span, wide_cols), BF)] * 3,
        scratch_shapes=[
            pltpu.VMEM((wide_cols, double), BF),
            pltpu.VMEM((2, span // 2, wide_cols), BF),
            pltpu.VMEM((3, span, wide_cols), BF),
            pltpu.SemaphoreType.DMA((4 + 3 * (wide_cols // TILE),)),
        ],
    )(gu, w_gate, w_up, top, bottom)


def sum_kernel(a_ref, b_ref, c_ref, out_ref, held, staged, sem):
    locs, _, cols = out_ref.shape
    steps = cols // TILE
    loads, stores = [], []
    for t in range(steps):
        window = slice(t * TILE, (t + 1) * TILE)
        for k, ref in enumerate((a_ref, b_ref, c_ref)):
            loads.append(
                pltpu.make_async_copy(ref.at[:, window], held.at[k, :, window], sem.at[4 * t + k])
            )
    start_all(loads)
    for t in range(steps):
        wait_all(loads[3 * t : 3 * t + 3])
        window = slice(t * TILE, (t + 1) * TILE)
        total = sum(held[k, :, window].astype(F32) for k in range(3))
        staged[:, :, window] = total.reshape(locs, CAP, TILE).astype(BF)
        source = staged.at[:, :, window]
        stores.append(pltpu.make_async_copy(source, out_ref.at[:, :, window], sem.at[4 * t + 3]))
        stores[-1].start()
    wait_all(stores)


def sum_blocks(a, b, c):
    rows, cols = a.shape
    return call(
        sum_kernel,
        "sum_blocks",
        2 * rows * cols,
        8 * rows * cols,
        mib=24,
        in_specs=[HBM, ANY, ANY],
        out_specs=ANY,
        out_shape=jax.ShapeDtypeStruct((rows // CAP, CAP, cols), BF),
        scratch_shapes=[
            pltpu.VMEM((3, rows, cols), BF),
            pltpu.VMEM((rows // CAP, CAP, cols), BF),
            pltpu.SemaphoreType.DMA((4 * (cols // TILE),)),
        ],
    )(a, b, c)


def row_grads_kernel(gu_ref, own_ref, next_ref, top_ref, bottom_ref, prev_ref, gate_ref, up_ref, wide):
    groups, span, double = gu_ref.shape
    ff = double // 2
    locs = span // CAP

    @pl.when(pl.program_id(0) == 0)
    def _():
        zero = jnp.zeros((locs, CAP, ff), F32)
        for group in range(groups):
            both = gu_ref[group].astype(F32).reshape(locs, CAP, double)
            gate, up = both[:, :, :ff], both[:, :, ff:]
            low = jnp.concatenate([gate, zero, up, zero], axis=2)
            high = jnp.concatenate([zero, gate, zero, up], axis=2)
            both = jnp.concatenate([low, high], axis=1).reshape(2 * span, 4 * ff)
            wide[2 * span * group : 2 * span * (group + 1), :] = both.astype(BF)

    x = jnp.concatenate(
        [own_ref[...], next_ref[...], top_ref[...], bottom_ref[...], prev_ref[...]], axis=0
    )
    total = contract_rows(x, wide[...]).astype(BF)
    gate_ref[0] = total[:, :ff]
    gate_ref[1] = total[:, ff : 2 * ff]
    up_ref[0] = total[:, 2 * ff : 3 * ff]
    up_ref[1] = total[:, 3 * ff :]


def row_grads(gu, blocks, share):
    groups, span, double = gu.shape
    ff = double // 2
    rows = 2 * groups * span
    half = blocks[0].shape[1] - share
    out = jax.ShapeDtypeStruct((2, half, ff), BF)
    gate, up = call(
        row_grads_kernel,
        "row_grads",
        8 * rows * half * ff,
        2 * half * (rows + 4 * ff),
        grid=(half // TILE,),
        in_specs=[
            whole(gu.shape),
            *[pl.BlockSpec((b.shape[0], TILE), lambda j: (0, j)) for b in blocks],
        ],
        out_specs=[pl.BlockSpec((2, TILE, ff), lambda j: (0, j, 0))] * 2,
        out_shape=[out, out],
        scratch_shapes=[pltpu.VMEM((rows, 4 * ff), BF)],
    )(gu, *blocks)
    return gate.reshape(2 * half, ff), up.reshape(2 * half, ff)


def down_kernel(g_ref, *refs):
    outers, blocks = refs[:3], refs[3:8]
    out_ref, wide, held, sem = refs[8:]
    own, side, far = outers
    span, ff = own.shape
    locs = span // CAP
    unit = 2 * CAP
    step = pl.program_id(0)
    tile = g_ref.shape[1]
    share = held.shape[1]

    def spread(outer):
        rows = outer.reshape(locs, CAP, ff)
        zero = jnp.zeros_like(rows)
        low = jnp.concatenate([rows, zero], axis=2)
        high = jnp.concatenate([zero, rows], axis=2)
        return jnp.concatenate([low, high], axis=1)

    @pl.when(step == 0)
    def _():
        copies = []
        at = 0
        for k, ref in enumerate(blocks):
            source = ref.at[:, ref.shape[1] - share :]
            copies.append(
                pltpu.make_async_copy(source, held.at[at : at + ref.shape[0], :], sem.at[k])
            )
            at += ref.shape[0]
        start_all(copies)
        rows = []
        for k, outer in enumerate((own[...], side[:span], far[...], side[span:])):
            block = spread(outer).astype(BF)
            wide[:, k * unit : (k + 1) * unit, :] = block
            rows.append(block.reshape(2 * span, 2 * ff))
        wait_all(copies)
        total = contract_rows(jnp.concatenate(rows, axis=0), held[...]).astype(BF)
        out_ref[:, :share] = total[:ff]
        out_ref[:, share : 2 * share] = total[ff:]

    rows = wide[...].reshape(g_ref.shape[0], 2 * ff)
    total = contract_rows(rows, g_ref[...]).astype(BF)
    low = 2 * share + step * tile
    high = low + pl.num_programs(0) * tile
    out_ref[:, pl.ds(pl.multiple_of(low, 128), tile)] = total[:ff]
    out_ref[:, pl.ds(pl.multiple_of(high, 128), tile)] = total[ff:]


def down(outers, blocks, g_rows, share):
    rows, cols = g_rows.shape
    span, ff = outers[0].shape
    width = 2 * (cols + share)
    tile = TILE if cols % TILE == 0 else TILE // 2
    return call(
        down_kernel,
        "down",
        4 * rows * (cols + share) * ff,
        2 * (cols + share) * (rows + 2 * ff),
        grid=(cols // tile,),
        in_specs=[
            pl.BlockSpec((rows, tile), lambda j: (0, j)),
            *[whole(o.shape) for o in outers],
            *[ANY] * 5,
        ],
        out_specs=whole((ff, width)),
        out_shape=jax.ShapeDtypeStruct((ff, width), BF),
        scratch_shapes=[
            pltpu.VMEM((span // CAP, rows * CAP // span, 2 * ff), BF),
            pltpu.VMEM((rows, share), BF),
            pltpu.SemaphoreType.DMA((5,)),
        ],
    )(g_rows, *outers, *blocks)


def fold_kernel(in_ref, own_ref, top_ref, bottom_ref, side_ref):
    _, experts, depth, tile = in_ref.shape
    total = in_ref[0].astype(F32) + in_ref[1].astype(F32)
    for step in range(depth // CAP):
        part = total[:, step * CAP : (step + 1) * CAP, :].reshape(experts * CAP, tile).astype(BF)
        if step == 2:
            top_ref[...] = part[: experts * CAP // 2]
            bottom_ref[...] = part[experts * CAP // 2 :]
        elif step == 0:
            own_ref[...] = part
        else:
            side_ref[step // 2] = part


def fold(home):
    _, experts, depth, width = home.shape
    buf = experts * CAP
    tile = TILE
    return call(
        fold_kernel,
        "fold",
        experts * depth * width,
        6 * experts * depth * width,
        mib=20,
        grid=(width // tile,),
        in_specs=[pl.BlockSpec((2, experts, depth, tile), lambda j: (0, 0, 0, j))],
        out_specs=[
            pl.BlockSpec((buf, tile), lambda j: (0, j)),
            pl.BlockSpec((buf // 2, tile), lambda j: (0, j)),
            pl.BlockSpec((buf // 2, tile), lambda j: (0, j)),
            pl.BlockSpec((2, buf, tile), lambda j: (0, 0, j)),
        ],
        out_shape=[
            jax.ShapeDtypeStruct((buf, width), BF),
            jax.ShapeDtypeStruct((buf // 2, width), BF),
            jax.ShapeDtypeStruct((buf // 2, width), BF),
            jax.ShapeDtypeStruct((2, buf, width), BF),
        ],
    )(home)


def add_kernel(side_ref, top_ref, bottom_ref, next_ref, prev_ref):
    mid = top_ref.shape[0]
    next_ref[:mid] = (side_ref[0, :mid].astype(F32) + top_ref[...].astype(F32)).astype(BF)
    next_ref[mid:] = side_ref[0, mid:]
    prev_ref[:mid] = side_ref[1, :mid]
    prev_ref[mid:] = (side_ref[1, mid:].astype(F32) + bottom_ref[...].astype(F32)).astype(BF)


def add_far(side, top, bottom):
    _, buf, cols = side.shape
    return call(
        add_kernel,
        "add_far",
        buf * cols,
        10 * buf * cols,
        mib=20,
        in_specs=[VMEM] * 3,
        out_specs=[VMEM] * 2,
        out_shape=[jax.ShapeDtypeStruct((buf, cols), BF)] * 2,
    )(side, top, bottom)


def combine_kernel(table_ref, own_ref, left_ref, right_ref, wide_ref, out_ref, ring, wide, staged, sem):
    buf = table_ref.shape[0]
    ring_cols = ring.shape[1]
    locs, _, wide_cols = wide.shape
    loads, stores = [], []

    def add(source, target):
        loads.append(pltpu.make_async_copy(source, target, sem.at[len(loads)]))

    for k, ref in enumerate((own_ref, left_ref, right_ref)):
        add(ref, ring.at[k * buf : (k + 1) * buf, :])
    for first in range(0, wide_cols, TILE):
        window = slice(first, first + TILE)
        add(wide_ref.at[:, :, window], wide.at[:, :, window])
    start_all(loads)
    table = table_ref[...]
    twice = jnp.concatenate([table] * 2, axis=0)
    thrice = jnp.concatenate([table] * 3, axis=0)
    wait_all(loads[:3])
    for t in range((ring_cols + wide_cols) // TILE):
        window = slice(t * TILE, (t + 1) * TILE)
        first = t * TILE - ring_cols
        if first < 0:
            total = contract_rows(thrice, ring[:, window])
        else:
            loads[3 + first // TILE].wait()
            rows = wide[:, :, first : first + TILE].astype(F32).reshape(locs * CAP, TILE).astype(BF)
            total = contract_rows(twice, rows)
        staged[:, window] = total.astype(BF)
        target = out_ref.at[:, window]
        index = len(loads) + len(stores)
        stores.append(pltpu.make_async_copy(staged.at[:, window], target, sem.at[index]))
        stores[-1].start()
    wait_all(stores)


def combine(table, own, left, right, wide):
    buf, tok = table.shape
    ring_cols, wide_cols = left.shape[1], wide.shape[2]
    width = ring_cols + wide_cols
    return call(
        combine_kernel,
        "combine",
        2 * tok * buf * width,
        2 * width * (tok + 2 * buf),
        mib=24,
        in_specs=[VMEM, HBM, ANY, ANY, ANY],
        out_specs=ANY,
        out_shape=jax.ShapeDtypeStruct((tok, width), BF),
        scratch_shapes=[
            pltpu.VMEM((3 * buf, ring_cols), BF),
            pltpu.VMEM((wide.shape[0], CAP, wide_cols), BF),
            pltpu.VMEM((tok, width), BF),
            pltpu.SemaphoreType.DMA((3 + wide_cols // TILE + width // TILE,)),
        ],
    )(table, own, left, right, wide)


def over_loc(a):
    return lax.all_to_all(a, "loc", split_axis=0, concat_axis=0, tiled=True)


def shift(a, step):
    groups = lax.axis_size("grp")
    return lax.ppermute(a, "grp", [(i, (i + step) % groups) for i in range(groups)])


def ring_gather(own):
    mid = own.shape[0] // 2
    before, after = shift(own, 1), shift(own, -1)
    return [own, after, shift(before[:mid], 1), shift(after[mid:], -1), before]


def body(tokens, grad_out, expert_ids, route_weight, gate_weight, up_weight, down_weight):
    groups = lax.axis_size("grp")
    locs = lax.axis_size("loc")
    experts = locs // 2
    width = tokens.shape[1]
    buf = experts * CAP
    unit = 2 * CAP
    share = 768
    ring_cols = 3072
    wide_cols = width - ring_cols

    w_gate, w_up, w_down = gate_weight[0], up_weight[0], down_weight[0]

    table, g_send, xg_send = dispatch(
        expert_ids.T, route_weight.T, grad_out, tokens, experts, share
    )
    g_blocks = ring_gather(g_send)
    xg = over_loc(xg_send.reshape(locs, unit, xg_send.shape[3]))
    xg, *g_blocks = lax.optimization_barrier((xg, *g_blocks))
    blocks = ring_gather(xg.reshape(locs * unit, xg.shape[2]))
    g_out = regroup(g_blocks)
    g_rows = over_loc(g_out.reshape(locs, groups * unit, g_out.shape[3]))
    g_rows = g_rows.reshape(locs * groups * unit, g_out.shape[3])

    own, after, top, bottom, before = blocks
    *pre_own, outer_own = pre([own], w_gate, w_up, w_down, share)
    *pre_side, outer_side = pre([after, before], w_gate, w_up, w_down, share)
    *pre_far, outer_far = pre([top, bottom], w_gate, w_up, w_down, share)
    gu, near, far_top, far_bottom = hidden(
        g_rows, w_down, w_gate, w_up, pre_own, pre_side, pre_far, wide_cols
    )

    came_top, came_bottom = shift(far_top, 1), shift(far_bottom, -1)
    part_ring = ring_part(near, w_gate, w_up, ring_cols)
    part_ring, gu = lax.optimization_barrier((part_ring, gu))
    home_ring = over_loc(part_ring.reshape(locs, groups * CAP, ring_cols))
    part_next, part_prev, part_own = side_part(gu, w_gate, w_up, came_top, came_bottom)
    from_before, from_after = shift(part_next, 1), shift(part_prev, -1)

    outers = (outer_own, outer_side, outer_far)
    part_own, gu, outers = lax.optimization_barrier((part_own, gu, outers))
    gate_grad, up_grad = row_grads(gu, blocks, share)
    down_grad = down(outers, blocks, g_rows, share)
    part_own, gate_grad, up_grad, down_grad = lax.optimization_barrier(
        (part_own, gate_grad, up_grad, down_grad)
    )
    fold_own, fold_top, fold_bottom, fold_side = fold(
        home_ring.reshape(2, experts, groups * CAP, ring_cols)
    )
    home_wide = over_loc(sum_blocks(part_own, from_before, from_after))
    fold_next, fold_prev = add_far(fold_side, shift(fold_top, 1), shift(fold_bottom, -1))
    tokens_grad = combine(table, fold_own, shift(fold_next, 1), shift(fold_prev, -1), home_wide)
    return (tokens_grad, gate_grad[None], up_grad[None], down_grad[None])


def solution(mesh):
    in_specs = (
        P(("grp", "loc"), None),
        P(("grp", "loc"), None),
        P(("grp", "loc"), None),
        P(("grp", "loc"), None),
        P("loc", None, "grp"),
        P("loc", None, "grp"),
        P("loc", "grp", None),
    )
    out_specs = (
        P(("grp", "loc"), None),
        P("loc", None, "grp"),
        P("loc", None, "grp"),
        P("loc", "grp", None),
    )
    return jax.shard_map(body, mesh=mesh, in_specs=in_specs, out_specs=out_specs, check_vma=False)
```
